128 devices in a mesh: row: 8 (over y, z_lo), col: 16 (over x, z_hi, core).
Axes of the slice: x: 4, y: 4, z: 4 (z_hi: 2, z_lo: 2; z = z_hi * 2 + z_lo), core: 2. Of those that a mesh axis runs over, the one named last changes fastest.
Arguments:
- stream_in: bfloat16 [2048, 8192], P('col', 'row'), may hold values from -6 to 6
- grad_out: bfloat16 [2048, 8192], P('col', 'row'), may hold values from -6 to 6
- gate_pre: bfloat16 [2048, 14336], P('row', 'col'), may hold values from -6 to 6
- up_pre: bfloat16 [2048, 14336], P('row', 'col'), may hold values from -6 to 6
- keep_mask: int32 [2048, 14336], P('row', 'col'), may hold values 0 or 1
- segment_ids: int32 [2048], P('row'), may hold values from 0 to 15, never falling along the last dimension, each value on 1 to 256 neighbouring positions
- norm_gain: float32 [8192], P('row'), may hold values from 0.25 to 1.75
- w_gate: bfloat16 [8192, 14336], P('row', 'col'), may hold values from -0.0625 to 0.0625
- w_up: bfloat16 [8192, 14336], P('row', 'col'), may hold values from -0.0625 to 0.0625
- w_down: bfloat16 [14336, 8192], P('col', 'row'), may hold values from -0.046875 to 0.046875
Outputs:
- grad_in: bfloat16 [2048, 8192], P('col', 'row')
- grad_gate: bfloat16 [8192, 14336], P('row', 'col')
- grad_up: bfloat16 [8192, 14336], P('row', 'col')
- grad_down: bfloat16 [14336, 8192], P('col', 'row')
The draws below stay inside these ranges and needn't reach their ends.
Inputs may be any that keep to these rules, and one draw needn't show every extreme that they name: `segment_ids`: never falls along the tokens; each of the 16 documents has 1 to 256 tokens, one exactly 256.
All inputs are finite; a program needn't handle non-finite values. No bound on the sum of `keep_mask` on one device may be relied on, other than what follows from the above.
Results may differ from the reference program's by a relative error of at most 0.0059.
Values may be sent and summed in bfloat16 or wider, within the bound.
A program may use at most 128 MiB of HBM per device.

```python
import math
import jax
import jax.numpy as jnp
import numpy as np
from jax import lax

D = 8192
FF = 14336
SEGS = 16
TOKENS = 2048
MOST = 256


def touch_ends(values, rng, low, high):
    extent = values.shape
    spot = [jax.random.randint(jax.random.fold_in(rng, axis), (), 0, extent[axis]) for axis in range(len(extent))]
    values = values.at[tuple(spot)].set(low)
    longest = extent.index(max(extent))
    spot[longest] = (spot[longest] + 1) % extent[longest]
    return values.at[tuple(spot)].set(high)


def shard_levels(key, shape, split, low, high):
    level = 1.0
    for position, blocks in split:
        heights = jax.random.uniform(jax.random.fold_in(jax.random.fold_in(key, 6), position), (blocks,), jnp.float32, low / len(split), high / len(split))
        level = level * jnp.repeat(jnp.exp(heights), shape[position] // blocks).reshape((-1,) + (1,) * (len(shape) - 1 - position))
    return level


def length_profile(count, total, limit, lean):
    portions = [(1 << 20) // math.isqrt(standing ** lean) + 1 for standing in range(2, count + 1)]
    spare, given = total - limit - (count - 1), [1] * (count - 1)
    while spare > 0:
        movable = [i for i in range(count - 1) if given[i] < limit]
        pool, remaining = sum([portions[i] for i in movable]), spare
        for i in movable:
            extra = min(limit - given[i], max(1, remaining * portions[i] // pool), spare)
            given[i] = given[i] + extra
            spare = spare - extra
    return np.array([limit] + given)


def ragged_sizes(key, number_of, total, reach, lean):
    if number_of == 2:
        one = jax.random.randint(key, (), max(1, total - reach), min(reach, total - 1) + 1)
        return jnp.stack([one, total - one])
    lengths = jnp.asarray(length_profile(number_of, total, reach, lean), jnp.int32)
    couples = (number_of - 1) // 2
    source_of, sink = lengths[1:1 + 2 * couples:2], lengths[2:2 + 2 * couples:2]
    margin = jnp.minimum(source_of - 1, reach - sink)
    shifted = jax.random.randint(jax.random.fold_in(key, 1), (couples,), 0, 1 << 20) % (margin + 1)
    lengths = lengths.at[1:1 + 2 * couples:2].set(source_of - shifted).at[2:2 + 2 * couples:2].set(sink + shifted)
    return lengths[jax.random.permutation(jax.random.fold_in(key, 2), number_of)]


def gaussian(own_key, extent, width, limit, shards=(), kind=jnp.bfloat16):
    array = jax.random.normal(own_key, extent, jnp.float32) * width
    if len(shards) > 0:
        array = shard_levels(own_key, extent, shards, -0.22, 0.18) * array
    return jnp.clip(array, min=-limit, max=limit).astype(kind)


def setup_inputs(seed: int = 0) -> dict:
    key_list = jax.random.split(jax.random.key(seed), 11)
    return {
        "stream_in": gaussian(key_list[0], (TOKENS, D), 1.0, 6.0, ((0, 16), (1, 8))),
        "grad_out": gaussian(key_list[1], (TOKENS, D), 1.0, 6.0, ((0, 16), (1, 8))),
        "gate_pre": gaussian(key_list[2], (TOKENS, FF), 1.5, 6.0, ((0, 8), (1, 16))),
        "up_pre": gaussian(key_list[3], (TOKENS, FF), 1.0, 6.0, ((0, 8), (1, 16))),
        "keep_mask": touch_ends((jax.random.randint(key_list[4], (TOKENS, FF), 0, 10) < 9).astype(jnp.int32), jax.random.fold_in(key_list[4], 1), 0, 1),
        "segment_ids": jnp.searchsorted(jnp.cumsum(ragged_sizes(key_list[5], SEGS, TOKENS, MOST, 1)), jnp.arange(TOKENS), side="right").astype(jnp.int32),
        "norm_gain": jnp.clip(1.0 + 0.15 * jax.random.normal(key_list[6], (D,), jnp.float32), 0.25, 1.75),
        "w_gate": gaussian(key_list[7], (D, FF), D ** -0.5, 0.0625, ((0, 8), (1, 16))),
        "w_up": gaussian(key_list[8], (D, FF), D ** -0.5, 0.0625, ((0, 8), (1, 16))),
        "w_down": gaussian(key_list[9], (FF, D), FF ** -0.5, 0.046875, ((0, 16), (1, 8))),
    }


eps = 1e-05
keep_scale = 1.0 / 0.9

def reference(stream_in, grad_out, gate_pre, up_pre, keep_mask, segment_ids, norm_gain, w_gate, w_up, w_down):
    xs = stream_in.astype(jnp.float32)
    onehot = (segment_ids[:, None] == jnp.arange(SEGS, dtype=jnp.int32)[None, :]).astype(jnp.float32)
    counts = lax.optimization_barrier(jnp.sum(onehot, axis=0))
    weights = lax.optimization_barrier(jnp.sum(onehot * (TOKENS / (SEGS * counts))[None, :], axis=1))
    recip = lax.rsqrt(lax.optimization_barrier(jnp.sum(xs * xs, axis=1)) / D + eps)
    normed = (xs * recip[:, None] * norm_gain[None, :]).astype(jnp.bfloat16)
    gate_f = gate_pre.astype(jnp.float32)
    up_f = up_pre.astype(jnp.float32)
    sig = jax.nn.sigmoid(gate_f)
    keep_f = keep_mask.astype(jnp.float32) * keep_scale
    dropped = (gate_f * sig * up_f * keep_f * weights[:, None]).astype(jnp.bfloat16)
    back = jnp.dot(grad_out, w_down.T, preferred_element_type=jnp.float32)
    grad_act = back * weights[:, None] * keep_f
    grad_gpre = (grad_act * up_f * sig * (1.0 + gate_f * (1.0 - sig))).astype(jnp.bfloat16)
    grad_upre = (grad_act * gate_f * sig).astype(jnp.bfloat16)
    grad_down = jnp.dot(dropped.T, grad_out, preferred_element_type=jnp.float32).astype(jnp.bfloat16)
    grad_gate = jnp.dot(normed.T, grad_gpre, preferred_element_type=jnp.float32).astype(jnp.bfloat16)
    grad_up = jnp.dot(normed.T, grad_upre, preferred_element_type=jnp.float32).astype(jnp.bfloat16)
    grad_normed = jnp.dot(grad_gpre, w_gate.T, preferred_element_type=jnp.float32) + jnp.dot(grad_upre, w_up.T, preferred_element_type=jnp.float32)
    scaled = grad_normed * norm_gain[None, :]
    inner = lax.optimization_barrier(jnp.sum(scaled * xs, axis=1)) / D
    branch = recip[:, None] * (scaled - xs * (recip * recip * inner)[:, None])
    grad_in = (grad_out.astype(jnp.float32) + branch).astype(jnp.bfloat16)
    return (grad_in, grad_gate, grad_up, grad_down)
```

```python
import jax
import jax.numpy as jnp
from jax import lax
from jax.sharding import PartitionSpec as P

D = 8192
SEGS = 16


eps = 1e-05
keep_scale = 1.0 / 0.9


def over_tokens(left, right):
    return lax.dot_general(
        left, right, (((0,), (0,)), ((), ())), preferred_element_type=jnp.float32
    )


def over_width(left, right):
    return lax.dot_general(
        left, right, (((1,), (1,)), ((), ())), preferred_element_type=jnp.float32
    )


def per_device(
    stream_in, grad_out, gate_pre, up_pre, keep_mask, segment_ids, norm_gain, w_gate, w_up, w_down
):
    n_row = lax.axis_size("row")
    n_col = lax.axis_size("col")
    tok_col, feat_loc = stream_in.shape
    total = tok_col * n_col
    xs = stream_in.astype(jnp.float32)
    onehot = (segment_ids[:, None] == jnp.arange(SEGS, dtype=jnp.int32)[None, :]).astype(
        jnp.float32
    )
    squares, counts = lax.psum((jnp.sum(xs * xs, axis=1), jnp.sum(onehot, axis=0)), "row")
    weights = jnp.sum(onehot * (total / (SEGS * counts))[None, :], axis=1)
    recip = lax.rsqrt(squares / D + eps)
    normed = (xs * recip[:, None] * norm_gain[None, :]).astype(jnp.bfloat16)
    gate_f = gate_pre.astype(jnp.float32)
    up_f = up_pre.astype(jnp.float32)
    sig = jax.nn.sigmoid(gate_f)
    keep_f = keep_mask.astype(jnp.float32) * keep_scale
    dropped = (gate_f * sig * up_f * keep_f * weights[:, None]).astype(jnp.bfloat16)
    cot_full, normed_full = (
        lax.all_gather(grad_out, "col", axis=0, tiled=True),
        lax.all_gather(normed, "col", axis=0, tiled=True),
    )
    back = lax.psum_scatter(over_width(cot_full, w_down), "row", scatter_dimension=0, tiled=True)
    grad_act = back * weights[:, None] * keep_f
    grad_gpre = (grad_act * up_f * sig * (1.0 + gate_f * (1.0 - sig))).astype(jnp.bfloat16)
    grad_upre = (grad_act * gate_f * sig).astype(jnp.bfloat16)
    dropped_full, gpre_full, upre_full = (
        lax.all_gather(dropped, "row", axis=0, tiled=True),
        lax.all_gather(grad_gpre, "row", axis=0, tiled=True),
        lax.all_gather(grad_upre, "row", axis=0, tiled=True),
    )
    grad_down = over_tokens(dropped_full, cot_full).astype(jnp.bfloat16)
    grad_gate = over_tokens(normed_full, gpre_full).astype(jnp.bfloat16)
    grad_up = over_tokens(normed_full, upre_full).astype(jnp.bfloat16)
    grad_normed = lax.psum_scatter(
        over_width(gpre_full, w_gate) + over_width(upre_full, w_up),
        "col",
        scatter_dimension=0,
        tiled=True,
    )
    scaled = grad_normed * norm_gain[None, :]
    inner = lax.psum(jnp.sum(scaled * xs, axis=1), "row") / D
    branch = recip[:, None] * (scaled - xs * (recip * recip * inner)[:, None])
    grad_in = (grad_out.astype(jnp.float32) + branch).astype(jnp.bfloat16)
    return (grad_in, grad_gate, grad_up, grad_down)


def solution(mesh):
    return jax.shard_map(
        per_device,
        mesh=mesh,
        in_specs=(
            P("col", "row"),
            P("col", "row"),
            P("row", "col"),
            P("row", "col"),
            P("row", "col"),
            P("row"),
            P("row"),
            P("row", "col"),
            P("row", "col"),
            P("col", "row"),
        ),
        out_specs=(P("col", "row"), P("row", "col"), P("row", "col"), P("col", "row")),
        check_vma=False,
    )
```

```python
import functools

import jax
import jax.numpy as jnp
from jax import lax
from jax.experimental import pallas as pl
from jax.experimental.pallas import tpu as pltpu
from jax.sharding import PartitionSpec as P

D = 8192
SEGS = 16
AXES = ("row", "col")

eps = 1e-05
keep_scale = 1.0 / 0.9


def over_tokens(left, right):
    return lax.dot_general(
        left, right, (((0,), (0,)), ((), ())), preferred_element_type=jnp.float32
    )


def over_width(left, right):
    return lax.dot_general(
        left, right, (((1,), (1,)), ((), ())), preferred_element_type=jnp.float32
    )


def _dev(axis, idx):
    return tuple(idx if a == axis else lax.axis_index(a) for a in AXES)


def _barrier(axes):
    barrier = pltpu.get_barrier_semaphore()
    count = 0
    for axis in sorted(set(axes)):
        k = lax.axis_size(axis)
        me = lax.axis_index(axis)
        for d in range(1, k):
            pl.semaphore_signal(
                barrier, inc=1, device_id=_dev(axis, (me + d) % k),
                device_id_type=pl.DeviceIdType.MESH,
            )
        count += k - 1
    pl.semaphore_wait(barrier, count)


def _exchange_kernel(modes, axes, *refs):
    n = len(modes)
    ins, outs = refs[:n], refs[n:2 * n]
    send_sem, recv_sem, local_sem = refs[2 * n:]
    _barrier(axes)
    sends = []
    for i, (mode, axis) in enumerate(zip(modes, axes)):
        k = lax.axis_size(axis)
        me = lax.axis_index(axis)
        m = outs[i].shape[1]
        for d in range(1, k):
            tgt = (me + d) % k
            src = ins[i] if mode == "gather" else ins[i].at[pl.ds(tgt * m, m)]
            c = pltpu.make_async_remote_copy(
                src, outs[i].at[me], send_sem.at[i, d], recv_sem.at[i, me],
                device_id=_dev(axis, tgt), device_id_type=pl.DeviceIdType.MESH,
            )
            c.start()
            sends.append(c)
        src = ins[i] if mode == "gather" else ins[i].at[pl.ds(me * m, m)]
        loc = pltpu.make_async_copy(src, outs[i].at[me], local_sem.at[i])
        loc.start()
        sends.append(loc)
    for c in sends:
        if c.is_remote:
            c.wait_send()
        else:
            c.wait()
    for i, (mode, axis) in enumerate(zip(modes, axes)):
        k = lax.axis_size(axis)
        me = lax.axis_index(axis)
        m = outs[i].shape[1]
        for d in range(1, k):
            srcdev = (me + k - d) % k
            src = ins[i] if mode == "gather" else ins[i].at[pl.ds(0, m)]
            pltpu.make_async_remote_copy(
                src, outs[i].at[srcdev], send_sem.at[i, d], recv_sem.at[i, srcdev],
                device_id=_dev(axis, srcdev), device_id_type=pl.DeviceIdType.MESH,
            ).wait_recv()


def exchange(items, cid):
    modes = tuple(mode for _, _, mode in items)
    axes = tuple(axis for _, axis, _ in items)
    out_shapes = []
    kmax = 1
    for x, axis, mode in items:
        k = lax.axis_size(axis)
        kmax = max(kmax, k)
        if mode == "gather":
            out_shapes.append(jax.ShapeDtypeStruct((k,) + x.shape, x.dtype))
        else:
            out_shapes.append(
                jax.ShapeDtypeStruct((k, x.shape[0] // k) + x.shape[1:], x.dtype)
            )
    n = len(items)
    return pl.pallas_call(
        functools.partial(_exchange_kernel, modes, axes),
        out_shape=tuple(out_shapes),
        in_specs=[pl.BlockSpec(memory_space=pl.ANY)] * n,
        out_specs=tuple(pl.BlockSpec(memory_space=pl.ANY) for _ in range(n)),
        scratch_shapes=[
            pltpu.SemaphoreType.DMA((n, kmax)),
            pltpu.SemaphoreType.DMA((n, kmax)),
            pltpu.SemaphoreType.DMA((n,)),
        ],
        compiler_params=pltpu.CompilerParams(collective_id=cid, has_side_effects=True),
    )(*[x for x, _, _ in items])


def per_device(
    stream_in, grad_out, gate_pre, up_pre, keep_mask, segment_ids, norm_gain, w_gate, w_up, w_down
):
    n_row = lax.axis_size("row")
    n_col = lax.axis_size("col")
    tok_col, feat_loc = stream_in.shape
    tok_row, ff_loc = gate_pre.shape
    total = tok_col * n_col
    xs = stream_in.astype(jnp.float32)
    onehot = (segment_ids[:, None] == jnp.arange(SEGS, dtype=jnp.int32)[None, :]).astype(
        jnp.float32
    )
    stats = jnp.concatenate([jnp.sum(xs * xs, axis=1), jnp.sum(onehot, axis=0)])[None, :]
    (stats_all,) = exchange([(stats, "row", "gather")], 0)
    stats_sum = jnp.sum(stats_all, axis=(0, 1))
    squares, counts = stats_sum[:tok_col], stats_sum[tok_col:]
    weights = jnp.sum(onehot * (total / (SEGS * counts))[None, :], axis=1)
    recip = lax.rsqrt(squares / D + eps)
    normed = (xs * recip[:, None] * norm_gain[None, :]).astype(jnp.bfloat16)
    gate_f = gate_pre.astype(jnp.float32)
    up_f = up_pre.astype(jnp.float32)
    sig = jax.nn.sigmoid(gate_f)
    keep_f = keep_mask.astype(jnp.float32) * keep_scale
    dropped = (gate_f * sig * up_f * keep_f * weights[:, None]).astype(jnp.bfloat16)
    cot_full, normed_full, dropped_full = exchange(
        [(grad_out, "col", "gather"), (normed, "col", "gather"), (dropped, "row", "gather")], 1
    )
    cot_full = cot_full.reshape(total, feat_loc)
    normed_full = normed_full.reshape(total, feat_loc)
    dropped_full = dropped_full.reshape(total, ff_loc)
    (back_parts,) = exchange([(over_width(cot_full, w_down), "row", "scatter")], 2)
    back = jnp.sum(back_parts, axis=0)
    grad_act = back * weights[:, None] * keep_f
    grad_gpre = (grad_act * up_f * sig * (1.0 + gate_f * (1.0 - sig))).astype(jnp.bfloat16)
    grad_upre = (grad_act * gate_f * sig).astype(jnp.bfloat16)
    gpre_full, upre_full = exchange([(grad_gpre, "row", "gather"), (grad_upre, "row", "gather")], 3)
    gpre_full = gpre_full.reshape(total, ff_loc)
    upre_full = upre_full.reshape(total, ff_loc)
    grad_down = over_tokens(dropped_full, cot_full).astype(jnp.bfloat16)
    grad_gate = over_tokens(normed_full, gpre_full).astype(jnp.bfloat16)
    grad_up = over_tokens(normed_full, upre_full).astype(jnp.bfloat16)
    partial = over_width(gpre_full, w_gate) + over_width(upre_full, w_up)
    (gn_parts,) = exchange([(partial, "col", "scatter")], 4)
    grad_normed = jnp.sum(gn_parts, axis=0)
    scaled = grad_normed * norm_gain[None, :]
    (inner_all,) = exchange([(jnp.sum(scaled * xs, axis=1)[None, :], "row", "gather")], 5)
    inner = jnp.sum(inner_all, axis=(0, 1)) / D
    branch = recip[:, None] * (scaled - xs * (recip * recip * inner)[:, None])
    grad_in = (grad_out.astype(jnp.float32) + branch).astype(jnp.bfloat16)
    return (grad_in, grad_gate, grad_up, grad_down)


def solution(mesh):
    return jax.shard_map(
        per_device,
        mesh=mesh,
        in_specs=(
            P("col", "row"),
            P("col", "row"),
            P("row", "col"),
            P("row", "col"),
            P("row", "col"),
            P("row"),
            P("row"),
            P("row", "col"),
            P("row", "col"),
            P("col", "row"),
        ),
        out_specs=(P("col", "row"), P("row", "col"), P("row", "col"), P("col", "row")),
        check_vma=False,
    )
```

```python
import functools

import jax
import jax.numpy as jnp
from jax import lax
from jax.experimental import pallas as pl
from jax.experimental.pallas import tpu as pltpu
from jax.sharding import PartitionSpec as P

D = 8192
SEGS = 16
AXES = ("row", "col")
WIRE = jnp.float32

eps = 1e-05
keep_scale = 1.0 / 0.9


def over_tokens(left, right):
    return lax.dot_general(
        left, right, (((0,), (0,)), ((), ())), preferred_element_type=jnp.float32
    )


def over_width(left, right):
    return lax.dot_general(
        left, right, (((1,), (1,)), ((), ())), preferred_element_type=jnp.float32
    )


def _dev(axis, idx):
    return tuple(idx if a == axis else lax.axis_index(a) for a in AXES)


def _barrier(axes):
    barrier = pltpu.get_barrier_semaphore()
    count = 0
    for axis in sorted(set(axes)):
        k = lax.axis_size(axis)
        me = lax.axis_index(axis)
        for d in range(1, k):
            pl.semaphore_signal(
                barrier, inc=1, device_id=_dev(axis, (me + d) % k),
                device_id_type=pl.DeviceIdType.MESH,
            )
        count += k - 1
    pl.semaphore_wait(barrier, count)


def _exchange_kernel(modes, axes, *refs):
    n = len(modes)
    ins, outs = refs[:n], refs[n:2 * n]
    send_sem, recv_sem, local_sem = refs[2 * n:]
    _barrier(axes)
    sends = []
    for i, (mode, axis) in enumerate(zip(modes, axes)):
        k = lax.axis_size(axis)
        me = lax.axis_index(axis)
        m = outs[i].shape[1]
        for d in range(1, k):
            tgt = (me + d) % k
            src = ins[i] if mode == "gather" else ins[i].at[pl.ds(tgt * m, m)]
            c = pltpu.make_async_remote_copy(
                src, outs[i].at[me], send_sem.at[i, d], recv_sem.at[i, me],
                device_id=_dev(axis, tgt), device_id_type=pl.DeviceIdType.MESH,
            )
            c.start()
            sends.append(c)
        if mode == "gather":
            loc = pltpu.make_async_copy(ins[i], outs[i].at[me], local_sem.at[i])
            loc.start()
            sends.append(loc)
    for c in sends:
        if c.is_remote:
            c.wait_send()
        else:
            c.wait()
    for i, (mode, axis) in enumerate(zip(modes, axes)):
        k = lax.axis_size(axis)
        me = lax.axis_index(axis)
        m = outs[i].shape[1]
        for d in range(1, k):
            srcdev = (me + k - d) % k
            src = ins[i] if mode == "gather" else ins[i].at[pl.ds(0, m)]
            pltpu.make_async_remote_copy(
                src, outs[i].at[srcdev], send_sem.at[i, d], recv_sem.at[i, srcdev],
                device_id=_dev(axis, srcdev), device_id_type=pl.DeviceIdType.MESH,
            ).wait_recv()


def exchange(items, cid):
    modes = tuple(mode for _, _, mode in items)
    axes = tuple(axis for _, axis, _ in items)
    out_shapes = []
    kmax = 1
    for x, axis, mode in items:
        k = lax.axis_size(axis)
        kmax = max(kmax, k)
        if mode == "gather":
            out_shapes.append(jax.ShapeDtypeStruct((k,) + x.shape, x.dtype))
        else:
            out_shapes.append(
                jax.ShapeDtypeStruct((k, x.shape[0] // k) + x.shape[1:], x.dtype)
            )
    n = len(items)
    return pl.pallas_call(
        functools.partial(_exchange_kernel, modes, axes),
        out_shape=tuple(out_shapes),
        in_specs=[pl.BlockSpec(memory_space=pl.ANY)] * n,
        out_specs=tuple(pl.BlockSpec(memory_space=pl.ANY) for _ in range(n)),
        scratch_shapes=[
            pltpu.SemaphoreType.DMA((n, kmax)),
            pltpu.SemaphoreType.DMA((n, kmax)),
            pltpu.SemaphoreType.DMA((n,)),
        ],
        compiler_params=pltpu.CompilerParams(collective_id=cid, has_side_effects=True),
    )(*[x for x, _, _ in items])


def reduce_scatter(parts, axis, cid, extra=()):
    k = lax.axis_size(axis)
    me = lax.axis_index(axis)
    m = parts.shape[0] // k
    outs = exchange([(parts.astype(WIRE), axis, "scatter")] + list(extra), cid)
    slots = outs[0]
    mine = lax.dynamic_slice_in_dim(parts, me * m, m, axis=0)
    keep = (jnp.arange(k) != me).reshape((k,) + (1,) * (slots.ndim - 1))
    other = jnp.sum(jnp.where(keep, slots.astype(jnp.float32), 0.0), axis=0)
    return (mine + other,) + tuple(outs[1:])


def per_device(
    stream_in, grad_out, gate_pre, up_pre, keep_mask, segment_ids, norm_gain, w_gate, w_up, w_down
):
    n_row = lax.axis_size("row")
    n_col = lax.axis_size("col")
    tok_col, feat_loc = stream_in.shape
    tok_row, ff_loc = gate_pre.shape
    total = tok_col * n_col
    xs = stream_in.astype(jnp.float32)
    onehot = (segment_ids[:, None] == jnp.arange(SEGS, dtype=jnp.int32)[None, :]).astype(
        jnp.float32
    )
    stats = jnp.concatenate([jnp.sum(xs * xs, axis=1), jnp.sum(onehot, axis=0)])[None, :]
    (stats_all,) = exchange([(stats, "row", "gather")], 0)
    stats_sum = jnp.sum(stats_all, axis=(0, 1))
    squares, counts = stats_sum[:tok_col], stats_sum[tok_col:]
    weights = jnp.sum(onehot * (total / (SEGS * counts))[None, :], axis=1)
    recip = lax.rsqrt(squares / D + eps)
    normed = (xs * recip[:, None] * norm_gain[None, :]).astype(jnp.bfloat16)
    gate_f = gate_pre.astype(jnp.float32)
    up_f = up_pre.astype(jnp.float32)
    sig = jax.nn.sigmoid(gate_f)
    keep_f = keep_mask.astype(jnp.float32) * keep_scale
    dropped = (gate_f * sig * up_f * keep_f * weights[:, None]).astype(jnp.bfloat16)
    cot_full, dropped_full = exchange([(grad_out, "col", "gather"), (dropped, "row", "gather")], 1)
    cot_full = cot_full.reshape(total, feat_loc)
    dropped_full = dropped_full.reshape(total, ff_loc)
    back, normed_full = reduce_scatter(
        over_width(cot_full, w_down), "row", 2, [(normed, "col", "gather")]
    )
    normed_full = normed_full.reshape(total, feat_loc)
    grad_act = back * weights[:, None] * keep_f
    grad_gpre = (grad_act * up_f * sig * (1.0 + gate_f * (1.0 - sig))).astype(jnp.bfloat16)
    grad_upre = (grad_act * gate_f * sig).astype(jnp.bfloat16)
    gpre_full, upre_full = exchange([(grad_gpre, "row", "gather"), (grad_upre, "row", "gather")], 3)
    gpre_full = gpre_full.reshape(total, ff_loc)
    upre_full = upre_full.reshape(total, ff_loc)
    grad_down = over_tokens(dropped_full, cot_full).astype(jnp.bfloat16)
    grad_gate = over_tokens(normed_full, gpre_full).astype(jnp.bfloat16)
    grad_up = over_tokens(normed_full, upre_full).astype(jnp.bfloat16)
    partial = over_width(gpre_full, w_gate) + over_width(upre_full, w_up)
    (grad_normed,) = reduce_scatter(partial, "col", 4)
    scaled = grad_normed * norm_gain[None, :]
    (inner_all,) = exchange([(jnp.sum(scaled * xs, axis=1)[None, :], "row", "gather")], 5)
    inner = jnp.sum(inner_all, axis=(0, 1)) / D
    branch = recip[:, None] * (scaled - xs * (recip * recip * inner)[:, None])
    grad_in = (grad_out.astype(jnp.float32) + branch).astype(jnp.bfloat16)
    return (grad_in, grad_gate, grad_up, grad_down)


def solution(mesh):
    return jax.shard_map(
        per_device,
        mesh=mesh,
        in_specs=(
            P("col", "row"),
            P("col", "row"),
            P("row", "col"),
            P("row", "col"),
            P("row", "col"),
            P("row"),
            P("row"),
            P("row", "col"),
            P("row", "col"),
            P("col", "row"),
        ),
        out_specs=(P("col", "row"), P("row", "col"), P("row", "col"), P("col", "row")),
        check_vma=False,
    )
```

```python
import functools

import jax
import jax.numpy as jnp
from jax import lax
from jax.experimental import pallas as pl
from jax.experimental.pallas import tpu as pltpu
from jax.sharding import PartitionSpec as P

D = 8192
SEGS = 16
AXES = ("row", "col")
WIRE = jnp.bfloat16

eps = 1e-05
keep_scale = 1.0 / 0.9


def over_tokens(left, right):
    return lax.dot_general(
        left, right, (((0,), (0,)), ((), ())), preferred_element_type=jnp.float32
    )


def over_width(left, right):
    return lax.dot_general(
        left, right, (((1,), (1,)), ((), ())), preferred_element_type=jnp.float32
    )


def _dev(axis, idx):
    return tuple(idx if a == axis else lax.axis_index(a) for a in AXES)


def _barrier(axes):
    barrier = pltpu.get_barrier_semaphore()
    count = 0
    for axis in sorted(set(axes)):
        k = lax.axis_size(axis)
        me = lax.axis_index(axis)
        for d in range(1, k):
            pl.semaphore_signal(
                barrier, inc=1, device_id=_dev(axis, (me + d) % k),
                device_id_type=pl.DeviceIdType.MESH,
            )
        count += k - 1
    pl.semaphore_wait(barrier, count)


def _exchange_kernel(modes, axes, *refs):
    n = len(modes)
    ins, outs = refs[:n], refs[n:2 * n]
    send_sem, recv_sem, local_sem = refs[2 * n:]
    _barrier(axes)
    sends = []
    for i, (mode, axis) in enumerate(zip(modes, axes)):
        k = lax.axis_size(axis)
        me = lax.axis_index(axis)
        m = outs[i].shape[1]
        for d in range(1, k):
            tgt = (me + d) % k
            src = ins[i] if mode == "gather" else ins[i].at[pl.ds(tgt * m, m)]
            c = pltpu.make_async_remote_copy(
                src, outs[i].at[me], send_sem.at[i, d], recv_sem.at[i, me],
                device_id=_dev(axis, tgt), device_id_type=pl.DeviceIdType.MESH,
            )
            c.start()
            sends.append(c)
        if mode == "gather":
            loc = pltpu.make_async_copy(ins[i], outs[i].at[me], local_sem.at[i])
            loc.start()
            sends.append(loc)
    for c in sends:
        if c.is_remote:
            c.wait_send()
        else:
            c.wait()
    for i, (mode, axis) in enumerate(zip(modes, axes)):
        k = lax.axis_size(axis)
        me = lax.axis_index(axis)
        m = outs[i].shape[1]
        for d in range(1, k):
            srcdev = (me + k - d) % k
            src = ins[i] if mode == "gather" else ins[i].at[pl.ds(0, m)]
            pltpu.make_async_remote_copy(
                src, outs[i].at[srcdev], send_sem.at[i, d], recv_sem.at[i, srcdev],
                device_id=_dev(axis, srcdev), device_id_type=pl.DeviceIdType.MESH,
            ).wait_recv()


def exchange(items, cid):
    modes = tuple(mode for _, _, mode in items)
    axes = tuple(axis for _, axis, _ in items)
    out_shapes = []
    kmax = 1
    for x, axis, mode in items:
        k = lax.axis_size(axis)
        kmax = max(kmax, k)
        if mode == "gather":
            out_shapes.append(jax.ShapeDtypeStruct((k,) + x.shape, x.dtype))
        else:
            out_shapes.append(
                jax.ShapeDtypeStruct((k, x.shape[0] // k) + x.shape[1:], x.dtype)
            )
    n = len(items)
    return pl.pallas_call(
        functools.partial(_exchange_kernel, modes, axes),
        out_shape=tuple(out_shapes),
        in_specs=[pl.BlockSpec(memory_space=pl.ANY)] * n,
        out_specs=tuple(pl.BlockSpec(memory_space=pl.ANY) for _ in range(n)),
        scratch_shapes=[
            pltpu.SemaphoreType.DMA((n, kmax)),
            pltpu.SemaphoreType.DMA((n, kmax)),
            pltpu.SemaphoreType.DMA((n,)),
        ],
        compiler_params=pltpu.CompilerParams(collective_id=cid, has_side_effects=True),
    )(*[x for x, _, _ in items])


def reduce_scatter(parts, axis, cid, extra=()):
    k = lax.axis_size(axis)
    me = lax.axis_index(axis)
    m = parts.shape[0] // k
    outs = exchange([(parts.astype(WIRE), axis, "scatter")] + list(extra), cid)
    slots = outs[0]
    mine = lax.dynamic_slice_in_dim(parts, me * m, m, axis=0)
    keep = (jnp.arange(k) != me).reshape((k,) + (1,) * (slots.ndim - 1))
    other = jnp.sum(jnp.where(keep, slots.astype(jnp.float32), 0.0), axis=0)
    return (mine + other,) + tuple(outs[1:])


def per_device(
    stream_in, grad_out, gate_pre, up_pre, keep_mask, segment_ids, norm_gain, w_gate, w_up, w_down
):
    n_row = lax.axis_size("row")
    n_col = lax.axis_size("col")
    tok_col, feat_loc = stream_in.shape
    tok_row, ff_loc = gate_pre.shape
    total = tok_col * n_col
    xs = stream_in.astype(jnp.float32)
    onehot = (segment_ids[:, None] == jnp.arange(SEGS, dtype=jnp.int32)[None, :]).astype(
        jnp.float32
    )
    stats = jnp.concatenate([jnp.sum(xs * xs, axis=1), jnp.sum(onehot, axis=0)])[None, :]
    (stats_all,) = exchange([(stats, "row", "gather")], 0)
    stats_sum = jnp.sum(stats_all, axis=(0, 1))
    squares, counts = stats_sum[:tok_col], stats_sum[tok_col:]
    weights = jnp.sum(onehot * (total / (SEGS * counts))[None, :], axis=1)
    recip = lax.rsqrt(squares / D + eps)
    normed = (xs * recip[:, None] * norm_gain[None, :]).astype(jnp.bfloat16)
    gate_f = gate_pre.astype(jnp.float32)
    up_f = up_pre.astype(jnp.float32)
    sig = jax.nn.sigmoid(gate_f)
    keep_f = keep_mask.astype(jnp.float32) * keep_scale
    dropped = (gate_f * sig * up_f * keep_f * weights[:, None]).astype(jnp.bfloat16)
    cot_full, dropped_full = exchange([(grad_out, "col", "gather"), (dropped, "row", "gather")], 1)
    cot_full = cot_full.reshape(total, feat_loc)
    dropped_full = dropped_full.reshape(total, ff_loc)
    back, normed_full = reduce_scatter(
        over_width(cot_full, w_down), "row", 2, [(normed, "col", "gather")]
    )
    normed_full = normed_full.reshape(total, feat_loc)
    grad_act = back * weights[:, None] * keep_f
    grad_gpre = (grad_act * up_f * sig * (1.0 + gate_f * (1.0 - sig))).astype(jnp.bfloat16)
    grad_upre = (grad_act * gate_f * sig).astype(jnp.bfloat16)
    gpre_full, upre_full = exchange([(grad_gpre, "row", "gather"), (grad_upre, "row", "gather")], 3)
    gpre_full = gpre_full.reshape(total, ff_loc)
    upre_full = upre_full.reshape(total, ff_loc)
    grad_down = over_tokens(dropped_full, cot_full).astype(jnp.bfloat16)
    grad_gate = over_tokens(normed_full, gpre_full).astype(jnp.bfloat16)
    grad_up = over_tokens(normed_full, upre_full).astype(jnp.bfloat16)
    partial = over_width(gpre_full, w_gate) + over_width(upre_full, w_up)
    (grad_normed,) = reduce_scatter(partial, "col", 4)
    scaled = grad_normed * norm_gain[None, :]
    (inner_all,) = exchange([(jnp.sum(scaled * xs, axis=1)[None, :], "row", "gather")], 5)
    inner = jnp.sum(inner_all, axis=(0, 1)) / D
    branch = recip[:, None] * (scaled - xs * (recip * recip * inner)[:, None])
    grad_in = (grad_out.astype(jnp.float32) + branch).astype(jnp.bfloat16)
    return (grad_in, grad_gate, grad_up, grad_down)


def solution(mesh):
    return jax.shard_map(
        per_device,
        mesh=mesh,
        in_specs=(
            P("col", "row"),
            P("col", "row"),
            P("row", "col"),
            P("row", "col"),
            P("row", "col"),
            P("row"),
            P("row"),
            P("row", "col"),
            P("row", "col"),
            P("col", "row"),
        ),
        out_specs=(P("col", "row"), P("row", "col"), P("row", "col"), P("col", "row")),
        check_vma=False,
    )
```

```python
import functools

import jax
import jax.numpy as jnp
from jax import lax
from jax.experimental import pallas as pl
from jax.experimental.pallas import tpu as pltpu
from jax.sharding import PartitionSpec as P

D = 8192
SEGS = 16
AXES = ("row", "col")
WIRE = jnp.bfloat16

eps = 1e-05
keep_scale = 1.0 / 0.9


def over_tokens(left, right):
    return lax.dot_general(
        left, right, (((0,), (0,)), ((), ())), preferred_element_type=jnp.float32
    )


def over_width(left, right):
    return lax.dot_general(
        left, right, (((1,), (1,)), ((), ())), preferred_element_type=jnp.float32
    )


def _dev(axis, idx):
    return tuple(idx if a == axis else lax.axis_index(a) for a in AXES)


def _barrier(axes):
    barrier = pltpu.get_barrier_semaphore()
    count = 0
    for axis in sorted(set(axes)):
        k = lax.axis_size(axis)
        me = lax.axis_index(axis)
        for d in range(1, k):
            pl.semaphore_signal(
                barrier, inc=1, device_id=_dev(axis, (me + d) % k),
                device_id_type=pl.DeviceIdType.MESH,
            )
        count += k - 1
    pl.semaphore_wait(barrier, count)


def _exchange_kernel(modes, axes, *refs):
    n = len(modes)
    ins, outs = refs[:n], refs[n:2 * n]
    send_sem, recv_sem, local_sem = refs[2 * n:]
    _barrier(axes)
    sends = []
    for i, (mode, axis) in enumerate(zip(modes, axes)):
        k = lax.axis_size(axis)
        me = lax.axis_index(axis)
        m = outs[i].shape[1]
        for d in range(1, k):
            tgt = (me + d) % k
            src = ins[i] if mode == "gather" else ins[i].at[pl.ds(tgt * m, m)]
            c = pltpu.make_async_remote_copy(
                src, outs[i].at[me], send_sem.at[i, d], recv_sem.at[i, me],
                device_id=_dev(axis, tgt), device_id_type=pl.DeviceIdType.MESH,
            )
            c.start()
            sends.append(c)
        if mode == "gather":
            loc = pltpu.make_async_copy(ins[i], outs[i].at[me], local_sem.at[i])
            loc.start()
            sends.append(loc)
    for c in sends:
        if c.is_remote:
            c.wait_send()
        else:
            c.wait()
    for i, (mode, axis) in enumerate(zip(modes, axes)):
        k = lax.axis_size(axis)
        me = lax.axis_index(axis)
        m = outs[i].shape[1]
        for d in range(1, k):
            srcdev = (me + k - d) % k
            src = ins[i] if mode == "gather" else ins[i].at[pl.ds(0, m)]
            pltpu.make_async_remote_copy(
                src, outs[i].at[srcdev], send_sem.at[i, d], recv_sem.at[i, srcdev],
                device_id=_dev(axis, srcdev), device_id_type=pl.DeviceIdType.MESH,
            ).wait_recv()


def exchange(items, cid):
    modes = tuple(mode for _, _, mode in items)
    axes = tuple(axis for _, axis, _ in items)
    out_shapes = []
    kmax = 1
    for x, axis, mode in items:
        k = lax.axis_size(axis)
        kmax = max(kmax, k)
        if mode == "gather":
            out_shapes.append(jax.ShapeDtypeStruct((k,) + x.shape, x.dtype))
        else:
            out_shapes.append(
                jax.ShapeDtypeStruct((k, x.shape[0] // k) + x.shape[1:], x.dtype)
            )
    n = len(items)
    return pl.pallas_call(
        functools.partial(_exchange_kernel, modes, axes),
        out_shape=tuple(out_shapes),
        in_specs=[pl.BlockSpec(memory_space=pl.ANY)] * n,
        out_specs=tuple(pl.BlockSpec(memory_space=pl.ANY) for _ in range(n)),
        scratch_shapes=[
            pltpu.SemaphoreType.DMA((n, kmax)),
            pltpu.SemaphoreType.DMA((n, kmax)),
            pltpu.SemaphoreType.DMA((n,)),
        ],
        compiler_params=pltpu.CompilerParams(collective_id=cid, has_side_effects=True),
    )(*[x for x, _, _ in items])


def reduce_scatter(parts, axis, cid, extra=()):
    k = lax.axis_size(axis)
    me = lax.axis_index(axis)
    m = parts.shape[0] // k
    outs = exchange([(parts.astype(WIRE), axis, "scatter")] + list(extra), cid)
    slots = outs[0]
    mine = lax.dynamic_slice_in_dim(parts, me * m, m, axis=0)
    keep = (jnp.arange(k) != me).reshape((k,) + (1,) * (slots.ndim - 1))
    other = jnp.sum(jnp.where(keep, slots.astype(jnp.float32), 0.0), axis=0)
    return (mine + other,) + tuple(outs[1:])


def per_device(
    stream_in, grad_out, gate_pre, up_pre, keep_mask, segment_ids, norm_gain, w_gate, w_up, w_down
):
    n_row = lax.axis_size("row")
    n_col = lax.axis_size("col")
    tok_col, feat_loc = stream_in.shape
    tok_row, ff_loc = gate_pre.shape
    total = tok_col * n_col
    xs = stream_in.astype(jnp.float32)
    onehot = (segment_ids[:, None] == jnp.arange(SEGS, dtype=jnp.int32)[None, :]).astype(
        jnp.float32
    )
    stats = jnp.concatenate([jnp.sum(xs * xs, axis=1), jnp.sum(onehot, axis=0)])[None, :]
    (stats_all,) = exchange([(stats, "row", "gather")], 0)
    stats_sum = jnp.sum(stats_all, axis=(0, 1))
    squares, counts = stats_sum[:tok_col], stats_sum[tok_col:]
    weights = jnp.sum(onehot * (total / (SEGS * counts))[None, :], axis=1)
    recip = lax.rsqrt(squares / D + eps)
    normed = (xs * recip[:, None] * norm_gain[None, :]).astype(jnp.bfloat16)
    gate_f = gate_pre.astype(jnp.float32)
    up_f = up_pre.astype(jnp.float32)
    sig = jax.nn.sigmoid(gate_f)
    keep_f = keep_mask.astype(jnp.float32) * keep_scale
    dropped = (gate_f * sig * up_f * keep_f * weights[:, None]).astype(jnp.bfloat16)
    cot_full, dropped_full = exchange([(grad_out, "col", "gather"), (dropped, "row", "gather")], 1)
    cot_full = cot_full.reshape(total, feat_loc)
    dropped_full = dropped_full.reshape(total, ff_loc)
    back, normed_full = reduce_scatter(
        over_width(cot_full, w_down), "row", 2, [(normed, "col", "gather")]
    )
    normed_full = normed_full.reshape(total, feat_loc)
    grad_act = back * weights[:, None] * keep_f
    grad_gpre = (grad_act * up_f * sig * (1.0 + gate_f * (1.0 - sig))).astype(jnp.bfloat16)
    grad_upre = (grad_act * gate_f * sig).astype(jnp.bfloat16)
    half = tok_col // 2
    n_chunk = tok_row // tok_col

    def split(v):
        v = v.reshape(n_chunk, 2, half, ff_loc)
        return v[:, 0].reshape(tok_row // 2, ff_loc), v[:, 1].reshape(tok_row // 2, ff_loc)

    def joined(a, b):
        a = a.reshape(n_row, n_chunk, 1, half, ff_loc)
        b = b.reshape(n_row, n_chunk, 1, half, ff_loc)
        return jnp.concatenate([a, b], axis=2).reshape(total, ff_loc)

    gpre_a, gpre_b = split(grad_gpre)
    upre_a, upre_b = split(grad_upre)
    ga_full, ua_full = exchange([(gpre_a, "row", "gather"), (upre_a, "row", "gather")], 3)
    ga_full = ga_full.reshape(total // 2, ff_loc)
    ua_full = ua_full.reshape(total // 2, ff_loc)
    part_a = over_width(ga_full, w_gate) + over_width(ua_full, w_up)
    gn_a, gb_full, ub_full = reduce_scatter(
        part_a, "col", 4, [(gpre_b, "row", "gather"), (upre_b, "row", "gather")]
    )
    gb_full = gb_full.reshape(total // 2, ff_loc)
    ub_full = ub_full.reshape(total // 2, ff_loc)
    part_b = over_width(gb_full, w_gate) + over_width(ub_full, w_up)
    (gn_b,) = reduce_scatter(part_b, "col", 6)
    grad_normed = jnp.concatenate([gn_a, gn_b], axis=0)
    gpre_full = joined(ga_full, gb_full)
    upre_full = joined(ua_full, ub_full)
    grad_down = over_tokens(dropped_full, cot_full).astype(jnp.bfloat16)
    grad_gate = over_tokens(normed_full, gpre_full).astype(jnp.bfloat16)
    grad_up = over_tokens(normed_full, upre_full).astype(jnp.bfloat16)
    scaled = grad_normed * norm_gain[None, :]
    (inner_all,) = exchange([(jnp.sum(scaled * xs, axis=1)[None, :], "row", "gather")], 5)
    inner = jnp.sum(inner_all, axis=(0, 1)) / D
    branch = recip[:, None] * (scaled - xs * (recip * recip * inner)[:, None])
    grad_in = (grad_out.astype(jnp.float32) + branch).astype(jnp.bfloat16)
    return (grad_in, grad_gate, grad_up, grad_down)


def solution(mesh):
    return jax.shard_map(
        per_device,
        mesh=mesh,
        in_specs=(
            P("col", "row"),
            P("col", "row"),
            P("row", "col"),
            P("row", "col"),
            P("row", "col"),
            P("row"),
            P("row"),
            P("row", "col"),
            P("row", "col"),
            P("col", "row"),
        ),
        out_specs=(P("col", "row"), P("row", "col"), P("row", "col"), P("col", "row")),
        check_vma=False,
    )
```

```python
import functools

import jax
import jax.numpy as jnp
from jax import lax
from jax.experimental import pallas as pl
from jax.experimental.pallas import tpu as pltpu
from jax.sharding import PartitionSpec as P

D = 8192
SEGS = 16
AXES = ("row", "col")
WIRE = jnp.bfloat16

eps = 1e-05
keep_scale = 1.0 / 0.9


def over_tokens(left, right):
    return lax.dot_general(
        left, right, (((0,), (0,)), ((), ())), preferred_element_type=jnp.float32
    )


def over_width(left, right):
    return lax.dot_general(
        left, right, (((1,), (1,)), ((), ())), preferred_element_type=jnp.float32
    )


def _dev(axis, idx):
    return tuple(idx if a == axis else lax.axis_index(a) for a in AXES)


def _barrier(axes):
    barrier = pltpu.get_barrier_semaphore()
    count = 0
    for axis in sorted(set(axes)):
        k = lax.axis_size(axis)
        me = lax.axis_index(axis)
        for d in range(1, k):
            pl.semaphore_signal(
                barrier, inc=1, device_id=_dev(axis, (me + d) % k),
                device_id_type=pl.DeviceIdType.MESH,
            )
        count += k - 1
    pl.semaphore_wait(barrier, count)


def _exchange_kernel(modes, axes, n_deps, *refs):
    n = len(modes)
    ins, outs = refs[:n], refs[n + n_deps:2 * n + n_deps]
    send_sem, recv_sem, local_sem = refs[2 * n + n_deps:]
    _barrier(axes)
    sends = []
    for i, (mode, axis) in enumerate(zip(modes, axes)):
        k = lax.axis_size(axis)
        me = lax.axis_index(axis)
        m = outs[i].shape[1]
        for d in range(1, k):
            tgt = (me + d) % k
            src = ins[i] if mode == "gather" else ins[i].at[pl.ds(tgt * m, m)]
            c = pltpu.make_async_remote_copy(
                src, outs[i].at[me], send_sem.at[i, d], recv_sem.at[i, me],
                device_id=_dev(axis, tgt), device_id_type=pl.DeviceIdType.MESH,
            )
            c.start()
            sends.append(c)
        if mode == "gather":
            loc = pltpu.make_async_copy(ins[i], outs[i].at[me], local_sem.at[i])
            loc.start()
            sends.append(loc)
    for c in sends:
        if c.is_remote:
            c.wait_send()
        else:
            c.wait()
    for i, (mode, axis) in enumerate(zip(modes, axes)):
        k = lax.axis_size(axis)
        me = lax.axis_index(axis)
        m = outs[i].shape[1]
        for d in range(1, k):
            srcdev = (me + k - d) % k
            src = ins[i] if mode == "gather" else ins[i].at[pl.ds(0, m)]
            pltpu.make_async_remote_copy(
                src, outs[i].at[srcdev], send_sem.at[i, d], recv_sem.at[i, srcdev],
                device_id=_dev(axis, srcdev), device_id_type=pl.DeviceIdType.MESH,
            ).wait_recv()


def exchange(items, cid, deps=()):
    modes = tuple(mode for _, _, mode in items)
    axes = tuple(axis for _, axis, _ in items)
    out_shapes = []
    kmax = 1
    for x, axis, mode in items:
        k = lax.axis_size(axis)
        kmax = max(kmax, k)
        if mode == "gather":
            out_shapes.append(jax.ShapeDtypeStruct((k,) + x.shape, x.dtype))
        else:
            out_shapes.append(
                jax.ShapeDtypeStruct((k, x.shape[0] // k) + x.shape[1:], x.dtype)
            )
    n = len(items)
    return pl.pallas_call(
        functools.partial(_exchange_kernel, modes, axes, len(deps)),
        out_shape=tuple(out_shapes),
        in_specs=[pl.BlockSpec(memory_space=pl.ANY)] * (n + len(deps)),
        out_specs=tuple(pl.BlockSpec(memory_space=pl.ANY) for _ in range(n)),
        scratch_shapes=[
            pltpu.SemaphoreType.DMA((n, kmax)),
            pltpu.SemaphoreType.DMA((n, kmax)),
            pltpu.SemaphoreType.DMA((n,)),
        ],
        compiler_params=pltpu.CompilerParams(collective_id=cid, has_side_effects=True),
        cost_estimate=pl.CostEstimate(
            flops=0, transcendentals=0,
            bytes_accessed=sum(int(o.size) * o.dtype.itemsize for o in out_shapes) * 40,
        ),
    )(*[x for x, _, _ in items], *deps)


def reduce_scatter(parts, axis, cid, extra=(), deps=()):
    k = lax.axis_size(axis)
    me = lax.axis_index(axis)
    m = parts.shape[0] // k
    outs = exchange([(parts.astype(WIRE), axis, "scatter")] + list(extra), cid, deps)
    slots = outs[0]
    mine = lax.dynamic_slice_in_dim(parts, me * m, m, axis=0)
    keep = (jnp.arange(k) != me).reshape((k,) + (1,) * (slots.ndim - 1))
    other = jnp.sum(jnp.where(keep, slots.astype(jnp.float32), 0.0), axis=0)
    return (mine + other,) + tuple(outs[1:])


def per_device(
    stream_in, grad_out, gate_pre, up_pre, keep_mask, segment_ids, norm_gain, w_gate, w_up, w_down
):
    n_row = lax.axis_size("row")
    n_col = lax.axis_size("col")
    tok_col, feat_loc = stream_in.shape
    tok_row, ff_loc = gate_pre.shape
    total = tok_col * n_col
    xs = stream_in.astype(jnp.float32)
    onehot = (segment_ids[:, None] == jnp.arange(SEGS, dtype=jnp.int32)[None, :]).astype(
        jnp.float32
    )
    stats = jnp.concatenate([jnp.sum(xs * xs, axis=1), jnp.sum(onehot, axis=0)])[None, :]
    (stats_all,) = exchange([(stats, "row", "gather")], 0)
    stats_sum = jnp.sum(stats_all, axis=(0, 1))
    squares, counts = stats_sum[:tok_col], stats_sum[tok_col:]
    weights = jnp.sum(onehot * (total / (SEGS * counts))[None, :], axis=1)
    recip = lax.rsqrt(squares / D + eps)
    normed = (xs * recip[:, None] * norm_gain[None, :]).astype(jnp.bfloat16)
    gate_f = gate_pre.astype(jnp.float32)
    up_f = up_pre.astype(jnp.float32)
    sig = jax.nn.sigmoid(gate_f)
    keep_f = keep_mask.astype(jnp.float32) * keep_scale
    dropped = (gate_f * sig * up_f * keep_f * weights[:, None]).astype(jnp.bfloat16)
    dropped_full = lax.all_gather(dropped, "row", axis=0, tiled=True)
    normed_full = lax.all_gather(normed, "col", axis=0, tiled=True)
    (cot_full,) = exchange([(grad_out, "col", "gather")], 1)
    cot_full = cot_full.reshape(total, feat_loc)
    (back,) = reduce_scatter(
        over_width(cot_full, w_down), "row", 2, deps=(dropped_full,)
    )
    grad_act = back * weights[:, None] * keep_f
    grad_gpre = (grad_act * up_f * sig * (1.0 + gate_f * (1.0 - sig))).astype(jnp.bfloat16)
    grad_upre = (grad_act * gate_f * sig).astype(jnp.bfloat16)
    half = tok_col // 2
    n_chunk = tok_row // tok_col

    def split(v):
        v = v.reshape(n_chunk, 2, half, ff_loc)
        return v[:, 0].reshape(tok_row // 2, ff_loc), v[:, 1].reshape(tok_row // 2, ff_loc)

    def joined(a, b):
        a = a.reshape(n_row, n_chunk, 1, half, ff_loc)
        b = b.reshape(n_row, n_chunk, 1, half, ff_loc)
        return jnp.concatenate([a, b], axis=2).reshape(total, ff_loc)

    gpre_a, gpre_b = split(grad_gpre)
    upre_a, upre_b = split(grad_upre)
    ga_full, ua_full = exchange(
        [(gpre_a, "row", "gather"), (upre_a, "row", "gather")], 3, (normed_full,)
    )
    ga_full = ga_full.reshape(total // 2, ff_loc)
    ua_full = ua_full.reshape(total // 2, ff_loc)
    part_a = over_width(ga_full, w_gate) + over_width(ua_full, w_up)
    gn_a, gb_full, ub_full = reduce_scatter(
        part_a, "col", 4, [(gpre_b, "row", "gather"), (upre_b, "row", "gather")]
    )
    gb_full = gb_full.reshape(total // 2, ff_loc)
    ub_full = ub_full.reshape(total // 2, ff_loc)
    part_b = over_width(gb_full, w_gate) + over_width(ub_full, w_up)
    (gn_b,) = reduce_scatter(part_b, "col", 6)
    grad_normed = jnp.concatenate([gn_a, gn_b], axis=0)
    gpre_full = joined(ga_full, gb_full)
    upre_full = joined(ua_full, ub_full)
    grad_down = over_tokens(dropped_full, cot_full).astype(jnp.bfloat16)
    grad_gate = over_tokens(normed_full, gpre_full).astype(jnp.bfloat16)
    grad_up = over_tokens(normed_full, upre_full).astype(jnp.bfloat16)
    scaled = grad_normed * norm_gain[None, :]
    (inner_all,) = exchange([(jnp.sum(scaled * xs, axis=1)[None, :], "row", "gather")], 5)
    inner = jnp.sum(inner_all, axis=(0, 1)) / D
    branch = recip[:, None] * (scaled - xs * (recip * recip * inner)[:, None])
    grad_in = (grad_out.astype(jnp.float32) + branch).astype(jnp.bfloat16)
    return (grad_in, grad_gate, grad_up, grad_down)


def solution(mesh):
    return jax.shard_map(
        per_device,
        mesh=mesh,
        in_specs=(
            P("col", "row"),
            P("col", "row"),
            P("row", "col"),
            P("row", "col"),
            P("row", "col"),
            P("row"),
            P("row"),
            P("row", "col"),
            P("row", "col"),
            P("col", "row"),
        ),
        out_specs=(P("col", "row"), P("row", "col"), P("row", "col"), P("col", "row")),
        check_vma=False,
    )
```

```python
import functools

import jax
import jax.numpy as jnp
from jax import lax
from jax.experimental import pallas as pl
from jax.experimental.pallas import tpu as pltpu
from jax.sharding import PartitionSpec as P

D = 8192
SEGS = 16
AXES = ("row", "col")
WIRE = jnp.bfloat16

eps = 1e-05
keep_scale = 1.0 / 0.9


def over_tokens(left, right):
    return lax.dot_general(
        left, right, (((0,), (0,)), ((), ())), preferred_element_type=jnp.float32
    )


def over_width(left, right):
    return lax.dot_general(
        left, right, (((1,), (1,)), ((), ())), preferred_element_type=jnp.float32
    )


def _dev(axis, idx):
    return tuple(idx if a == axis else lax.axis_index(a) for a in AXES)


def _barrier(axes):
    barrier = pltpu.get_barrier_semaphore()
    count = 0
    for axis in sorted(set(axes)):
        k = lax.axis_size(axis)
        me = lax.axis_index(axis)
        for d in range(1, k):
            pl.semaphore_signal(
                barrier, inc=1, device_id=_dev(axis, (me + d) % k),
                device_id_type=pl.DeviceIdType.MESH,
            )
        count += k - 1
    pl.semaphore_wait(barrier, count)


def _exchange_kernel(modes, axes, n_deps, *refs):
    n = len(modes)
    ins, outs = refs[:n], refs[n + n_deps:2 * n + n_deps]
    send_sem, recv_sem, local_sem = refs[2 * n + n_deps:]
    _barrier(axes)
    sends = []
    for i, (mode, axis) in enumerate(zip(modes, axes)):
        k = lax.axis_size(axis)
        me = lax.axis_index(axis)
        m = outs[i].shape[1]
        for d in range(1, k):
            tgt = (me + d) % k
            src = ins[i] if mode == "gather" else ins[i].at[pl.ds(tgt * m, m)]
            c = pltpu.make_async_remote_copy(
                src, outs[i].at[me], send_sem.at[i, d], recv_sem.at[i, me],
                device_id=_dev(axis, tgt), device_id_type=pl.DeviceIdType.MESH,
            )
            c.start()
            sends.append(c)
        if mode == "gather":
            loc = pltpu.make_async_copy(ins[i], outs[i].at[me], local_sem.at[i])
            loc.start()
            sends.append(loc)
    for c in sends:
        if c.is_remote:
            c.wait_send()
        else:
            c.wait()
    for i, (mode, axis) in enumerate(zip(modes, axes)):
        k = lax.axis_size(axis)
        me = lax.axis_index(axis)
        m = outs[i].shape[1]
        for d in range(1, k):
            srcdev = (me + k - d) % k
            src = ins[i] if mode == "gather" else ins[i].at[pl.ds(0, m)]
            pltpu.make_async_remote_copy(
                src, outs[i].at[srcdev], send_sem.at[i, d], recv_sem.at[i, srcdev],
                device_id=_dev(axis, srcdev), device_id_type=pl.DeviceIdType.MESH,
            ).wait_recv()


def exchange(items, cid, deps=()):
    modes = tuple(mode for _, _, mode in items)
    axes = tuple(axis for _, axis, _ in items)
    out_shapes = []
    kmax = 1
    for x, axis, mode in items:
        k = lax.axis_size(axis)
        kmax = max(kmax, k)
        if mode == "gather":
            out_shapes.append(jax.ShapeDtypeStruct((k,) + x.shape, x.dtype))
        else:
            out_shapes.append(
                jax.ShapeDtypeStruct((k, x.shape[0] // k) + x.shape[1:], x.dtype)
            )
    n = len(items)
    return pl.pallas_call(
        functools.partial(_exchange_kernel, modes, axes, len(deps)),
        out_shape=tuple(out_shapes),
        in_specs=[pl.BlockSpec(memory_space=pl.ANY)] * (n + len(deps)),
        out_specs=tuple(pl.BlockSpec(memory_space=pl.ANY) for _ in range(n)),
        scratch_shapes=[
            pltpu.SemaphoreType.DMA((n, kmax)),
            pltpu.SemaphoreType.DMA((n, kmax)),
            pltpu.SemaphoreType.DMA((n,)),
        ],
        compiler_params=pltpu.CompilerParams(collective_id=cid, has_side_effects=True),
        cost_estimate=pl.CostEstimate(
            flops=0, transcendentals=0,
            bytes_accessed=sum(int(o.size) * o.dtype.itemsize for o in out_shapes),
        ),
    )(*[x for x, _, _ in items], *deps)


def reduce_scatter(parts, axis, cid, extra=(), deps=()):
    k = lax.axis_size(axis)
    me = lax.axis_index(axis)
    m = parts.shape[0] // k
    outs = exchange([(parts.astype(WIRE), axis, "scatter")] + list(extra), cid, deps)
    slots = outs[0]
    mine = lax.dynamic_slice_in_dim(parts, me * m, m, axis=0)
    keep = (jnp.arange(k) != me).reshape((k,) + (1,) * (slots.ndim - 1))
    other = jnp.sum(jnp.where(keep, slots.astype(jnp.float32), 0.0), axis=0)
    return (mine + other,) + tuple(outs[1:])


def per_device(
    stream_in, grad_out, gate_pre, up_pre, keep_mask, segment_ids, norm_gain, w_gate, w_up, w_down
):
    n_row = lax.axis_size("row")
    n_col = lax.axis_size("col")
    tok_col, feat_loc = stream_in.shape
    tok_row, ff_loc = gate_pre.shape
    total = tok_col * n_col
    xs = stream_in.astype(jnp.float32)
    onehot = (segment_ids[:, None] == jnp.arange(SEGS, dtype=jnp.int32)[None, :]).astype(
        jnp.float32
    )
    stats = jnp.concatenate([jnp.sum(xs * xs, axis=1), jnp.sum(onehot, axis=0)])[None, :]
    (stats_all,) = exchange([(stats, "row", "gather")], 0)
    stats_sum = jnp.sum(stats_all, axis=(0, 1))
    squares, counts = stats_sum[:tok_col], stats_sum[tok_col:]
    weights = jnp.sum(onehot * (total / (SEGS * counts))[None, :], axis=1)
    recip = lax.rsqrt(squares / D + eps)
    normed = (xs * recip[:, None] * norm_gain[None, :]).astype(jnp.bfloat16)
    gate_f = gate_pre.astype(jnp.float32)
    up_f = up_pre.astype(jnp.float32)
    sig = jax.nn.sigmoid(gate_f)
    keep_f = keep_mask.astype(jnp.float32) * keep_scale
    dropped = (gate_f * sig * up_f * keep_f * weights[:, None]).astype(jnp.bfloat16)
    dropped_full = lax.all_gather(dropped, "row", axis=0, tiled=True)
    normed_full = lax.all_gather(normed, "col", axis=0, tiled=True)
    (cot_full,) = exchange([(grad_out, "col", "gather")], 1)
    cot_full = cot_full.reshape(total, feat_loc)
    (back,) = reduce_scatter(over_width(cot_full, w_down), "row", 2)
    grad_act = back * weights[:, None] * keep_f
    grad_gpre = (grad_act * up_f * sig * (1.0 + gate_f * (1.0 - sig))).astype(jnp.bfloat16)
    grad_upre = (grad_act * gate_f * sig).astype(jnp.bfloat16)
    half = tok_col // 2
    n_chunk = tok_row // tok_col

    def split(v):
        v = v.reshape(n_chunk, 2, half, ff_loc)
        return v[:, 0].reshape(tok_row // 2, ff_loc), v[:, 1].reshape(tok_row // 2, ff_loc)

    def joined(a, b):
        a = a.reshape(n_row, n_chunk, 1, half, ff_loc)
        b = b.reshape(n_row, n_chunk, 1, half, ff_loc)
        return jnp.concatenate([a, b], axis=2).reshape(total, ff_loc)

    gpre_a, gpre_b = split(grad_gpre)
    upre_a, upre_b = split(grad_upre)
    ga_full, ua_full = exchange([(gpre_a, "row", "gather"), (upre_a, "row", "gather")], 3)
    ga_full = ga_full.reshape(total // 2, ff_loc)
    ua_full = ua_full.reshape(total // 2, ff_loc)
    part_a = over_width(ga_full, w_gate) + over_width(ua_full, w_up)
    gn_a, gb_full, ub_full = reduce_scatter(
        part_a, "col", 4, [(gpre_b, "row", "gather"), (upre_b, "row", "gather")]
    )
    gb_full = gb_full.reshape(total // 2, ff_loc)
    ub_full = ub_full.reshape(total // 2, ff_loc)
    part_b = over_width(gb_full, w_gate) + over_width(ub_full, w_up)
    (gn_b,) = reduce_scatter(part_b, "col", 6, deps=(dropped_full, normed_full))
    grad_normed = jnp.concatenate([gn_a, gn_b], axis=0)
    gpre_full = joined(ga_full, gb_full)
    upre_full = joined(ua_full, ub_full)
    grad_down = over_tokens(dropped_full, cot_full).astype(jnp.bfloat16)
    grad_gate = over_tokens(normed_full, gpre_full).astype(jnp.bfloat16)
    grad_up = over_tokens(normed_full, upre_full).astype(jnp.bfloat16)
    scaled = grad_normed * norm_gain[None, :]
    (inner_all,) = exchange([(jnp.sum(scaled * xs, axis=1)[None, :], "row", "gather")], 5)
    inner = jnp.sum(inner_all, axis=(0, 1)) / D
    branch = recip[:, None] * (scaled - xs * (recip * recip * inner)[:, None])
    grad_in = (grad_out.astype(jnp.float32) + branch).astype(jnp.bfloat16)
    return (grad_in, grad_gate, grad_up, grad_down)


def solution(mesh):
    return jax.shard_map(
        per_device,
        mesh=mesh,
        in_specs=(
            P("col", "row"),
            P("col", "row"),
            P("row", "col"),
            P("row", "col"),
            P("row", "col"),
            P("row"),
            P("row"),
            P("row", "col"),
            P("row", "col"),
            P("col", "row"),
        ),
        out_specs=(P("col", "row"), P("row", "col"), P("row", "col"), P("col", "row")),
        check_vma=False,
    )
```

```python
import functools

import jax
import jax.numpy as jnp
from jax import lax
from jax.experimental import pallas as pl
from jax.experimental.pallas import tpu as pltpu
from jax.sharding import PartitionSpec as P

D = 8192
SEGS = 16
AXES = ("row", "col")
WIRE = jnp.bfloat16

eps = 1e-05
keep_scale = 1.0 / 0.9


def over_tokens(left, right):
    return lax.dot_general(
        left, right, (((0,), (0,)), ((), ())), preferred_element_type=jnp.float32
    )


def over_width(left, right):
    return lax.dot_general(
        left, right, (((1,), (1,)), ((), ())), preferred_element_type=jnp.float32
    )


def _dev(axis, idx):
    return tuple(idx if a == axis else lax.axis_index(a) for a in AXES)


def _barrier(axes):
    barrier = pltpu.get_barrier_semaphore()
    count = 0
    for axis in sorted(set(axes)):
        k = lax.axis_size(axis)
        me = lax.axis_index(axis)
        for d in range(1, k):
            pl.semaphore_signal(
                barrier, inc=1, device_id=_dev(axis, (me + d) % k),
                device_id_type=pl.DeviceIdType.MESH,
            )
        count += k - 1
    pl.semaphore_wait(barrier, count)


def _exchange_kernel(modes, axes, *refs):
    n = len(modes)
    ins, outs = refs[:n], refs[n:2 * n]
    send_sem, recv_sem, local_sem = refs[2 * n:]
    _barrier(axes)
    sends, relays = [], []
    for i, (mode, axis) in enumerate(zip(modes, axes)):
        k = lax.axis_size(axis)
        me = lax.axis_index(axis)
        if mode == "pgather":
            p = me % 2
            for d in range(1, k // 2):
                tgt = (me + 2 * d) % k
                c = pltpu.make_async_remote_copy(
                    ins[i], outs[i].at[p, me // 2], send_sem.at[i, d], recv_sem.at[i, me],
                    device_id=_dev(axis, tgt), device_id_type=pl.DeviceIdType.MESH,
                )
                c.start()
                sends.append(c)
            loc = pltpu.make_async_copy(ins[i], outs[i].at[p, me // 2], local_sem.at[i])
            loc.start()
            relays.append((i, loc))
            continue
        m = outs[i].shape[1]
        for d in range(1, k):
            tgt = (me + d) % k
            src = ins[i] if mode == "gather" else ins[i].at[pl.ds(tgt * m, m)]
            c = pltpu.make_async_remote_copy(
                src, outs[i].at[me], send_sem.at[i, d], recv_sem.at[i, me],
                device_id=_dev(axis, tgt), device_id_type=pl.DeviceIdType.MESH,
            )
            c.start()
            sends.append(c)
        if mode == "gather":
            loc = pltpu.make_async_copy(ins[i], outs[i].at[me], local_sem.at[i])
            loc.start()
            sends.append(loc)
    for i, loc in relays:
        axis = axes[i]
        k = lax.axis_size(axis)
        me = lax.axis_index(axis)
        p = me % 2
        partner = me + 1 - 2 * p
        for d in range(1, k // 2):
            srcdev = (me + k - 2 * d) % k
            pltpu.make_async_remote_copy(
                ins[i], outs[i].at[p, srcdev // 2], send_sem.at[i, d], recv_sem.at[i, srcdev],
                device_id=_dev(axis, srcdev), device_id_type=pl.DeviceIdType.MESH,
            ).wait_recv()
        loc.wait()
        c = pltpu.make_async_remote_copy(
            outs[i].at[p], outs[i].at[p], send_sem.at[i, 0], recv_sem.at[i, me],
            device_id=_dev(axis, partner), device_id_type=pl.DeviceIdType.MESH,
        )
        c.start()
        sends.append(c)
    for c in sends:
        if c.is_remote:
            c.wait_send()
        else:
            c.wait()
    for i, (mode, axis) in enumerate(zip(modes, axes)):
        k = lax.axis_size(axis)
        me = lax.axis_index(axis)
        if mode == "pgather":
            p = me % 2
            partner = me + 1 - 2 * p
            pltpu.make_async_remote_copy(
                outs[i].at[1 - p], outs[i].at[1 - p], send_sem.at[i, 0], recv_sem.at[i, partner],
                device_id=_dev(axis, partner), device_id_type=pl.DeviceIdType.MESH,
            ).wait_recv()
            continue
        m = outs[i].shape[1]
        for d in range(1, k):
            srcdev = (me + k - d) % k
            src = ins[i] if mode == "gather" else ins[i].at[pl.ds(0, m)]
            pltpu.make_async_remote_copy(
                src, outs[i].at[srcdev], send_sem.at[i, d], recv_sem.at[i, srcdev],
                device_id=_dev(axis, srcdev), device_id_type=pl.DeviceIdType.MESH,
            ).wait_recv()


def exchange(items, cid):
    modes = tuple(mode for _, _, mode in items)
    axes = tuple(axis for _, axis, _ in items)
    out_shapes = []
    kmax = 1
    for x, axis, mode in items:
        k = lax.axis_size(axis)
        kmax = max(kmax, k)
        if mode == "gather":
            out_shapes.append(jax.ShapeDtypeStruct((k,) + x.shape, x.dtype))
        elif mode == "pgather":
            out_shapes.append(jax.ShapeDtypeStruct((2, k // 2) + x.shape, x.dtype))
        else:
            out_shapes.append(
                jax.ShapeDtypeStruct((k, x.shape[0] // k) + x.shape[1:], x.dtype)
            )
    n = len(items)
    return pl.pallas_call(
        functools.partial(_exchange_kernel, modes, axes),
        out_shape=tuple(out_shapes),
        in_specs=[pl.BlockSpec(memory_space=pl.ANY)] * n,
        out_specs=tuple(pl.BlockSpec(memory_space=pl.ANY) for _ in range(n)),
        scratch_shapes=[
            pltpu.SemaphoreType.DMA((n, kmax)),
            pltpu.SemaphoreType.DMA((n, kmax)),
            pltpu.SemaphoreType.DMA((n,)),
        ],
        compiler_params=pltpu.CompilerParams(collective_id=cid, has_side_effects=True),
    )(*[x for x, _, _ in items])


def pair_order(v):
    return jnp.swapaxes(v, 0, 1).reshape((-1,) + v.shape[3:])


def reduce_scatter(parts, axis, cid, extra=()):
    k = lax.axis_size(axis)
    me = lax.axis_index(axis)
    m = parts.shape[0] // k
    outs = exchange([(parts.astype(WIRE), axis, "scatter")] + list(extra), cid)
    slots = outs[0]
    mine = lax.dynamic_slice_in_dim(parts, me * m, m, axis=0)
    keep = (jnp.arange(k) != me).reshape((k,) + (1,) * (slots.ndim - 1))
    other = jnp.sum(jnp.where(keep, slots.astype(jnp.float32), 0.0), axis=0)
    return (mine + other,) + tuple(outs[1:])


def per_device(
    stream_in, grad_out, gate_pre, up_pre, keep_mask, segment_ids, norm_gain, w_gate, w_up, w_down
):
    n_row = lax.axis_size("row")
    n_col = lax.axis_size("col")
    tok_col, feat_loc = stream_in.shape
    tok_row, ff_loc = gate_pre.shape
    total = tok_col * n_col
    xs = stream_in.astype(jnp.float32)
    onehot = (segment_ids[:, None] == jnp.arange(SEGS, dtype=jnp.int32)[None, :]).astype(
        jnp.float32
    )
    stats = jnp.concatenate([jnp.sum(xs * xs, axis=1), jnp.sum(onehot, axis=0)])[None, :]
    (stats_all,) = exchange([(stats, "row", "gather")], 0)
    stats_sum = jnp.sum(stats_all, axis=(0, 1))
    squares, counts = stats_sum[:tok_col], stats_sum[tok_col:]
    weights = jnp.sum(onehot * (total / (SEGS * counts))[None, :], axis=1)
    recip = lax.rsqrt(squares / D + eps)
    normed = (xs * recip[:, None] * norm_gain[None, :]).astype(jnp.bfloat16)
    gate_f = gate_pre.astype(jnp.float32)
    up_f = up_pre.astype(jnp.float32)
    sig = jax.nn.sigmoid(gate_f)
    keep_f = keep_mask.astype(jnp.float32) * keep_scale
    dropped = (gate_f * sig * up_f * keep_f * weights[:, None]).astype(jnp.bfloat16)
    cot_full, dropped_full = exchange([(grad_out, "col", "pgather"), (dropped, "row", "gather")], 1)
    cot_full = pair_order(cot_full)
    dropped_full = dropped_full.reshape(total, ff_loc)
    back, normed_full = reduce_scatter(
        over_width(cot_full, w_down), "row", 2, [(normed, "col", "pgather")]
    )
    normed_full = pair_order(normed_full)
    grad_act = back * weights[:, None] * keep_f
    grad_gpre = (grad_act * up_f * sig * (1.0 + gate_f * (1.0 - sig))).astype(jnp.bfloat16)
    grad_upre = (grad_act * gate_f * sig).astype(jnp.bfloat16)
    half = tok_col // 2
    n_chunk = tok_row // tok_col

    def split(v):
        v = v.reshape(n_chunk, 2, half, ff_loc)
        return v[:, 0].reshape(tok_row // 2, ff_loc), v[:, 1].reshape(tok_row // 2, ff_loc)

    def joined(a, b):
        a = a.reshape(n_row, n_chunk, 1, half, ff_loc)
        b = b.reshape(n_row, n_chunk, 1, half, ff_loc)
        return jnp.concatenate([a, b], axis=2).reshape(total, ff_loc)

    gpre_a, gpre_b = split(grad_gpre)
    upre_a, upre_b = split(grad_upre)
    ga_full, ua_full = exchange([(gpre_a, "row", "gather"), (upre_a, "row", "gather")], 3)
    ga_full = ga_full.reshape(total // 2, ff_loc)
    ua_full = ua_full.reshape(total // 2, ff_loc)
    part_a = over_width(ga_full, w_gate) + over_width(ua_full, w_up)
    gn_a, gb_full, ub_full = reduce_scatter(
        part_a, "col", 4, [(gpre_b, "row", "gather"), (upre_b, "row", "gather")]
    )
    gb_full = gb_full.reshape(total // 2, ff_loc)
    ub_full = ub_full.reshape(total // 2, ff_loc)
    part_b = over_width(gb_full, w_gate) + over_width(ub_full, w_up)
    (gn_b,) = reduce_scatter(part_b, "col", 6)
    grad_normed = jnp.concatenate([gn_a, gn_b], axis=0)
    gpre_full = joined(ga_full, gb_full)
    upre_full = joined(ua_full, ub_full)
    grad_down = over_tokens(dropped_full, cot_full).astype(jnp.bfloat16)
    grad_gate = over_tokens(normed_full, gpre_full).astype(jnp.bfloat16)
    grad_up = over_tokens(normed_full, upre_full).astype(jnp.bfloat16)
    scaled = grad_normed * norm_gain[None, :]
    (inner_all,) = exchange([(jnp.sum(scaled * xs, axis=1)[None, :], "row", "gather")], 5)
    inner = jnp.sum(inner_all, axis=(0, 1)) / D
    branch = recip[:, None] * (scaled - xs * (recip * recip * inner)[:, None])
    grad_in = (grad_out.astype(jnp.float32) + branch).astype(jnp.bfloat16)
    return (grad_in, grad_gate, grad_up, grad_down)


def solution(mesh):
    return jax.shard_map(
        per_device,
        mesh=mesh,
        in_specs=(
            P("col", "row"),
            P("col", "row"),
            P("row", "col"),
            P("row", "col"),
            P("row", "col"),
            P("row"),
            P("row"),
            P("row", "col"),
            P("row", "col"),
            P("col", "row"),
        ),
        out_specs=(P("col", "row"), P("row", "col"), P("row", "col"), P("col", "row")),
        check_vma=False,
    )
```

```python
import functools

import jax
import jax.numpy as jnp
from jax import lax
from jax.experimental import pallas as pl
from jax.experimental.pallas import tpu as pltpu
from jax.sharding import PartitionSpec as P

D = 8192
SEGS = 16
AXES = ("row", "col")
WIRE = jnp.bfloat16

eps = 1e-05
keep_scale = 1.0 / 0.9


def over_tokens(left, right):
    return lax.dot_general(
        left, right, (((0,), (0,)), ((), ())), preferred_element_type=jnp.float32
    )


def over_width(left, right):
    return lax.dot_general(
        left, right, (((1,), (1,)), ((), ())), preferred_element_type=jnp.float32
    )


def _dev(axis, idx):
    return tuple(idx if a == axis else lax.axis_index(a) for a in AXES)


def _barrier(modes, axes):
    barrier = pltpu.get_barrier_semaphore()
    count = 0
    for axis in sorted(set(axes)):
        k = lax.axis_size(axis)
        me = lax.axis_index(axis)
        kinds = {mode for mode, a in zip(modes, axes) if a == axis}
        if kinds <= {"pswap"}:
            peers = [1 - 2 * (me % 2)]
        elif kinds <= {"pswap", "pgather", "pscatter"}:
            peers = [2 * d for d in range(1, k // 2)] + [1 - 2 * (me % 2)]
        else:
            peers = list(range(1, k))
        for d in peers:
            pl.semaphore_signal(
                barrier, inc=1, device_id=_dev(axis, (me + d) % k),
                device_id_type=pl.DeviceIdType.MESH,
            )
        count += len(peers)
    pl.semaphore_wait(barrier, count)


def _exchange_kernel(modes, axes, *refs):
    n = len(modes)
    ins, outs = refs[:n], refs[n:2 * n]
    send_sem, recv_sem, local_sem = refs[2 * n:]
    _barrier(modes, axes)
    sends, relays = [], []
    for i, (mode, axis) in enumerate(zip(modes, axes)):
        k = lax.axis_size(axis)
        me = lax.axis_index(axis)
        if mode == "pswap":
            c = pltpu.make_async_remote_copy(
                ins[i], outs[i], send_sem.at[i, 0], recv_sem.at[i, me],
                device_id=_dev(axis, me + 1 - 2 * (me % 2)),
                device_id_type=pl.DeviceIdType.MESH,
            )
            c.start()
            sends.append(c)
            continue
        if mode == "pscatter":
            for d in range(1, k // 2):
                tgt = (me + 2 * d) % k
                c = pltpu.make_async_remote_copy(
                    ins[i].at[tgt // 2], outs[i].at[me // 2], send_sem.at[i, d],
                    recv_sem.at[i, me], device_id=_dev(axis, tgt),
                    device_id_type=pl.DeviceIdType.MESH,
                )
                c.start()
                sends.append(c)
            continue
        if mode == "pgather":
            p = me % 2
            for d in range(1, k // 2):
                tgt = (me + 2 * d) % k
                c = pltpu.make_async_remote_copy(
                    ins[i], outs[i].at[p, me // 2], send_sem.at[i, d], recv_sem.at[i, me],
                    device_id=_dev(axis, tgt), device_id_type=pl.DeviceIdType.MESH,
                )
                c.start()
                sends.append(c)
            loc = pltpu.make_async_copy(ins[i], outs[i].at[p, me // 2], local_sem.at[i])
            loc.start()
            relays.append((i, loc))
            continue
        m = outs[i].shape[1]
        for d in range(1, k):
            tgt = (me + d) % k
            src = ins[i] if mode == "gather" else ins[i].at[pl.ds(tgt * m, m)]
            c = pltpu.make_async_remote_copy(
                src, outs[i].at[me], send_sem.at[i, d], recv_sem.at[i, me],
                device_id=_dev(axis, tgt), device_id_type=pl.DeviceIdType.MESH,
            )
            c.start()
            sends.append(c)
        if mode == "gather":
            loc = pltpu.make_async_copy(ins[i], outs[i].at[me], local_sem.at[i])
            loc.start()
            sends.append(loc)
    for i, loc in relays:
        axis = axes[i]
        k = lax.axis_size(axis)
        me = lax.axis_index(axis)
        p = me % 2
        partner = me + 1 - 2 * p
        for d in range(1, k // 2):
            srcdev = (me + k - 2 * d) % k
            pltpu.make_async_remote_copy(
                ins[i], outs[i].at[p, srcdev // 2], send_sem.at[i, d], recv_sem.at[i, srcdev],
                device_id=_dev(axis, srcdev), device_id_type=pl.DeviceIdType.MESH,
            ).wait_recv()
        loc.wait()
        c = pltpu.make_async_remote_copy(
            outs[i].at[p], outs[i].at[p], send_sem.at[i, 0], recv_sem.at[i, me],
            device_id=_dev(axis, partner), device_id_type=pl.DeviceIdType.MESH,
        )
        c.start()
        sends.append(c)
    for c in sends:
        if c.is_remote:
            c.wait_send()
        else:
            c.wait()
    for i, (mode, axis) in enumerate(zip(modes, axes)):
        k = lax.axis_size(axis)
        me = lax.axis_index(axis)
        if mode == "pswap":
            partner = me + 1 - 2 * (me % 2)
            pltpu.make_async_remote_copy(
                ins[i], outs[i], send_sem.at[i, 0], recv_sem.at[i, partner],
                device_id=_dev(axis, partner), device_id_type=pl.DeviceIdType.MESH,
            ).wait_recv()
            continue
        if mode == "pscatter":
            for d in range(1, k // 2):
                srcdev = (me + k - 2 * d) % k
                pltpu.make_async_remote_copy(
                    ins[i].at[0], outs[i].at[srcdev // 2], send_sem.at[i, d],
                    recv_sem.at[i, srcdev], device_id=_dev(axis, srcdev),
                    device_id_type=pl.DeviceIdType.MESH,
                ).wait_recv()
            continue
        if mode == "pgather":
            p = me % 2
            partner = me + 1 - 2 * p
            pltpu.make_async_remote_copy(
                outs[i].at[1 - p], outs[i].at[1 - p], send_sem.at[i, 0], recv_sem.at[i, partner],
                device_id=_dev(axis, partner), device_id_type=pl.DeviceIdType.MESH,
            ).wait_recv()
            continue
        m = outs[i].shape[1]
        for d in range(1, k):
            srcdev = (me + k - d) % k
            src = ins[i] if mode == "gather" else ins[i].at[pl.ds(0, m)]
            pltpu.make_async_remote_copy(
                src, outs[i].at[srcdev], send_sem.at[i, d], recv_sem.at[i, srcdev],
                device_id=_dev(axis, srcdev), device_id_type=pl.DeviceIdType.MESH,
            ).wait_recv()


def exchange(items, cid):
    modes = tuple(mode for _, _, mode in items)
    axes = tuple(axis for _, axis, _ in items)
    out_shapes = []
    kmax = 1
    for x, axis, mode in items:
        k = lax.axis_size(axis)
        kmax = max(kmax, k)
        if mode == "gather":
            out_shapes.append(jax.ShapeDtypeStruct((k,) + x.shape, x.dtype))
        elif mode in ("pswap", "pscatter"):
            out_shapes.append(jax.ShapeDtypeStruct(x.shape, x.dtype))
        elif mode == "pgather":
            out_shapes.append(jax.ShapeDtypeStruct((2, k // 2) + x.shape, x.dtype))
        else:
            out_shapes.append(
                jax.ShapeDtypeStruct((k, x.shape[0] // k) + x.shape[1:], x.dtype)
            )
    n = len(items)
    return pl.pallas_call(
        functools.partial(_exchange_kernel, modes, axes),
        out_shape=tuple(out_shapes),
        in_specs=[pl.BlockSpec(memory_space=pl.ANY)] * n,
        out_specs=tuple(pl.BlockSpec(memory_space=pl.ANY) for _ in range(n)),
        scratch_shapes=[
            pltpu.SemaphoreType.DMA((n, kmax)),
            pltpu.SemaphoreType.DMA((n, kmax)),
            pltpu.SemaphoreType.DMA((n,)),
        ],
        compiler_params=pltpu.CompilerParams(collective_id=cid, has_side_effects=True),
    )(*[x for x, _, _ in items])


def pair_order(v):
    return jnp.swapaxes(v, 0, 1).reshape((-1,) + v.shape[3:])


def reduce_scatter(parts, axis, cid, extra=()):
    k = lax.axis_size(axis)
    me = lax.axis_index(axis)
    m = parts.shape[0] // k
    outs = exchange([(parts.astype(WIRE), axis, "scatter")] + list(extra), cid)
    slots = outs[0]
    mine = lax.dynamic_slice_in_dim(parts, me * m, m, axis=0)
    keep = (jnp.arange(k) != me).reshape((k,) + (1,) * (slots.ndim - 1))
    other = jnp.sum(jnp.where(keep, slots.astype(jnp.float32), 0.0), axis=0)
    return (mine + other,) + tuple(outs[1:])


def pair_reduce_scatter(parts, axis, cid, extra=()):
    k = lax.axis_size(axis)
    me = lax.axis_index(axis)
    p = me % 2
    m = parts.shape[0] // k
    quad = parts.reshape((k // 2, 2, m) + parts.shape[1:])
    mine_half = jnp.where(p == 0, quad[:, 0], quad[:, 1])
    theirs_half = jnp.where(p == 0, quad[:, 1], quad[:, 0])
    (got,) = exchange([(theirs_half, axis, "pswap")], cid)
    pair = mine_half + got
    outs = exchange([(pair.astype(WIRE), axis, "pscatter")] + list(extra), cid + 1)
    slots = outs[0]
    own = lax.dynamic_index_in_dim(pair, me // 2, axis=0, keepdims=False)
    keep = (jnp.arange(k // 2) != me // 2).reshape((k // 2,) + (1,) * (slots.ndim - 1))
    other = jnp.sum(jnp.where(keep, slots.astype(jnp.float32), 0.0), axis=0)
    return (own + other,) + tuple(outs[1:])


def per_device(
    stream_in, grad_out, gate_pre, up_pre, keep_mask, segment_ids, norm_gain, w_gate, w_up, w_down
):
    n_row = lax.axis_size("row")
    n_col = lax.axis_size("col")
    tok_col, feat_loc = stream_in.shape
    tok_row, ff_loc = gate_pre.shape
    total = tok_col * n_col
    xs = stream_in.astype(jnp.float32)
    onehot = (segment_ids[:, None] == jnp.arange(SEGS, dtype=jnp.int32)[None, :]).astype(
        jnp.float32
    )
    stats = jnp.concatenate([jnp.sum(xs * xs, axis=1), jnp.sum(onehot, axis=0)])[None, :]
    (stats_all,) = exchange([(stats, "row", "gather")], 0)
    stats_sum = jnp.sum(stats_all, axis=(0, 1))
    squares, counts = stats_sum[:tok_col], stats_sum[tok_col:]
    weights = jnp.sum(onehot * (total / (SEGS * counts))[None, :], axis=1)
    recip = lax.rsqrt(squares / D + eps)
    normed = (xs * recip[:, None] * norm_gain[None, :]).astype(jnp.bfloat16)
    gate_f = gate_pre.astype(jnp.float32)
    up_f = up_pre.astype(jnp.float32)
    sig = jax.nn.sigmoid(gate_f)
    keep_f = keep_mask.astype(jnp.float32) * keep_scale
    dropped = (gate_f * sig * up_f * keep_f * weights[:, None]).astype(jnp.bfloat16)
    cot_full, dropped_full = exchange([(grad_out, "col", "pgather"), (dropped, "row", "gather")], 1)
    cot_full = pair_order(cot_full)
    dropped_full = dropped_full.reshape(total, ff_loc)
    back, normed_full = reduce_scatter(
        over_width(cot_full, w_down), "row", 2, [(normed, "col", "pgather")]
    )
    normed_full = pair_order(normed_full)
    grad_act = back * weights[:, None] * keep_f
    grad_gpre = (grad_act * up_f * sig * (1.0 + gate_f * (1.0 - sig))).astype(jnp.bfloat16)
    grad_upre = (grad_act * gate_f * sig).astype(jnp.bfloat16)
    half = tok_col // 2
    n_chunk = tok_row // tok_col

    def split(v):
        v = v.reshape(n_chunk, 2, half, ff_loc)
        return v[:, 0].reshape(tok_row // 2, ff_loc), v[:, 1].reshape(tok_row // 2, ff_loc)

    def joined(a, b):
        a = a.reshape(n_row, n_chunk, 1, half, ff_loc)
        b = b.reshape(n_row, n_chunk, 1, half, ff_loc)
        return jnp.concatenate([a, b], axis=2).reshape(total, ff_loc)

    gpre_a, gpre_b = split(grad_gpre)
    upre_a, upre_b = split(grad_upre)
    ga_full, ua_full = exchange([(gpre_a, "row", "gather"), (upre_a, "row", "gather")], 3)
    ga_full = ga_full.reshape(total // 2, ff_loc)
    ua_full = ua_full.reshape(total // 2, ff_loc)
    part_a = over_width(ga_full, w_gate) + over_width(ua_full, w_up)
    gn_a, gb_full, ub_full = pair_reduce_scatter(
        part_a, "col", 4, [(gpre_b, "row", "gather"), (upre_b, "row", "gather")]
    )
    gb_full = gb_full.reshape(total // 2, ff_loc)
    ub_full = ub_full.reshape(total // 2, ff_loc)
    part_b = over_width(gb_full, w_gate) + over_width(ub_full, w_up)
    (gn_b,) = pair_reduce_scatter(part_b, "col", 6)
    grad_normed = jnp.concatenate([gn_a, gn_b], axis=0)
    gpre_full = joined(ga_full, gb_full)
    upre_full = joined(ua_full, ub_full)
    grad_down = over_tokens(dropped_full, cot_full).astype(jnp.bfloat16)
    grad_gate = over_tokens(normed_full, gpre_full).astype(jnp.bfloat16)
    grad_up = over_tokens(normed_full, upre_full).astype(jnp.bfloat16)
    scaled = grad_normed * norm_gain[None, :]
    (inner_all,) = exchange([(jnp.sum(scaled * xs, axis=1)[None, :], "row", "gather")], 8)
    inner = jnp.sum(inner_all, axis=(0, 1)) / D
    branch = recip[:, None] * (scaled - xs * (recip * recip * inner)[:, None])
    grad_in = (grad_out.astype(jnp.float32) + branch).astype(jnp.bfloat16)
    return (grad_in, grad_gate, grad_up, grad_down)


def solution(mesh):
    return jax.shard_map(
        per_device,
        mesh=mesh,
        in_specs=(
            P("col", "row"),
            P("col", "row"),
            P("row", "col"),
            P("row", "col"),
            P("row", "col"),
            P("row"),
            P("row"),
            P("row", "col"),
            P("row", "col"),
            P("col", "row"),
        ),
        out_specs=(P("col", "row"), P("row", "col"), P("row", "col"), P("col", "row")),
        check_vma=False,
    )
```

```python
import functools

import jax
import jax.numpy as jnp
from jax import lax
from jax.experimental import pallas as pl
from jax.experimental.pallas import tpu as pltpu
from jax.sharding import PartitionSpec as P

D = 8192
SEGS = 16
AXES = ("row", "col")
WIRE = jnp.bfloat16

eps = 1e-05
keep_scale = 1.0 / 0.9


def over_tokens(left, right):
    return lax.dot_general(
        left, right, (((0,), (0,)), ((), ())), preferred_element_type=jnp.float32
    )


def over_width(left, right):
    return lax.dot_general(
        left, right, (((1,), (1,)), ((), ())), preferred_element_type=jnp.float32
    )


def _dev(axis, idx):
    return tuple(idx if a == axis else lax.axis_index(a) for a in AXES)


def _barrier(modes, axes):
    barrier = pltpu.get_barrier_semaphore()
    count = 0
    for axis in sorted(set(axes)):
        k = lax.axis_size(axis)
        me = lax.axis_index(axis)
        kinds = {mode for mode, a in zip(modes, axes) if a == axis}
        if kinds <= {"pswap"}:
            peers = [1 - 2 * (me % 2)]
        elif kinds <= {"pswap", "pgather", "pscatter"}:
            peers = [2 * d for d in range(1, k // 2)] + [1 - 2 * (me % 2)]
        else:
            peers = list(range(1, k))
        for d in peers:
            pl.semaphore_signal(
                barrier, inc=1, device_id=_dev(axis, (me + d) % k),
                device_id_type=pl.DeviceIdType.MESH,
            )
        count += len(peers)
    pl.semaphore_wait(barrier, count)


def _exchange_kernel(modes, axes, *refs):
    n = len(modes)
    ins, outs = refs[:n], refs[n:2 * n]
    send_sem, recv_sem, local_sem = refs[2 * n:]
    _barrier(modes, axes)
    sends, relays = [], []
    for i, (mode, axis) in enumerate(zip(modes, axes)):
        k = lax.axis_size(axis)
        me = lax.axis_index(axis)
        if mode == "rgather":
            ym, zm = me // 2, me % 2
            ny = k // 2
            direct = [ym * 2 + 1 - zm] + [((ym + dy) % ny) * 2 + z for dy in (1, ny - 1) for z in (0, 1)]
            for d, tgt in enumerate(direct):
                c = pltpu.make_async_remote_copy(
                    ins[i], outs[i].at[me], send_sem.at[i, d], recv_sem.at[i, me],
                    device_id=_dev(axis, tgt), device_id_type=pl.DeviceIdType.MESH,
                )
                c.start()
                sends.append(c)
            loc = pltpu.make_async_copy(ins[i], outs[i].at[me], local_sem.at[i])
            loc.start()
            sends.append(loc)
            m = outs[i].shape[1]
            h = m // 2
            for e, (dy, lo, off) in enumerate([(ny - 1, 0, 0), (1, h, k)]):
                for z in (0, 1):
                    src = ((ym + dy) % ny) * 2 + z
                    pltpu.make_async_remote_copy(
                        ins[i], outs[i].at[src], send_sem.at[i, 0], recv_sem.at[i, src],
                        device_id=_dev(axis, src), device_id_type=pl.DeviceIdType.MESH,
                    ).wait_recv()
                    fwd = ((ym + ny - dy) % ny) * 2 + zm
                    c = pltpu.make_async_remote_copy(
                        outs[i].at[src, pl.ds(lo, h)], outs[i].at[src, pl.ds(lo, h)],
                        send_sem.at[i, k + 2 * e + z], recv_sem.at[i, off + src],
                        device_id=_dev(axis, fwd), device_id_type=pl.DeviceIdType.MESH,
                    )
                    c.start()
                    sends.append(c)
            continue
        if mode == "pswap":
            c = pltpu.make_async_remote_copy(
                ins[i], outs[i], send_sem.at[i, 0], recv_sem.at[i, me],
                device_id=_dev(axis, me + 1 - 2 * (me % 2)),
                device_id_type=pl.DeviceIdType.MESH,
            )
            c.start()
            sends.append(c)
            continue
        if mode == "pscatter":
            for d in range(1, k // 2):
                tgt = (me + 2 * d) % k
                c = pltpu.make_async_remote_copy(
                    ins[i].at[tgt // 2], outs[i].at[me // 2], send_sem.at[i, d],
                    recv_sem.at[i, me], device_id=_dev(axis, tgt),
                    device_id_type=pl.DeviceIdType.MESH,
                )
                c.start()
                sends.append(c)
            continue
        if mode == "pgather":
            p = me % 2
            for d in range(1, k // 2):
                tgt = (me + 2 * d) % k
                c = pltpu.make_async_remote_copy(
                    ins[i], outs[i].at[p, me // 2], send_sem.at[i, d], recv_sem.at[i, me],
                    device_id=_dev(axis, tgt), device_id_type=pl.DeviceIdType.MESH,
                )
                c.start()
                sends.append(c)
            loc = pltpu.make_async_copy(ins[i], outs[i].at[p, me // 2], local_sem.at[i])
            loc.start()
            relays.append((i, loc))
            continue
        m = outs[i].shape[1]
        for d in range(1, k):
            tgt = (me + d) % k
            src = ins[i] if mode == "gather" else ins[i].at[pl.ds(tgt * m, m)]
            c = pltpu.make_async_remote_copy(
                src, outs[i].at[me], send_sem.at[i, d], recv_sem.at[i, me],
                device_id=_dev(axis, tgt), device_id_type=pl.DeviceIdType.MESH,
            )
            c.start()
            sends.append(c)
        if mode == "gather":
            loc = pltpu.make_async_copy(ins[i], outs[i].at[me], local_sem.at[i])
            loc.start()
            sends.append(loc)
    for i, loc in relays:
        axis = axes[i]
        k = lax.axis_size(axis)
        me = lax.axis_index(axis)
        p = me % 2
        partner = me + 1 - 2 * p
        for d in range(1, k // 2):
            srcdev = (me + k - 2 * d) % k
            pltpu.make_async_remote_copy(
                ins[i], outs[i].at[p, srcdev // 2], send_sem.at[i, d], recv_sem.at[i, srcdev],
                device_id=_dev(axis, srcdev), device_id_type=pl.DeviceIdType.MESH,
            ).wait_recv()
        loc.wait()
        c = pltpu.make_async_remote_copy(
            outs[i].at[p], outs[i].at[p], send_sem.at[i, 0], recv_sem.at[i, me],
            device_id=_dev(axis, partner), device_id_type=pl.DeviceIdType.MESH,
        )
        c.start()
        sends.append(c)
    for c in sends:
        if c.is_remote:
            c.wait_send()
        else:
            c.wait()
    for i, (mode, axis) in enumerate(zip(modes, axes)):
        k = lax.axis_size(axis)
        me = lax.axis_index(axis)
        if mode == "rgather":
            ym, zm = me // 2, me % 2
            ny = k // 2
            m = outs[i].shape[1]
            h = m // 2
            partner = ym * 2 + 1 - zm
            pltpu.make_async_remote_copy(
                ins[i], outs[i].at[partner], send_sem.at[i, 0], recv_sem.at[i, partner],
                device_id=_dev(axis, partner), device_id_type=pl.DeviceIdType.MESH,
            ).wait_recv()
            for z in (0, 1):
                far = ((ym + 2) % ny) * 2 + z
                for lo, off in ((0, 0), (h, k)):
                    pltpu.make_async_remote_copy(
                        outs[i].at[far, pl.ds(lo, h)], outs[i].at[far, pl.ds(lo, h)],
                        send_sem.at[i, 0], recv_sem.at[i, off + far],
                        device_id=_dev(axis, far), device_id_type=pl.DeviceIdType.MESH,
                    ).wait_recv()
            continue
        if mode == "pswap":
            partner = me + 1 - 2 * (me % 2)
            pltpu.make_async_remote_copy(
                ins[i], outs[i], send_sem.at[i, 0], recv_sem.at[i, partner],
                device_id=_dev(axis, partner), device_id_type=pl.DeviceIdType.MESH,
            ).wait_recv()
            continue
        if mode == "pscatter":
            for d in range(1, k // 2):
                srcdev = (me + k - 2 * d) % k
                pltpu.make_async_remote_copy(
                    ins[i].at[0], outs[i].at[srcdev // 2], send_sem.at[i, d],
                    recv_sem.at[i, srcdev], device_id=_dev(axis, srcdev),
                    device_id_type=pl.DeviceIdType.MESH,
                ).wait_recv()
            continue
        if mode == "pgather":
            p = me % 2
            partner = me + 1 - 2 * p
            pltpu.make_async_remote_copy(
                outs[i].at[1 - p], outs[i].at[1 - p], send_sem.at[i, 0], recv_sem.at[i, partner],
                device_id=_dev(axis, partner), device_id_type=pl.DeviceIdType.MESH,
            ).wait_recv()
            continue
        m = outs[i].shape[1]
        for d in range(1, k):
            srcdev = (me + k - d) % k
            src = ins[i] if mode == "gather" else ins[i].at[pl.ds(0, m)]
            pltpu.make_async_remote_copy(
                src, outs[i].at[srcdev], send_sem.at[i, d], recv_sem.at[i, srcdev],
                device_id=_dev(axis, srcdev), device_id_type=pl.DeviceIdType.MESH,
            ).wait_recv()


def exchange(items, cid):
    modes = tuple(mode for _, _, mode in items)
    axes = tuple(axis for _, axis, _ in items)
    out_shapes = []
    kmax = 1
    for x, axis, mode in items:
        k = lax.axis_size(axis)
        kmax = max(kmax, k)
        if mode in ("gather", "rgather"):
            out_shapes.append(jax.ShapeDtypeStruct((k,) + x.shape, x.dtype))
        elif mode in ("pswap", "pscatter"):
            out_shapes.append(jax.ShapeDtypeStruct(x.shape, x.dtype))
        elif mode == "pgather":
            out_shapes.append(jax.ShapeDtypeStruct((2, k // 2) + x.shape, x.dtype))
        else:
            out_shapes.append(
                jax.ShapeDtypeStruct((k, x.shape[0] // k) + x.shape[1:], x.dtype)
            )
    n = len(items)
    return pl.pallas_call(
        functools.partial(_exchange_kernel, modes, axes),
        out_shape=tuple(out_shapes),
        in_specs=[pl.BlockSpec(memory_space=pl.ANY)] * n,
        out_specs=tuple(pl.BlockSpec(memory_space=pl.ANY) for _ in range(n)),
        scratch_shapes=[
            pltpu.SemaphoreType.DMA((n, 2 * kmax)),
            pltpu.SemaphoreType.DMA((n, 2 * kmax)),
            pltpu.SemaphoreType.DMA((n,)),
        ],
        compiler_params=pltpu.CompilerParams(collective_id=cid, has_side_effects=True),
    )(*[x for x, _, _ in items])


def pair_order(v):
    return jnp.swapaxes(v, 0, 1).reshape((-1,) + v.shape[3:])


def reduce_scatter(parts, axis, cid, extra=()):
    k = lax.axis_size(axis)
    me = lax.axis_index(axis)
    m = parts.shape[0] // k
    outs = exchange([(parts.astype(WIRE), axis, "scatter")] + list(extra), cid)
    slots = outs[0]
    mine = lax.dynamic_slice_in_dim(parts, me * m, m, axis=0)
    keep = (jnp.arange(k) != me).reshape((k,) + (1,) * (slots.ndim - 1))
    other = jnp.sum(jnp.where(keep, slots.astype(jnp.float32), 0.0), axis=0)
    return (mine + other,) + tuple(outs[1:])


def pair_reduce_scatter(parts, axis, cid, extra=()):
    k = lax.axis_size(axis)
    me = lax.axis_index(axis)
    p = me % 2
    m = parts.shape[0] // k
    quad = parts.reshape((k // 2, 2, m) + parts.shape[1:])
    mine_half = jnp.where(p == 0, quad[:, 0], quad[:, 1])
    theirs_half = jnp.where(p == 0, quad[:, 1], quad[:, 0])
    (got,) = exchange([(theirs_half, axis, "pswap")], cid)
    pair = mine_half + got
    outs = exchange([(pair.astype(WIRE), axis, "pscatter")] + list(extra), cid + 1)
    slots = outs[0]
    own = lax.dynamic_index_in_dim(pair, me // 2, axis=0, keepdims=False)
    keep = (jnp.arange(k // 2) != me // 2).reshape((k // 2,) + (1,) * (slots.ndim - 1))
    other = jnp.sum(jnp.where(keep, slots.astype(jnp.float32), 0.0), axis=0)
    return (own + other,) + tuple(outs[1:])


def per_device(
    stream_in, grad_out, gate_pre, up_pre, keep_mask, segment_ids, norm_gain, w_gate, w_up, w_down
):
    n_row = lax.axis_size("row")
    n_col = lax.axis_size("col")
    RG = "rgather" if n_row == 8 else "gather"
    tok_col, feat_loc = stream_in.shape
    tok_row, ff_loc = gate_pre.shape
    total = tok_col * n_col
    xs = stream_in.astype(jnp.float32)
    onehot = (segment_ids[:, None] == jnp.arange(SEGS, dtype=jnp.int32)[None, :]).astype(
        jnp.float32
    )
    stats = jnp.concatenate([jnp.sum(xs * xs, axis=1), jnp.sum(onehot, axis=0)])[None, :]
    (stats_all,) = exchange([(stats, "row", "gather")], 0)
    stats_sum = jnp.sum(stats_all, axis=(0, 1))
    squares, counts = stats_sum[:tok_col], stats_sum[tok_col:]
    weights = jnp.sum(onehot * (total / (SEGS * counts))[None, :], axis=1)
    recip = lax.rsqrt(squares / D + eps)
    normed = (xs * recip[:, None] * norm_gain[None, :]).astype(jnp.bfloat16)
    gate_f = gate_pre.astype(jnp.float32)
    up_f = up_pre.astype(jnp.float32)
    sig = jax.nn.sigmoid(gate_f)
    keep_f = keep_mask.astype(jnp.float32) * keep_scale
    dropped = (gate_f * sig * up_f * keep_f * weights[:, None]).astype(jnp.bfloat16)
    cot_full, dropped_full = exchange([(grad_out, "col", "pgather"), (dropped, "row", RG)], 1)
    cot_full = pair_order(cot_full)
    dropped_full = dropped_full.reshape(total, ff_loc)
    back, normed_full = reduce_scatter(
        over_width(cot_full, w_down), "row", 2, [(normed, "col", "pgather")]
    )
    normed_full = pair_order(normed_full)
    grad_act = back * weights[:, None] * keep_f
    grad_gpre = (grad_act * up_f * sig * (1.0 + gate_f * (1.0 - sig))).astype(jnp.bfloat16)
    grad_upre = (grad_act * gate_f * sig).astype(jnp.bfloat16)
    half = tok_col // 2
    n_chunk = tok_row // tok_col

    def split(v):
        v = v.reshape(n_chunk, 2, half, ff_loc)
        return v[:, 0].reshape(tok_row // 2, ff_loc), v[:, 1].reshape(tok_row // 2, ff_loc)

    def joined(a, b):
        a = a.reshape(n_row, n_chunk, 1, half, ff_loc)
        b = b.reshape(n_row, n_chunk, 1, half, ff_loc)
        return jnp.concatenate([a, b], axis=2).reshape(total, ff_loc)

    gpre_a, gpre_b = split(grad_gpre)
    upre_a, upre_b = split(grad_upre)
    ga_full, ua_full = exchange([(gpre_a, "row", RG), (upre_a, "row", RG)], 3)
    ga_full = ga_full.reshape(total // 2, ff_loc)
    ua_full = ua_full.reshape(total // 2, ff_loc)
    part_a = over_width(ga_full, w_gate) + over_width(ua_full, w_up)
    gn_a, gb_full, ub_full = pair_reduce_scatter(
        part_a, "col", 4, [(gpre_b, "row", RG), (upre_b, "row", RG)]
    )
    gb_full = gb_full.reshape(total // 2, ff_loc)
    ub_full = ub_full.reshape(total // 2, ff_loc)
    part_b = over_width(gb_full, w_gate) + over_width(ub_full, w_up)
    (gn_b,) = pair_reduce_scatter(part_b, "col", 6)
    grad_normed = jnp.concatenate([gn_a, gn_b], axis=0)
    gpre_full = joined(ga_full, gb_full)
    upre_full = joined(ua_full, ub_full)
    grad_down = over_tokens(dropped_full, cot_full).astype(jnp.bfloat16)
    grad_gate = over_tokens(normed_full, gpre_full).astype(jnp.bfloat16)
    grad_up = over_tokens(normed_full, upre_full).astype(jnp.bfloat16)
    scaled = grad_normed * norm_gain[None, :]
    (inner_all,) = exchange([(jnp.sum(scaled * xs, axis=1)[None, :], "row", "gather")], 8)
    inner = jnp.sum(inner_all, axis=(0, 1)) / D
    branch = recip[:, None] * (scaled - xs * (recip * recip * inner)[:, None])
    grad_in = (grad_out.astype(jnp.float32) + branch).astype(jnp.bfloat16)
    return (grad_in, grad_gate, grad_up, grad_down)


def solution(mesh):
    return jax.shard_map(
        per_device,
        mesh=mesh,
        in_specs=(
            P("col", "row"),
            P("col", "row"),
            P("row", "col"),
            P("row", "col"),
            P("row", "col"),
            P("row"),
            P("row"),
            P("row", "col"),
            P("row", "col"),
            P("col", "row"),
        ),
        out_specs=(P("col", "row"), P("row", "col"), P("row", "col"), P("col", "row")),
        check_vma=False,
    )
```

```python
import functools

import jax
import jax.numpy as jnp
from jax import lax
from jax.experimental import pallas as pl
from jax.experimental.pallas import tpu as pltpu
from jax.sharding import PartitionSpec as P

D = 8192
SEGS = 16
AXES = ("row", "col")
WIRE = jnp.bfloat16

eps = 1e-05
keep_scale = 1.0 / 0.9


def over_tokens(left, right):
    return lax.dot_general(
        left, right, (((0,), (0,)), ((), ())), preferred_element_type=jnp.float32
    )


def over_width(left, right):
    return lax.dot_general(
        left, right, (((1,), (1,)), ((), ())), preferred_element_type=jnp.float32
    )


def _dev(axis, idx):
    return tuple(idx if a == axis else lax.axis_index(a) for a in AXES)


def _barrier(modes, axes):
    barrier = pltpu.get_barrier_semaphore()
    count = 0
    for axis in sorted(set(axes)):
        k = lax.axis_size(axis)
        me = lax.axis_index(axis)
        kinds = {mode for mode, a in zip(modes, axes) if a == axis}
        if kinds <= {"pswap"}:
            peers = [1 - 2 * (me % 2)]
        elif kinds <= {"pswap", "pgather", "pscatter", "prgather"}:
            peers = [2 * d for d in range(1, k // 2)] + [1 - 2 * (me % 2)]
        else:
            peers = list(range(1, k))
        for d in peers:
            pl.semaphore_signal(
                barrier, inc=1, device_id=_dev(axis, (me + d) % k),
                device_id_type=pl.DeviceIdType.MESH,
            )
        count += len(peers)
    pl.semaphore_wait(barrier, count)


def _ring_pair_send(i, src_ref, slot, dev, me_g, ng, send_sem, recv_sem, sends, axis):
    ny = ng // 2
    ym, zm = me_g // 2, me_g % 2
    direct = [ym * 2 + 1 - zm] + [((ym + dy) % ny) * 2 + z for dy in (1, ny - 1) for z in (0, 1)]
    for d, tgt in enumerate(direct):
        c = pltpu.make_async_remote_copy(
            src_ref, slot(me_g), send_sem.at[i, d], recv_sem.at[i, me_g],
            device_id=_dev(axis, dev(tgt)), device_id_type=pl.DeviceIdType.MESH,
        )
        c.start()
        sends.append(c)
    h = src_ref.shape[0] // 2
    for e, (dy, lo, off) in enumerate([(ny - 1, 0, 0), (1, h, ng)]):
        for z in (0, 1):
            src = ((ym + dy) % ny) * 2 + z
            pltpu.make_async_remote_copy(
                src_ref, slot(src), send_sem.at[i, 0], recv_sem.at[i, src],
                device_id=_dev(axis, dev(src)), device_id_type=pl.DeviceIdType.MESH,
            ).wait_recv()
            fwd = ((ym + ny - dy) % ny) * 2 + zm
            c = pltpu.make_async_remote_copy(
                slot(src).at[pl.ds(lo, h)], slot(src).at[pl.ds(lo, h)],
                send_sem.at[i, ng + 2 * e + z], recv_sem.at[i, off + src],
                device_id=_dev(axis, dev(fwd)), device_id_type=pl.DeviceIdType.MESH,
            )
            c.start()
            sends.append(c)


def _ring_pair_wait(i, src_ref, slot, dev, me_g, ng, send_sem, recv_sem, axis):
    ny = ng // 2
    ym, zm = me_g // 2, me_g % 2
    h = src_ref.shape[0] // 2
    peer = ym * 2 + 1 - zm
    pltpu.make_async_remote_copy(
        src_ref, slot(peer), send_sem.at[i, 0], recv_sem.at[i, peer],
        device_id=_dev(axis, dev(peer)), device_id_type=pl.DeviceIdType.MESH,
    ).wait_recv()
    for z in (0, 1):
        far = ((ym + 2) % ny) * 2 + z
        for lo, off in ((0, 0), (h, ng)):
            pltpu.make_async_remote_copy(
                slot(far).at[pl.ds(lo, h)], slot(far).at[pl.ds(lo, h)],
                send_sem.at[i, 0], recv_sem.at[i, off + far],
                device_id=_dev(axis, dev(far)), device_id_type=pl.DeviceIdType.MESH,
            ).wait_recv()


def _exchange_kernel(modes, axes, *refs):
    n = len(modes)
    ins, outs = refs[:n], refs[n:2 * n]
    send_sem, recv_sem, local_sem = refs[2 * n:]
    _barrier(modes, axes)
    sends, relays = [], []
    for i, (mode, axis) in enumerate(zip(modes, axes)):
        k = lax.axis_size(axis)
        me = lax.axis_index(axis)
        if mode == "rgather":
            loc = pltpu.make_async_copy(ins[i], outs[i].at[me], local_sem.at[i])
            loc.start()
            sends.append(loc)
            _ring_pair_send(i, ins[i], lambda g: outs[i].at[g], lambda g: g, me, k,
                            send_sem, recv_sem, sends, axis)
            continue
        if mode == "prgather":
            p = me % 2
            partner = me + 1 - 2 * p
            slot = lambda g: outs[i].at[p, g]
            dev = lambda g: g * 2 + p
            loc = pltpu.make_async_copy(ins[i], slot(me // 2), local_sem.at[i])
            loc.start()
            _ring_pair_send(i, ins[i], slot, dev, me // 2, k // 2, send_sem, recv_sem, sends, axis)
            _ring_pair_wait(i, ins[i], slot, dev, me // 2, k // 2, send_sem, recv_sem, axis)
            loc.wait()
            c = pltpu.make_async_remote_copy(
                outs[i].at[p], outs[i].at[p], send_sem.at[i, 2 * k - 1], recv_sem.at[i, 2 * k - 1],
                device_id=_dev(axis, partner), device_id_type=pl.DeviceIdType.MESH,
            )
            c.start()
            sends.append(c)
            continue
        if mode == "pswap":
            c = pltpu.make_async_remote_copy(
                ins[i], outs[i], send_sem.at[i, 0], recv_sem.at[i, me],
                device_id=_dev(axis, me + 1 - 2 * (me % 2)),
                device_id_type=pl.DeviceIdType.MESH,
            )
            c.start()
            sends.append(c)
            continue
        if mode == "pscatter":
            for d in range(1, k // 2):
                tgt = (me + 2 * d) % k
                c = pltpu.make_async_remote_copy(
                    ins[i].at[tgt // 2], outs[i].at[me // 2], send_sem.at[i, d],
                    recv_sem.at[i, me], device_id=_dev(axis, tgt),
                    device_id_type=pl.DeviceIdType.MESH,
                )
                c.start()
                sends.append(c)
            continue
        if mode == "pgather":
            p = me % 2
            for d in range(1, k // 2):
                tgt = (me + 2 * d) % k
                c = pltpu.make_async_remote_copy(
                    ins[i], outs[i].at[p, me // 2], send_sem.at[i, d], recv_sem.at[i, me],
                    device_id=_dev(axis, tgt), device_id_type=pl.DeviceIdType.MESH,
                )
                c.start()
                sends.append(c)
            loc = pltpu.make_async_copy(ins[i], outs[i].at[p, me // 2], local_sem.at[i])
            loc.start()
            relays.append((i, loc))
            continue
        m = outs[i].shape[1]
        for d in range(1, k):
            tgt = (me + d) % k
            src = ins[i] if mode == "gather" else ins[i].at[pl.ds(tgt * m, m)]
            c = pltpu.make_async_remote_copy(
                src, outs[i].at[me], send_sem.at[i, d], recv_sem.at[i, me],
                device_id=_dev(axis, tgt), device_id_type=pl.DeviceIdType.MESH,
            )
            c.start()
            sends.append(c)
        if mode == "gather":
            loc = pltpu.make_async_copy(ins[i], outs[i].at[me], local_sem.at[i])
            loc.start()
            sends.append(loc)
    for i, loc in relays:
        axis = axes[i]
        k = lax.axis_size(axis)
        me = lax.axis_index(axis)
        p = me % 2
        partner = me + 1 - 2 * p
        for d in range(1, k // 2):
            srcdev = (me + k - 2 * d) % k
            pltpu.make_async_remote_copy(
                ins[i], outs[i].at[p, srcdev // 2], send_sem.at[i, d], recv_sem.at[i, srcdev],
                device_id=_dev(axis, srcdev), device_id_type=pl.DeviceIdType.MESH,
            ).wait_recv()
        loc.wait()
        c = pltpu.make_async_remote_copy(
            outs[i].at[p], outs[i].at[p], send_sem.at[i, 0], recv_sem.at[i, me],
            device_id=_dev(axis, partner), device_id_type=pl.DeviceIdType.MESH,
        )
        c.start()
        sends.append(c)
    for c in sends:
        if c.is_remote:
            c.wait_send()
        else:
            c.wait()
    for i, (mode, axis) in enumerate(zip(modes, axes)):
        k = lax.axis_size(axis)
        me = lax.axis_index(axis)
        if mode == "rgather":
            _ring_pair_wait(i, ins[i], lambda g: outs[i].at[g], lambda g: g, me, k,
                            send_sem, recv_sem, axis)
            continue
        if mode == "prgather":
            p = me % 2
            partner = me + 1 - 2 * p
            pltpu.make_async_remote_copy(
                outs[i].at[1 - p], outs[i].at[1 - p], send_sem.at[i, 2 * k - 1],
                recv_sem.at[i, 2 * k - 1],
                device_id=_dev(axis, partner), device_id_type=pl.DeviceIdType.MESH,
            ).wait_recv()
            continue
        if mode == "pswap":
            partner = me + 1 - 2 * (me % 2)
            pltpu.make_async_remote_copy(
                ins[i], outs[i], send_sem.at[i, 0], recv_sem.at[i, partner],
                device_id=_dev(axis, partner), device_id_type=pl.DeviceIdType.MESH,
            ).wait_recv()
            continue
        if mode == "pscatter":
            for d in range(1, k // 2):
                srcdev = (me + k - 2 * d) % k
                pltpu.make_async_remote_copy(
                    ins[i].at[0], outs[i].at[srcdev // 2], send_sem.at[i, d],
                    recv_sem.at[i, srcdev], device_id=_dev(axis, srcdev),
                    device_id_type=pl.DeviceIdType.MESH,
                ).wait_recv()
            continue
        if mode == "pgather":
            p = me % 2
            partner = me + 1 - 2 * p
            pltpu.make_async_remote_copy(
                outs[i].at[1 - p], outs[i].at[1 - p], send_sem.at[i, 0], recv_sem.at[i, partner],
                device_id=_dev(axis, partner), device_id_type=pl.DeviceIdType.MESH,
            ).wait_recv()
            continue
        m = outs[i].shape[1]
        for d in range(1, k):
            srcdev = (me + k - d) % k
            src = ins[i] if mode == "gather" else ins[i].at[pl.ds(0, m)]
            pltpu.make_async_remote_copy(
                src, outs[i].at[srcdev], send_sem.at[i, d], recv_sem.at[i, srcdev],
                device_id=_dev(axis, srcdev), device_id_type=pl.DeviceIdType.MESH,
            ).wait_recv()


def exchange(items, cid):
    modes = tuple(mode for _, _, mode in items)
    axes = tuple(axis for _, axis, _ in items)
    out_shapes = []
    kmax = 1
    for x, axis, mode in items:
        k = lax.axis_size(axis)
        kmax = max(kmax, k)
        if mode in ("gather", "rgather"):
            out_shapes.append(jax.ShapeDtypeStruct((k,) + x.shape, x.dtype))
        elif mode in ("pswap", "pscatter"):
            out_shapes.append(jax.ShapeDtypeStruct(x.shape, x.dtype))
        elif mode in ("pgather", "prgather"):
            out_shapes.append(jax.ShapeDtypeStruct((2, k // 2) + x.shape, x.dtype))
        else:
            out_shapes.append(
                jax.ShapeDtypeStruct((k, x.shape[0] // k) + x.shape[1:], x.dtype)
            )
    n = len(items)
    return pl.pallas_call(
        functools.partial(_exchange_kernel, modes, axes),
        out_shape=tuple(out_shapes),
        in_specs=[pl.BlockSpec(memory_space=pl.ANY)] * n,
        out_specs=tuple(pl.BlockSpec(memory_space=pl.ANY) for _ in range(n)),
        scratch_shapes=[
            pltpu.SemaphoreType.DMA((n, 2 * kmax)),
            pltpu.SemaphoreType.DMA((n, 2 * kmax)),
            pltpu.SemaphoreType.DMA((n,)),
        ],
        compiler_params=pltpu.CompilerParams(collective_id=cid, has_side_effects=True),
    )(*[x for x, _, _ in items])


def pair_order(v):
    return jnp.swapaxes(v, 0, 1).reshape((-1,) + v.shape[3:])


def reduce_scatter(parts, axis, cid, extra=()):
    k = lax.axis_size(axis)
    me = lax.axis_index(axis)
    m = parts.shape[0] // k
    outs = exchange([(parts.astype(WIRE), axis, "scatter")] + list(extra), cid)
    slots = outs[0]
    mine = lax.dynamic_slice_in_dim(parts, me * m, m, axis=0)
    keep = (jnp.arange(k) != me).reshape((k,) + (1,) * (slots.ndim - 1))
    other = jnp.sum(jnp.where(keep, slots.astype(jnp.float32), 0.0), axis=0)
    return (mine + other,) + tuple(outs[1:])


def pair_reduce_scatter(parts, axis, cid, extra=()):
    k = lax.axis_size(axis)
    me = lax.axis_index(axis)
    p = me % 2
    m = parts.shape[0] // k
    quad = parts.reshape((k // 2, 2, m) + parts.shape[1:])
    mine_half = jnp.where(p == 0, quad[:, 0], quad[:, 1])
    theirs_half = jnp.where(p == 0, quad[:, 1], quad[:, 0])
    (got,) = exchange([(theirs_half, axis, "pswap")], cid)
    pair = mine_half + got
    outs = exchange([(pair.astype(WIRE), axis, "pscatter")] + list(extra), cid + 1)
    slots = outs[0]
    own = lax.dynamic_index_in_dim(pair, me // 2, axis=0, keepdims=False)
    keep = (jnp.arange(k // 2) != me // 2).reshape((k // 2,) + (1,) * (slots.ndim - 1))
    other = jnp.sum(jnp.where(keep, slots.astype(jnp.float32), 0.0), axis=0)
    return (own + other,) + tuple(outs[1:])


def per_device(
    stream_in, grad_out, gate_pre, up_pre, keep_mask, segment_ids, norm_gain, w_gate, w_up, w_down
):
    n_row = lax.axis_size("row")
    n_col = lax.axis_size("col")
    RG = "rgather" if n_row == 8 else "gather"
    PG = "prgather" if n_col == 16 else "pgather"
    tok_col, feat_loc = stream_in.shape
    tok_row, ff_loc = gate_pre.shape
    total = tok_col * n_col
    xs = stream_in.astype(jnp.float32)
    onehot = (segment_ids[:, None] == jnp.arange(SEGS, dtype=jnp.int32)[None, :]).astype(
        jnp.float32
    )
    stats = jnp.concatenate([jnp.sum(xs * xs, axis=1), jnp.sum(onehot, axis=0)])[None, :]
    (stats_all,) = exchange([(stats, "row", "gather")], 0)
    stats_sum = jnp.sum(stats_all, axis=(0, 1))
    squares, counts = stats_sum[:tok_col], stats_sum[tok_col:]
    weights = jnp.sum(onehot * (total / (SEGS * counts))[None, :], axis=1)
    recip = lax.rsqrt(squares / D + eps)
    normed = (xs * recip[:, None] * norm_gain[None, :]).astype(jnp.bfloat16)
    gate_f = gate_pre.astype(jnp.float32)
    up_f = up_pre.astype(jnp.float32)
    sig = jax.nn.sigmoid(gate_f)
    keep_f = keep_mask.astype(jnp.float32) * keep_scale
    dropped = (gate_f * sig * up_f * keep_f * weights[:, None]).astype(jnp.bfloat16)
    cot_full, dropped_full = exchange([(grad_out, "col", PG), (dropped, "row", RG)], 1)
    cot_full = pair_order(cot_full)
    dropped_full = dropped_full.reshape(total, ff_loc)
    back, normed_full = reduce_scatter(
        over_width(cot_full, w_down), "row", 2, [(normed, "col", PG)]
    )
    normed_full = pair_order(normed_full)
    grad_act = back * weights[:, None] * keep_f
    grad_gpre = (grad_act * up_f * sig * (1.0 + gate_f * (1.0 - sig))).astype(jnp.bfloat16)
    grad_upre = (grad_act * gate_f * sig).astype(jnp.bfloat16)
    half = tok_col // 2
    n_chunk = tok_row // tok_col

    def split(v):
        v = v.reshape(n_chunk, 2, half, ff_loc)
        return v[:, 0].reshape(tok_row // 2, ff_loc), v[:, 1].reshape(tok_row // 2, ff_loc)

    def joined(a, b):
        a = a.reshape(n_row, n_chunk, 1, half, ff_loc)
        b = b.reshape(n_row, n_chunk, 1, half, ff_loc)
        return jnp.concatenate([a, b], axis=2).reshape(total, ff_loc)

    gpre_a, gpre_b = split(grad_gpre)
    upre_a, upre_b = split(grad_upre)
    ga_full, ua_full = exchange([(gpre_a, "row", RG), (upre_a, "row", RG)], 3)
    ga_full = ga_full.reshape(total // 2, ff_loc)
    ua_full = ua_full.reshape(total // 2, ff_loc)
    part_a = over_width(ga_full, w_gate) + over_width(ua_full, w_up)
    gn_a, gb_full, ub_full = pair_reduce_scatter(
        part_a, "col", 4, [(gpre_b, "row", RG), (upre_b, "row", RG)]
    )
    gb_full = gb_full.reshape(total // 2, ff_loc)
    ub_full = ub_full.reshape(total // 2, ff_loc)
    part_b = over_width(gb_full, w_gate) + over_width(ub_full, w_up)
    (gn_b,) = pair_reduce_scatter(part_b, "col", 6)
    grad_normed = jnp.concatenate([gn_a, gn_b], axis=0)
    gpre_full = joined(ga_full, gb_full)
    upre_full = joined(ua_full, ub_full)
    grad_down = over_tokens(dropped_full, cot_full).astype(jnp.bfloat16)
    grad_gate = over_tokens(normed_full, gpre_full).astype(jnp.bfloat16)
    grad_up = over_tokens(normed_full, upre_full).astype(jnp.bfloat16)
    scaled = grad_normed * norm_gain[None, :]
    (inner_all,) = exchange([(jnp.sum(scaled * xs, axis=1)[None, :], "row", "gather")], 8)
    inner = jnp.sum(inner_all, axis=(0, 1)) / D
    branch = recip[:, None] * (scaled - xs * (recip * recip * inner)[:, None])
    grad_in = (grad_out.astype(jnp.float32) + branch).astype(jnp.bfloat16)
    return (grad_in, grad_gate, grad_up, grad_down)


def solution(mesh):
    return jax.shard_map(
        per_device,
        mesh=mesh,
        in_specs=(
            P("col", "row"),
            P("col", "row"),
            P("row", "col"),
            P("row", "col"),
            P("row", "col"),
            P("row"),
            P("row"),
            P("row", "col"),
            P("row", "col"),
            P("col", "row"),
        ),
        out_specs=(P("col", "row"), P("row", "col"), P("row", "col"), P("col", "row")),
        check_vma=False,
    )
```

```python
import functools

import jax
import jax.numpy as jnp
from jax import lax
from jax.experimental import pallas as pl
from jax.experimental.pallas import tpu as pltpu
from jax.sharding import PartitionSpec as P

D = 8192
SEGS = 16
AXES = ("row", "col")
WIRE = jnp.bfloat16

eps = 1e-05
keep_scale = 1.0 / 0.9


def over_tokens(left, right):
    return lax.dot_general(
        left, right, (((0,), (0,)), ((), ())), preferred_element_type=jnp.float32
    )


def over_width(left, right):
    return lax.dot_general(
        left, right, (((1,), (1,)), ((), ())), preferred_element_type=jnp.float32
    )


def _dev(axis, idx):
    return tuple(idx if a == axis else lax.axis_index(a) for a in AXES)


def _barrier(modes, axes):
    barrier = pltpu.get_barrier_semaphore()
    count = 0
    for axis in sorted(set(axes)):
        k = lax.axis_size(axis)
        me = lax.axis_index(axis)
        kinds = {mode for mode, a in zip(modes, axes) if a == axis}
        if kinds <= {"pswap"}:
            peers = [1 - 2 * (me % 2)]
        elif kinds <= {"pswap", "pgather", "pscatter", "prgather"}:
            peers = [2 * d for d in range(1, k // 2)] + [1 - 2 * (me % 2)]
        else:
            peers = list(range(1, k))
        for d in peers:
            pl.semaphore_signal(
                barrier, inc=1, device_id=_dev(axis, (me + d) % k),
                device_id_type=pl.DeviceIdType.MESH,
            )
        count += len(peers)
    pl.semaphore_wait(barrier, count)


def _ring_pair_send(i, src_ref, slot, dev, me_g, ng, send_sem, recv_sem, sends, axis):
    ny = ng // 2
    ym, zm = me_g // 2, me_g % 2
    direct = [ym * 2 + 1 - zm] + [((ym + dy) % ny) * 2 + z for dy in (1, ny - 1) for z in (0, 1)]
    for d, tgt in enumerate(direct):
        c = pltpu.make_async_remote_copy(
            src_ref, slot(me_g), send_sem.at[i, d], recv_sem.at[i, me_g],
            device_id=_dev(axis, dev(tgt)), device_id_type=pl.DeviceIdType.MESH,
        )
        c.start()
        sends.append(c)
    h = src_ref.shape[0] // 2
    for e, (dy, lo, off) in enumerate([(ny - 1, 0, 0), (1, h, ng)]):
        for z in (0, 1):
            src = ((ym + dy) % ny) * 2 + z
            pltpu.make_async_remote_copy(
                src_ref, slot(src), send_sem.at[i, 0], recv_sem.at[i, src],
                device_id=_dev(axis, dev(src)), device_id_type=pl.DeviceIdType.MESH,
            ).wait_recv()
            fwd = ((ym + ny - dy) % ny) * 2 + zm
            c = pltpu.make_async_remote_copy(
                slot(src).at[pl.ds(lo, h)], slot(src).at[pl.ds(lo, h)],
                send_sem.at[i, ng + 2 * e + z], recv_sem.at[i, off + src],
                device_id=_dev(axis, dev(fwd)), device_id_type=pl.DeviceIdType.MESH,
            )
            c.start()
            sends.append(c)


def _ring_pair_wait(i, src_ref, slot, dev, me_g, ng, send_sem, recv_sem, axis):
    ny = ng // 2
    ym, zm = me_g // 2, me_g % 2
    h = src_ref.shape[0] // 2
    peer = ym * 2 + 1 - zm
    pltpu.make_async_remote_copy(
        src_ref, slot(peer), send_sem.at[i, 0], recv_sem.at[i, peer],
        device_id=_dev(axis, dev(peer)), device_id_type=pl.DeviceIdType.MESH,
    ).wait_recv()
    for z in (0, 1):
        far = ((ym + 2) % ny) * 2 + z
        for lo, off in ((0, 0), (h, ng)):
            pltpu.make_async_remote_copy(
                slot(far).at[pl.ds(lo, h)], slot(far).at[pl.ds(lo, h)],
                send_sem.at[i, 0], recv_sem.at[i, off + far],
                device_id=_dev(axis, dev(far)), device_id_type=pl.DeviceIdType.MESH,
            ).wait_recv()


def _exchange_kernel(modes, axes, *refs):
    n = len(modes)
    ins, outs = refs[:n], refs[n:2 * n]
    send_sem, recv_sem, local_sem = refs[2 * n:]
    _barrier(modes, axes)
    sends, relays = [], []
    for i, (mode, axis) in enumerate(zip(modes, axes)):
        k = lax.axis_size(axis)
        me = lax.axis_index(axis)
        if mode == "rscatter":
            ny = k // 2
            ym, zm = me // 2, me % 2
            m = outs[i].shape[1]
            h = m // 2
            direct = [ym * 2 + 1 - zm] + [((ym + dy) % ny) * 2 + z for dy in (1, ny - 1) for z in (0, 1)]
            for d, tgt in enumerate(direct):
                c = pltpu.make_async_remote_copy(
                    ins[i].at[pl.ds(tgt * m, m)], outs[i].at[me], send_sem.at[i, d],
                    recv_sem.at[i, me], device_id=_dev(axis, tgt),
                    device_id_type=pl.DeviceIdType.MESH,
                )
                c.start()
                sends.append(c)
            for zt in (0, 1):
                far = ((ym + 2) % ny) * 2 + zt
                for e, (dy, lo) in enumerate(((1, 0), (ny - 1, h))):
                    relay = ((ym + dy) % ny) * 2 + zt
                    c = pltpu.make_async_remote_copy(
                        ins[i].at[pl.ds(far * m + lo, h)], outs[i].at[k + e, pl.ds(zm * h, h)],
                        send_sem.at[i, 5 + 2 * e + zt], recv_sem.at[i, 3 * k + 2 * e + zm],
                        device_id=_dev(axis, relay), device_id_type=pl.DeviceIdType.MESH,
                    )
                    c.start()
                    sends.append(c)
            for e, (dy, lo, off) in enumerate(((ny - 1, 0, k), (1, h, 2 * k))):
                for z in (0, 1):
                    src = ((ym + dy) % ny) * 2 + z
                    buf = outs[i].at[k + e, pl.ds(z * h, h)]
                    pltpu.make_async_remote_copy(
                        buf, buf, send_sem.at[i, 0], recv_sem.at[i, 3 * k + 2 * e + z],
                        device_id=_dev(axis, src), device_id_type=pl.DeviceIdType.MESH,
                    ).wait_recv()
                    tgt = ((ym + ny - dy) % ny) * 2 + zm
                    c = pltpu.make_async_remote_copy(
                        buf, outs[i].at[src, pl.ds(lo, h)], send_sem.at[i, 9 + 2 * e + z],
                        recv_sem.at[i, off + src], device_id=_dev(axis, tgt),
                        device_id_type=pl.DeviceIdType.MESH,
                    )
                    c.start()
                    sends.append(c)
            continue
        if mode == "rgather":
            loc = pltpu.make_async_copy(ins[i], outs[i].at[me], local_sem.at[i])
            loc.start()
            sends.append(loc)
            _ring_pair_send(i, ins[i], lambda g: outs[i].at[g], lambda g: g, me, k,
                            send_sem, recv_sem, sends, axis)
            continue
        if mode == "prgather":
            p = me % 2
            partner = me + 1 - 2 * p
            slot = lambda g: outs[i].at[p, g]
            dev = lambda g: g * 2 + p
            loc = pltpu.make_async_copy(ins[i], slot(me // 2), local_sem.at[i])
            loc.start()
            _ring_pair_send(i, ins[i], slot, dev, me // 2, k // 2, send_sem, recv_sem, sends, axis)
            _ring_pair_wait(i, ins[i], slot, dev, me // 2, k // 2, send_sem, recv_sem, axis)
            loc.wait()
            c = pltpu.make_async_remote_copy(
                outs[i].at[p], outs[i].at[p], send_sem.at[i, 2 * k - 1], recv_sem.at[i, 2 * k - 1],
                device_id=_dev(axis, partner), device_id_type=pl.DeviceIdType.MESH,
            )
            c.start()
            sends.append(c)
            continue
        if mode == "pswap":
            c = pltpu.make_async_remote_copy(
                ins[i], outs[i], send_sem.at[i, 0], recv_sem.at[i, me],
                device_id=_dev(axis, me + 1 - 2 * (me % 2)),
                device_id_type=pl.DeviceIdType.MESH,
            )
            c.start()
            sends.append(c)
            continue
        if mode == "pscatter":
            for d in range(1, k // 2):
                tgt = (me + 2 * d) % k
                c = pltpu.make_async_remote_copy(
                    ins[i].at[tgt // 2], outs[i].at[me // 2], send_sem.at[i, d],
                    recv_sem.at[i, me], device_id=_dev(axis, tgt),
                    device_id_type=pl.DeviceIdType.MESH,
                )
                c.start()
                sends.append(c)
            continue
        if mode == "pgather":
            p = me % 2
            for d in range(1, k // 2):
                tgt = (me + 2 * d) % k
                c = pltpu.make_async_remote_copy(
                    ins[i], outs[i].at[p, me // 2], send_sem.at[i, d], recv_sem.at[i, me],
                    device_id=_dev(axis, tgt), device_id_type=pl.DeviceIdType.MESH,
                )
                c.start()
                sends.append(c)
            loc = pltpu.make_async_copy(ins[i], outs[i].at[p, me // 2], local_sem.at[i])
            loc.start()
            relays.append((i, loc))
            continue
        m = outs[i].shape[1]
        for d in range(1, k):
            tgt = (me + d) % k
            src = ins[i] if mode == "gather" else ins[i].at[pl.ds(tgt * m, m)]
            c = pltpu.make_async_remote_copy(
                src, outs[i].at[me], send_sem.at[i, d], recv_sem.at[i, me],
                device_id=_dev(axis, tgt), device_id_type=pl.DeviceIdType.MESH,
            )
            c.start()
            sends.append(c)
        if mode == "gather":
            loc = pltpu.make_async_copy(ins[i], outs[i].at[me], local_sem.at[i])
            loc.start()
            sends.append(loc)
    for i, loc in relays:
        axis = axes[i]
        k = lax.axis_size(axis)
        me = lax.axis_index(axis)
        p = me % 2
        partner = me + 1 - 2 * p
        for d in range(1, k // 2):
            srcdev = (me + k - 2 * d) % k
            pltpu.make_async_remote_copy(
                ins[i], outs[i].at[p, srcdev // 2], send_sem.at[i, d], recv_sem.at[i, srcdev],
                device_id=_dev(axis, srcdev), device_id_type=pl.DeviceIdType.MESH,
            ).wait_recv()
        loc.wait()
        c = pltpu.make_async_remote_copy(
            outs[i].at[p], outs[i].at[p], send_sem.at[i, 0], recv_sem.at[i, me],
            device_id=_dev(axis, partner), device_id_type=pl.DeviceIdType.MESH,
        )
        c.start()
        sends.append(c)
    for c in sends:
        if c.is_remote:
            c.wait_send()
        else:
            c.wait()
    for i, (mode, axis) in enumerate(zip(modes, axes)):
        k = lax.axis_size(axis)
        me = lax.axis_index(axis)
        if mode == "rscatter":
            ny = k // 2
            ym, zm = me // 2, me % 2
            m = outs[i].shape[1]
            h = m // 2
            direct = [ym * 2 + 1 - zm] + [((ym + dy) % ny) * 2 + z for dy in (1, ny - 1) for z in (0, 1)]
            for srcdev in direct:
                pltpu.make_async_remote_copy(
                    ins[i].at[pl.ds(0, m)], outs[i].at[srcdev], send_sem.at[i, 0],
                    recv_sem.at[i, srcdev], device_id=_dev(axis, srcdev),
                    device_id_type=pl.DeviceIdType.MESH,
                ).wait_recv()
            for z in (0, 1):
                far = ((ym + 2) % ny) * 2 + z
                for lo, off in ((0, k), (h, 2 * k)):
                    dst = outs[i].at[far, pl.ds(lo, h)]
                    pltpu.make_async_remote_copy(
                        dst, dst, send_sem.at[i, 0], recv_sem.at[i, off + far],
                        device_id=_dev(axis, far), device_id_type=pl.DeviceIdType.MESH,
                    ).wait_recv()
            continue
        if mode == "rgather":
            _ring_pair_wait(i, ins[i], lambda g: outs[i].at[g], lambda g: g, me, k,
                            send_sem, recv_sem, axis)
            continue
        if mode == "prgather":
            p = me % 2
            partner = me + 1 - 2 * p
            pltpu.make_async_remote_copy(
                outs[i].at[1 - p], outs[i].at[1 - p], send_sem.at[i, 2 * k - 1],
                recv_sem.at[i, 2 * k - 1],
                device_id=_dev(axis, partner), device_id_type=pl.DeviceIdType.MESH,
            ).wait_recv()
            continue
        if mode == "pswap":
            partner = me + 1 - 2 * (me % 2)
            pltpu.make_async_remote_copy(
                ins[i], outs[i], send_sem.at[i, 0], recv_sem.at[i, partner],
                device_id=_dev(axis, partner), device_id_type=pl.DeviceIdType.MESH,
            ).wait_recv()
            continue
        if mode == "pscatter":
            for d in range(1, k // 2):
                srcdev = (me + k - 2 * d) % k
                pltpu.make_async_remote_copy(
                    ins[i].at[0], outs[i].at[srcdev // 2], send_sem.at[i, d],
                    recv_sem.at[i, srcdev], device_id=_dev(axis, srcdev),
                    device_id_type=pl.DeviceIdType.MESH,
                ).wait_recv()
            continue
        if mode == "pgather":
            p = me % 2
            partner = me + 1 - 2 * p
            pltpu.make_async_remote_copy(
                outs[i].at[1 - p], outs[i].at[1 - p], send_sem.at[i, 0], recv_sem.at[i, partner],
                device_id=_dev(axis, partner), device_id_type=pl.DeviceIdType.MESH,
            ).wait_recv()
            continue
        m = outs[i].shape[1]
        for d in range(1, k):
            srcdev = (me + k - d) % k
            src = ins[i] if mode == "gather" else ins[i].at[pl.ds(0, m)]
            pltpu.make_async_remote_copy(
                src, outs[i].at[srcdev], send_sem.at[i, d], recv_sem.at[i, srcdev],
                device_id=_dev(axis, srcdev), device_id_type=pl.DeviceIdType.MESH,
            ).wait_recv()


def exchange(items, cid):
    modes = tuple(mode for _, _, mode in items)
    axes = tuple(axis for _, axis, _ in items)
    out_shapes = []
    kmax = 1
    for x, axis, mode in items:
        k = lax.axis_size(axis)
        kmax = max(kmax, k)
        if mode in ("gather", "rgather"):
            out_shapes.append(jax.ShapeDtypeStruct((k,) + x.shape, x.dtype))
        elif mode == "rscatter":
            out_shapes.append(
                jax.ShapeDtypeStruct((k + 2, x.shape[0] // k) + x.shape[1:], x.dtype)
            )
        elif mode in ("pswap", "pscatter"):
            out_shapes.append(jax.ShapeDtypeStruct(x.shape, x.dtype))
        elif mode in ("pgather", "prgather"):
            out_shapes.append(jax.ShapeDtypeStruct((2, k // 2) + x.shape, x.dtype))
        else:
            out_shapes.append(
                jax.ShapeDtypeStruct((k, x.shape[0] // k) + x.shape[1:], x.dtype)
            )
    n = len(items)
    return pl.pallas_call(
        functools.partial(_exchange_kernel, modes, axes),
        out_shape=tuple(out_shapes),
        in_specs=[pl.BlockSpec(memory_space=pl.ANY)] * n,
        out_specs=tuple(pl.BlockSpec(memory_space=pl.ANY) for _ in range(n)),
        scratch_shapes=[
            pltpu.SemaphoreType.DMA((n, 4 * kmax)),
            pltpu.SemaphoreType.DMA((n, 4 * kmax)),
            pltpu.SemaphoreType.DMA((n,)),
        ],
        compiler_params=pltpu.CompilerParams(collective_id=cid, has_side_effects=True),
    )(*[x for x, _, _ in items])


def pair_order(v):
    return jnp.swapaxes(v, 0, 1).reshape((-1,) + v.shape[3:])


def reduce_scatter(parts, axis, cid, extra=(), mode="scatter"):
    k = lax.axis_size(axis)
    me = lax.axis_index(axis)
    m = parts.shape[0] // k
    outs = exchange([(parts.astype(WIRE), axis, mode)] + list(extra), cid)
    slots = outs[0][:k]
    mine = lax.dynamic_slice_in_dim(parts, me * m, m, axis=0)
    keep = (jnp.arange(k) != me).reshape((k,) + (1,) * (slots.ndim - 1))
    other = jnp.sum(jnp.where(keep, slots.astype(jnp.float32), 0.0), axis=0)
    return (mine + other,) + tuple(outs[1:])


def pair_reduce_scatter(parts, axis, cid, extra=()):
    k = lax.axis_size(axis)
    me = lax.axis_index(axis)
    p = me % 2
    m = parts.shape[0] // k
    quad = parts.reshape((k // 2, 2, m) + parts.shape[1:])
    mine_half = jnp.where(p == 0, quad[:, 0], quad[:, 1])
    theirs_half = jnp.where(p == 0, quad[:, 1], quad[:, 0])
    (got,) = exchange([(theirs_half, axis, "pswap")], cid)
    pair = mine_half + got
    outs = exchange([(pair.astype(WIRE), axis, "pscatter")] + list(extra), cid + 1)
    slots = outs[0]
    own = lax.dynamic_index_in_dim(pair, me // 2, axis=0, keepdims=False)
    keep = (jnp.arange(k // 2) != me // 2).reshape((k // 2,) + (1,) * (slots.ndim - 1))
    other = jnp.sum(jnp.where(keep, slots.astype(jnp.float32), 0.0), axis=0)
    return (own + other,) + tuple(outs[1:])


def per_device(
    stream_in, grad_out, gate_pre, up_pre, keep_mask, segment_ids, norm_gain, w_gate, w_up, w_down
):
    n_row = lax.axis_size("row")
    n_col = lax.axis_size("col")
    RG = "rgather" if n_row == 8 else "gather"
    PG = "prgather" if n_col == 16 else "pgather"
    tok_col, feat_loc = stream_in.shape
    tok_row, ff_loc = gate_pre.shape
    total = tok_col * n_col
    xs = stream_in.astype(jnp.float32)
    onehot = (segment_ids[:, None] == jnp.arange(SEGS, dtype=jnp.int32)[None, :]).astype(
        jnp.float32
    )
    stats = jnp.concatenate([jnp.sum(xs * xs, axis=1), jnp.sum(onehot, axis=0)])[None, :]
    (stats_all,) = exchange([(stats, "row", "gather")], 0)
    stats_sum = jnp.sum(stats_all, axis=(0, 1))
    squares, counts = stats_sum[:tok_col], stats_sum[tok_col:]
    weights = jnp.sum(onehot * (total / (SEGS * counts))[None, :], axis=1)
    recip = lax.rsqrt(squares / D + eps)
    normed = (xs * recip[:, None] * norm_gain[None, :]).astype(jnp.bfloat16)
    gate_f = gate_pre.astype(jnp.float32)
    up_f = up_pre.astype(jnp.float32)
    sig = jax.nn.sigmoid(gate_f)
    keep_f = keep_mask.astype(jnp.float32) * keep_scale
    dropped = (gate_f * sig * up_f * keep_f * weights[:, None]).astype(jnp.bfloat16)
    cot_full, dropped_full = exchange([(grad_out, "col", PG), (dropped, "row", RG)], 1)
    cot_full = pair_order(cot_full)
    dropped_full = dropped_full.reshape(total, ff_loc)
    back, normed_full = reduce_scatter(
        over_width(cot_full, w_down), "row", 2, [(normed, "col", PG)],
        "rscatter" if n_row == 8 else "scatter",
    )
    normed_full = pair_order(normed_full)
    grad_act = back * weights[:, None] * keep_f
    grad_gpre = (grad_act * up_f * sig * (1.0 + gate_f * (1.0 - sig))).astype(jnp.bfloat16)
    grad_upre = (grad_act * gate_f * sig).astype(jnp.bfloat16)
    half = tok_col // 2
    n_chunk = tok_row // tok_col

    def split(v):
        v = v.reshape(n_chunk, 2, half, ff_loc)
        return v[:, 0].reshape(tok_row // 2, ff_loc), v[:, 1].reshape(tok_row // 2, ff_loc)

    def joined(a, b):
        a = a.reshape(n_row, n_chunk, 1, half, ff_loc)
        b = b.reshape(n_row, n_chunk, 1, half, ff_loc)
        return jnp.concatenate([a, b], axis=2).reshape(total, ff_loc)

    gpre_a, gpre_b = split(grad_gpre)
    upre_a, upre_b = split(grad_upre)
    ga_full, ua_full = exchange([(gpre_a, "row", RG), (upre_a, "row", RG)], 3)
    ga_full = ga_full.reshape(total // 2, ff_loc)
    ua_full = ua_full.reshape(total // 2, ff_loc)
    part_a = over_width(ga_full, w_gate) + over_width(ua_full, w_up)
    gn_a, gb_full, ub_full = pair_reduce_scatter(
        part_a, "col", 4, [(gpre_b, "row", RG), (upre_b, "row", RG)]
    )
    gb_full = gb_full.reshape(total // 2, ff_loc)
    ub_full = ub_full.reshape(total // 2, ff_loc)
    part_b = over_width(gb_full, w_gate) + over_width(ub_full, w_up)
    (gn_b,) = pair_reduce_scatter(part_b, "col", 6)
    grad_normed = jnp.concatenate([gn_a, gn_b], axis=0)
    gpre_full = joined(ga_full, gb_full)
    upre_full = joined(ua_full, ub_full)
    grad_down = over_tokens(dropped_full, cot_full).astype(jnp.bfloat16)
    grad_gate = over_tokens(normed_full, gpre_full).astype(jnp.bfloat16)
    grad_up = over_tokens(normed_full, upre_full).astype(jnp.bfloat16)
    scaled = grad_normed * norm_gain[None, :]
    (inner_all,) = exchange([(jnp.sum(scaled * xs, axis=1)[None, :], "row", "gather")], 8)
    inner = jnp.sum(inner_all, axis=(0, 1)) / D
    branch = recip[:, None] * (scaled - xs * (recip * recip * inner)[:, None])
    grad_in = (grad_out.astype(jnp.float32) + branch).astype(jnp.bfloat16)
    return (grad_in, grad_gate, grad_up, grad_down)


def solution(mesh):
    return jax.shard_map(
        per_device,
        mesh=mesh,
        in_specs=(
            P("col", "row"),
            P("col", "row"),
            P("row", "col"),
            P("row", "col"),
            P("row", "col"),
            P("row"),
            P("row"),
            P("row", "col"),
            P("row", "col"),
            P("col", "row"),
        ),
        out_specs=(P("col", "row"), P("row", "col"), P("row", "col"), P("col", "row")),
        check_vma=False,
    )
```

```python
import functools

import jax
import jax.numpy as jnp
from jax import lax
from jax.experimental import pallas as pl
from jax.experimental.pallas import tpu as pltpu
from jax.sharding import PartitionSpec as P

D = 8192
SEGS = 16
AXES = ("row", "col")
WIRE = jnp.bfloat16

eps = 1e-05
keep_scale = 1.0 / 0.9


def over_tokens(left, right):
    return lax.dot_general(
        left, right, (((0,), (0,)), ((), ())), preferred_element_type=jnp.float32
    )


def over_width(left, right):
    return lax.dot_general(
        left, right, (((1,), (1,)), ((), ())), preferred_element_type=jnp.float32
    )


def _dev(axis, idx):
    return tuple(idx if a == axis else lax.axis_index(a) for a in AXES)


def _barrier(modes, axes):
    barrier = pltpu.get_barrier_semaphore()
    count = 0
    for axis in sorted(set(axes)):
        k = lax.axis_size(axis)
        me = lax.axis_index(axis)
        kinds = {mode for mode, a in zip(modes, axes) if a == axis}
        if kinds <= {"pswap"}:
            peers = [1 - 2 * (me % 2)]
        elif kinds <= {"pswap", "pgather", "pscatter", "prgather"}:
            peers = [2 * d for d in range(1, k // 2)] + [1 - 2 * (me % 2)]
        else:
            peers = list(range(1, k))
        for d in peers:
            pl.semaphore_signal(
                barrier, inc=1, device_id=_dev(axis, (me + d) % k),
                device_id_type=pl.DeviceIdType.MESH,
            )
        count += len(peers)
    pl.semaphore_wait(barrier, count)


def _ring_pair_send(i, src_ref, slot, dev, me_g, ng, send_sem, recv_sem, sends, axis):
    ny = ng // 2
    ym, zm = me_g // 2, me_g % 2
    direct = [ym * 2 + 1 - zm] + [((ym + dy) % ny) * 2 + z for dy in (1, ny - 1) for z in (0, 1)]
    for d, tgt in enumerate(direct):
        c = pltpu.make_async_remote_copy(
            src_ref, slot(me_g), send_sem.at[i, d], recv_sem.at[i, me_g],
            device_id=_dev(axis, dev(tgt)), device_id_type=pl.DeviceIdType.MESH,
        )
        c.start()
        sends.append(c)
    h = src_ref.shape[0] // 2
    for e, (dy, lo, off) in enumerate([(ny - 1, 0, 0), (1, h, ng)]):
        for z in (0, 1):
            src = ((ym + dy) % ny) * 2 + z
            pltpu.make_async_remote_copy(
                src_ref, slot(src), send_sem.at[i, 0], recv_sem.at[i, src],
                device_id=_dev(axis, dev(src)), device_id_type=pl.DeviceIdType.MESH,
            ).wait_recv()
            fwd = ((ym + ny - dy) % ny) * 2 + zm
            c = pltpu.make_async_remote_copy(
                slot(src).at[pl.ds(lo, h)], slot(src).at[pl.ds(lo, h)],
                send_sem.at[i, ng + 2 * e + z], recv_sem.at[i, off + src],
                device_id=_dev(axis, dev(fwd)), device_id_type=pl.DeviceIdType.MESH,
            )
            c.start()
            sends.append(c)


def _ring_pair_wait(i, src_ref, slot, dev, me_g, ng, send_sem, recv_sem, axis):
    ny = ng // 2
    ym, zm = me_g // 2, me_g % 2
    h = src_ref.shape[0] // 2
    peer = ym * 2 + 1 - zm
    pltpu.make_async_remote_copy(
        src_ref, slot(peer), send_sem.at[i, 0], recv_sem.at[i, peer],
        device_id=_dev(axis, dev(peer)), device_id_type=pl.DeviceIdType.MESH,
    ).wait_recv()
    for z in (0, 1):
        far = ((ym + 2) % ny) * 2 + z
        for lo, off in ((0, 0), (h, ng)):
            pltpu.make_async_remote_copy(
                slot(far).at[pl.ds(lo, h)], slot(far).at[pl.ds(lo, h)],
                send_sem.at[i, 0], recv_sem.at[i, off + far],
                device_id=_dev(axis, dev(far)), device_id_type=pl.DeviceIdType.MESH,
            ).wait_recv()


def _exchange_kernel(modes, axes, *refs):
    n = len(modes)
    ins, outs = refs[:n], refs[n:2 * n]
    send_sem, recv_sem, local_sem = refs[2 * n:]
    _barrier(modes, axes)
    sends, relays = [], []
    for i, (mode, axis) in enumerate(zip(modes, axes)):
        k = lax.axis_size(axis)
        me = lax.axis_index(axis)
        if mode == "rgather":
            loc = pltpu.make_async_copy(ins[i], outs[i].at[me], local_sem.at[i])
            loc.start()
            sends.append(loc)
            _ring_pair_send(i, ins[i], lambda g: outs[i].at[g], lambda g: g, me, k,
                            send_sem, recv_sem, sends, axis)
            continue
        if mode == "prgather":
            p = me % 2
            partner = me + 1 - 2 * p
            slot = lambda g: outs[i].at[p, g]
            dev = lambda g: g * 2 + p
            loc = pltpu.make_async_copy(ins[i], slot(me // 2), local_sem.at[i])
            loc.start()
            _ring_pair_send(i, ins[i], slot, dev, me // 2, k // 2, send_sem, recv_sem, sends, axis)
            _ring_pair_wait(i, ins[i], slot, dev, me // 2, k // 2, send_sem, recv_sem, axis)
            loc.wait()
            c = pltpu.make_async_remote_copy(
                outs[i].at[p], outs[i].at[p], send_sem.at[i, 2 * k - 1], recv_sem.at[i, 2 * k - 1],
                device_id=_dev(axis, partner), device_id_type=pl.DeviceIdType.MESH,
            )
            c.start()
            sends.append(c)
            continue
        if mode == "pswap":
            c = pltpu.make_async_remote_copy(
                ins[i], outs[i], send_sem.at[i, 0], recv_sem.at[i, me],
                device_id=_dev(axis, me + 1 - 2 * (me % 2)),
                device_id_type=pl.DeviceIdType.MESH,
            )
            c.start()
            sends.append(c)
            continue
        if mode == "pscatter":
            for d in range(1, k // 2):
                tgt = (me + 2 * d) % k
                c = pltpu.make_async_remote_copy(
                    ins[i].at[tgt // 2], outs[i].at[me // 2], send_sem.at[i, d],
                    recv_sem.at[i, me], device_id=_dev(axis, tgt),
                    device_id_type=pl.DeviceIdType.MESH,
                )
                c.start()
                sends.append(c)
            continue
        if mode == "pgather":
            p = me % 2
            for d in range(1, k // 2):
                tgt = (me + 2 * d) % k
                c = pltpu.make_async_remote_copy(
                    ins[i], outs[i].at[p, me // 2], send_sem.at[i, d], recv_sem.at[i, me],
                    device_id=_dev(axis, tgt), device_id_type=pl.DeviceIdType.MESH,
                )
                c.start()
                sends.append(c)
            loc = pltpu.make_async_copy(ins[i], outs[i].at[p, me // 2], local_sem.at[i])
            loc.start()
            relays.append((i, loc))
            continue
        m = outs[i].shape[1]
        for d in range(1, k):
            tgt = (me + d) % k
            src = ins[i] if mode == "gather" else ins[i].at[pl.ds(tgt * m, m)]
            c = pltpu.make_async_remote_copy(
                src, outs[i].at[me], send_sem.at[i, d], recv_sem.at[i, me],
                device_id=_dev(axis, tgt), device_id_type=pl.DeviceIdType.MESH,
            )
            c.start()
            sends.append(c)
        if mode == "gather":
            loc = pltpu.make_async_copy(ins[i], outs[i].at[me], local_sem.at[i])
            loc.start()
            sends.append(loc)
    for i, loc in relays:
        axis = axes[i]
        k = lax.axis_size(axis)
        me = lax.axis_index(axis)
        p = me % 2
        partner = me + 1 - 2 * p
        for d in range(1, k // 2):
            srcdev = (me + k - 2 * d) % k
            pltpu.make_async_remote_copy(
                ins[i], outs[i].at[p, srcdev // 2], send_sem.at[i, d], recv_sem.at[i, srcdev],
                device_id=_dev(axis, srcdev), device_id_type=pl.DeviceIdType.MESH,
            ).wait_recv()
        loc.wait()
        c = pltpu.make_async_remote_copy(
            outs[i].at[p], outs[i].at[p], send_sem.at[i, 0], recv_sem.at[i, me],
            device_id=_dev(axis, partner), device_id_type=pl.DeviceIdType.MESH,
        )
        c.start()
        sends.append(c)
    for c in sends:
        if c.is_remote:
            c.wait_send()
        else:
            c.wait()
    for i, (mode, axis) in enumerate(zip(modes, axes)):
        k = lax.axis_size(axis)
        me = lax.axis_index(axis)
        if mode == "rgather":
            _ring_pair_wait(i, ins[i], lambda g: outs[i].at[g], lambda g: g, me, k,
                            send_sem, recv_sem, axis)
            continue
        if mode == "prgather":
            p = me % 2
            partner = me + 1 - 2 * p
            pltpu.make_async_remote_copy(
                outs[i].at[1 - p], outs[i].at[1 - p], send_sem.at[i, 2 * k - 1],
                recv_sem.at[i, 2 * k - 1],
                device_id=_dev(axis, partner), device_id_type=pl.DeviceIdType.MESH,
            ).wait_recv()
            continue
        if mode == "pswap":
            partner = me + 1 - 2 * (me % 2)
            pltpu.make_async_remote_copy(
                ins[i], outs[i], send_sem.at[i, 0], recv_sem.at[i, partner],
                device_id=_dev(axis, partner), device_id_type=pl.DeviceIdType.MESH,
            ).wait_recv()
            continue
        if mode == "pscatter":
            for d in range(1, k // 2):
                srcdev = (me + k - 2 * d) % k
                pltpu.make_async_remote_copy(
                    ins[i].at[0], outs[i].at[srcdev // 2], send_sem.at[i, d],
                    recv_sem.at[i, srcdev], device_id=_dev(axis, srcdev),
                    device_id_type=pl.DeviceIdType.MESH,
                ).wait_recv()
            continue
        if mode == "pgather":
            p = me % 2
            partner = me + 1 - 2 * p
            pltpu.make_async_remote_copy(
                outs[i].at[1 - p], outs[i].at[1 - p], send_sem.at[i, 0], recv_sem.at[i, partner],
                device_id=_dev(axis, partner), device_id_type=pl.DeviceIdType.MESH,
            ).wait_recv()
            continue
        m = outs[i].shape[1]
        for d in range(1, k):
            srcdev = (me + k - d) % k
            src = ins[i] if mode == "gather" else ins[i].at[pl.ds(0, m)]
            pltpu.make_async_remote_copy(
                src, outs[i].at[srcdev], send_sem.at[i, d], recv_sem.at[i, srcdev],
                device_id=_dev(axis, srcdev), device_id_type=pl.DeviceIdType.MESH,
            ).wait_recv()


def exchange(items, cid):
    modes = tuple(mode for _, _, mode in items)
    axes = tuple(axis for _, axis, _ in items)
    out_shapes = []
    kmax = 1
    for x, axis, mode in items:
        k = lax.axis_size(axis)
        kmax = max(kmax, k)
        if mode in ("gather", "rgather"):
            out_shapes.append(jax.ShapeDtypeStruct((k,) + x.shape, x.dtype))
        elif mode in ("pswap", "pscatter"):
            out_shapes.append(jax.ShapeDtypeStruct(x.shape, x.dtype))
        elif mode in ("pgather", "prgather"):
            out_shapes.append(jax.ShapeDtypeStruct((2, k // 2) + x.shape, x.dtype))
        else:
            out_shapes.append(
                jax.ShapeDtypeStruct((k, x.shape[0] // k) + x.shape[1:], x.dtype)
            )
    n = len(items)
    return pl.pallas_call(
        functools.partial(_exchange_kernel, modes, axes),
        out_shape=tuple(out_shapes),
        in_specs=[pl.BlockSpec(memory_space=pl.ANY)] * n,
        out_specs=tuple(pl.BlockSpec(memory_space=pl.ANY) for _ in range(n)),
        scratch_shapes=[
            pltpu.SemaphoreType.DMA((n, 2 * kmax)),
            pltpu.SemaphoreType.DMA((n, 2 * kmax)),
            pltpu.SemaphoreType.DMA((n,)),
        ],
        compiler_params=pltpu.CompilerParams(collective_id=cid, has_side_effects=True),
    )(*[x for x, _, _ in items])


def pair_order(v):
    return jnp.swapaxes(v, 0, 1).reshape((-1,) + v.shape[3:])


def reduce_scatter(parts, axis, cid, extra=()):
    k = lax.axis_size(axis)
    me = lax.axis_index(axis)
    m = parts.shape[0] // k
    outs = exchange([(parts.astype(WIRE), axis, "scatter")] + list(extra), cid)
    slots = outs[0]
    mine = lax.dynamic_slice_in_dim(parts, me * m, m, axis=0)
    keep = (jnp.arange(k) != me).reshape((k,) + (1,) * (slots.ndim - 1))
    other = jnp.sum(jnp.where(keep, slots.astype(jnp.float32), 0.0), axis=0)
    return (mine + other,) + tuple(outs[1:])


def pair_reduce_scatter(parts, axis, cid, extra=()):
    k = lax.axis_size(axis)
    me = lax.axis_index(axis)
    p = me % 2
    m = parts.shape[0] // k
    quad = parts.reshape((k // 2, 2, m) + parts.shape[1:])
    mine_half = jnp.where(p == 0, quad[:, 0], quad[:, 1])
    theirs_half = jnp.where(p == 0, quad[:, 1], quad[:, 0])
    (got,) = exchange([(theirs_half, axis, "pswap")], cid)
    pair = mine_half + got
    outs = exchange([(pair.astype(WIRE), axis, "pscatter")] + list(extra), cid + 1)
    slots = outs[0]
    own = lax.dynamic_index_in_dim(pair, me // 2, axis=0, keepdims=False)
    keep = (jnp.arange(k // 2) != me // 2).reshape((k // 2,) + (1,) * (slots.ndim - 1))
    other = jnp.sum(jnp.where(keep, slots.astype(jnp.float32), 0.0), axis=0)
    return (own + other,) + tuple(outs[1:])


def per_device(
    stream_in, grad_out, gate_pre, up_pre, keep_mask, segment_ids, norm_gain, w_gate, w_up, w_down
):
    n_row = lax.axis_size("row")
    n_col = lax.axis_size("col")
    RG = "rgather" if n_row == 8 else "gather"
    PG = "prgather" if n_col == 16 else "pgather"
    tok_col, feat_loc = stream_in.shape
    tok_row, ff_loc = gate_pre.shape
    total = tok_col * n_col
    xs = stream_in.astype(jnp.float32)
    onehot = (segment_ids[:, None] == jnp.arange(SEGS, dtype=jnp.int32)[None, :]).astype(
        jnp.float32
    )
    stats = jnp.concatenate([jnp.sum(xs * xs, axis=1), jnp.sum(onehot, axis=0)])[None, :]
    (stats_all,) = exchange([(stats, "row", "gather")], 0)
    stats_sum = jnp.sum(stats_all, axis=(0, 1))
    squares, counts = stats_sum[:tok_col], stats_sum[tok_col:]
    weights = jnp.sum(onehot * (total / (SEGS * counts))[None, :], axis=1)
    recip = lax.rsqrt(squares / D + eps)
    normed = (xs * recip[:, None] * norm_gain[None, :]).astype(jnp.bfloat16)
    gate_f = gate_pre.astype(jnp.float32)
    up_f = up_pre.astype(jnp.float32)
    sig = jax.nn.sigmoid(gate_f)
    keep_f = keep_mask.astype(jnp.float32) * keep_scale
    dropped = (gate_f * sig * up_f * keep_f * weights[:, None]).astype(jnp.bfloat16)
    (cot_full,) = exchange([(grad_out, "col", PG)], 1)
    cot_full = pair_order(cot_full)
    back, normed_full = reduce_scatter(
        over_width(cot_full, w_down), "row", 2, [(normed, "col", PG)]
    )
    normed_full = pair_order(normed_full)
    grad_act = back * weights[:, None] * keep_f
    grad_gpre = (grad_act * up_f * sig * (1.0 + gate_f * (1.0 - sig))).astype(jnp.bfloat16)
    grad_upre = (grad_act * gate_f * sig).astype(jnp.bfloat16)
    half = tok_col // 2
    n_chunk = tok_row // tok_col

    def split(v):
        v = v.reshape(n_chunk, 2, half, ff_loc)
        return v[:, 0].reshape(tok_row // 2, ff_loc), v[:, 1].reshape(tok_row // 2, ff_loc)

    def joined(a, b):
        a = a.reshape(n_row, n_chunk, 1, half, ff_loc)
        b = b.reshape(n_row, n_chunk, 1, half, ff_loc)
        return jnp.concatenate([a, b], axis=2).reshape(total, ff_loc)

    gpre_a, gpre_b = split(grad_gpre)
    upre_a, upre_b = split(grad_upre)
    ga_full, ua_full = exchange([(gpre_a, "row", RG), (upre_a, "row", RG)], 3)
    ga_full = ga_full.reshape(total // 2, ff_loc)
    ua_full = ua_full.reshape(total // 2, ff_loc)
    part_a = over_width(ga_full, w_gate) + over_width(ua_full, w_up)
    gn_a, gb_full, ub_full = pair_reduce_scatter(
        part_a, "col", 4, [(gpre_b, "row", RG), (upre_b, "row", RG)]
    )
    gb_full = gb_full.reshape(total // 2, ff_loc)
    ub_full = ub_full.reshape(total // 2, ff_loc)
    part_b = over_width(gb_full, w_gate) + over_width(ub_full, w_up)
    gn_b, dropped_full = pair_reduce_scatter(part_b, "col", 6, [(dropped, "row", RG)])
    dropped_full = dropped_full.reshape(total, ff_loc)
    grad_normed = jnp.concatenate([gn_a, gn_b], axis=0)
    gpre_full = joined(ga_full, gb_full)
    upre_full = joined(ua_full, ub_full)
    grad_down = over_tokens(dropped_full, cot_full).astype(jnp.bfloat16)
    grad_gate = over_tokens(normed_full, gpre_full).astype(jnp.bfloat16)
    grad_up = over_tokens(normed_full, upre_full).astype(jnp.bfloat16)
    scaled = grad_normed * norm_gain[None, :]
    (inner_all,) = exchange([(jnp.sum(scaled * xs, axis=1)[None, :], "row", "gather")], 8)
    inner = jnp.sum(inner_all, axis=(0, 1)) / D
    branch = recip[:, None] * (scaled - xs * (recip * recip * inner)[:, None])
    grad_in = (grad_out.astype(jnp.float32) + branch).astype(jnp.bfloat16)
    return (grad_in, grad_gate, grad_up, grad_down)


def solution(mesh):
    return jax.shard_map(
        per_device,
        mesh=mesh,
        in_specs=(
            P("col", "row"),
            P("col", "row"),
            P("row", "col"),
            P("row", "col"),
            P("row", "col"),
            P("row"),
            P("row"),
            P("row", "col"),
            P("row", "col"),
            P("col", "row"),
        ),
        out_specs=(P("col", "row"), P("row", "col"), P("row", "col"), P("col", "row")),
        check_vma=False,
    )
```

```python
import functools

import jax
import jax.numpy as jnp
from jax import lax
from jax.experimental import pallas as pl
from jax.experimental.pallas import tpu as pltpu
from jax.sharding import PartitionSpec as P

D = 8192
SEGS = 16
AXES = ("row", "col")
WIRE = jnp.bfloat16

eps = 1e-05
keep_scale = 1.0 / 0.9


def over_tokens(left, right):
    return lax.dot_general(
        left, right, (((0,), (0,)), ((), ())), preferred_element_type=jnp.float32
    )


def over_width(left, right):
    return lax.dot_general(
        left, right, (((1,), (1,)), ((), ())), preferred_element_type=jnp.float32
    )


def _dev(axis, idx):
    return tuple(idx if a == axis else lax.axis_index(a) for a in AXES)


def _barrier(modes, axes):
    barrier = pltpu.get_barrier_semaphore()
    count = 0
    for axis in sorted(set(axes)):
        k = lax.axis_size(axis)
        me = lax.axis_index(axis)
        kinds = {mode for mode, a in zip(modes, axes) if a == axis}
        if kinds <= {"pswap"}:
            peers = [1 - 2 * (me % 2)]
        elif kinds <= {"pswap", "pgather", "pscatter", "prgather"}:
            peers = [2 * d for d in range(1, k // 2)] + [1 - 2 * (me % 2)]
        else:
            peers = list(range(1, k))
        for d in peers:
            pl.semaphore_signal(
                barrier, inc=1, device_id=_dev(axis, (me + d) % k),
                device_id_type=pl.DeviceIdType.MESH,
            )
        count += len(peers)
    pl.semaphore_wait(barrier, count)


def _ring_pair_send(i, src_ref, slot, dev, me_g, ng, send_sem, recv_sem, sends, axis):
    ny = ng // 2
    ym, zm = me_g // 2, me_g % 2
    direct = [ym * 2 + 1 - zm] + [((ym + dy) % ny) * 2 + z for dy in (1, ny - 1) for z in (0, 1)]
    for d, tgt in enumerate(direct):
        c = pltpu.make_async_remote_copy(
            src_ref, slot(me_g), send_sem.at[i, d], recv_sem.at[i, me_g],
            device_id=_dev(axis, dev(tgt)), device_id_type=pl.DeviceIdType.MESH,
        )
        c.start()
        sends.append(c)
    h = src_ref.shape[0] // 2
    for e, (dy, lo, off) in enumerate([(ny - 1, 0, 0), (1, h, ng)]):
        for z in (0, 1):
            src = ((ym + dy) % ny) * 2 + z
            pltpu.make_async_remote_copy(
                src_ref, slot(src), send_sem.at[i, 0], recv_sem.at[i, src],
                device_id=_dev(axis, dev(src)), device_id_type=pl.DeviceIdType.MESH,
            ).wait_recv()
            fwd = ((ym + ny - dy) % ny) * 2 + zm
            c = pltpu.make_async_remote_copy(
                slot(src).at[pl.ds(lo, h)], slot(src).at[pl.ds(lo, h)],
                send_sem.at[i, ng + 2 * e + z], recv_sem.at[i, off + src],
                device_id=_dev(axis, dev(fwd)), device_id_type=pl.DeviceIdType.MESH,
            )
            c.start()
            sends.append(c)


def _ring_pair_wait(i, src_ref, slot, dev, me_g, ng, send_sem, recv_sem, axis):
    ny = ng // 2
    ym, zm = me_g // 2, me_g % 2
    h = src_ref.shape[0] // 2
    peer = ym * 2 + 1 - zm
    pltpu.make_async_remote_copy(
        src_ref, slot(peer), send_sem.at[i, 0], recv_sem.at[i, peer],
        device_id=_dev(axis, dev(peer)), device_id_type=pl.DeviceIdType.MESH,
    ).wait_recv()
    for z in (0, 1):
        far = ((ym + 2) % ny) * 2 + z
        for lo, off in ((0, 0), (h, ng)):
            pltpu.make_async_remote_copy(
                slot(far).at[pl.ds(lo, h)], slot(far).at[pl.ds(lo, h)],
                send_sem.at[i, 0], recv_sem.at[i, off + far],
                device_id=_dev(axis, dev(far)), device_id_type=pl.DeviceIdType.MESH,
            ).wait_recv()


def _exchange_kernel(modes, axes, *refs):
    n = len(modes)
    ins, outs = refs[:n], refs[n:2 * n]
    send_sem, recv_sem, local_sem = refs[2 * n:]
    _barrier(modes, axes)
    sends, relays = [], []
    for i, (mode, axis) in enumerate(zip(modes, axes)):
        k = lax.axis_size(axis)
        me = lax.axis_index(axis)
        if mode == "rgather":
            loc = pltpu.make_async_copy(ins[i], outs[i].at[me], local_sem.at[i])
            loc.start()
            sends.append(loc)
            _ring_pair_send(i, ins[i], lambda g: outs[i].at[g], lambda g: g, me, k,
                            send_sem, recv_sem, sends, axis)
            continue
        if mode == "prgather":
            p = me % 2
            partner = me + 1 - 2 * p
            slot = lambda g: outs[i].at[p, g]
            dev = lambda g: g * 2 + p
            loc = pltpu.make_async_copy(ins[i], slot(me // 2), local_sem.at[i])
            loc.start()
            _ring_pair_send(i, ins[i], slot, dev, me // 2, k // 2, send_sem, recv_sem, sends, axis)
            _ring_pair_wait(i, ins[i], slot, dev, me // 2, k // 2, send_sem, recv_sem, axis)
            loc.wait()
            c = pltpu.make_async_remote_copy(
                outs[i].at[p], outs[i].at[p], send_sem.at[i, 2 * k - 1], recv_sem.at[i, 2 * k - 1],
                device_id=_dev(axis, partner), device_id_type=pl.DeviceIdType.MESH,
            )
            c.start()
            sends.append(c)
            continue
        if mode == "pswap":
            c = pltpu.make_async_remote_copy(
                ins[i], outs[i], send_sem.at[i, 0], recv_sem.at[i, me],
                device_id=_dev(axis, me + 1 - 2 * (me % 2)),
                device_id_type=pl.DeviceIdType.MESH,
            )
            c.start()
            sends.append(c)
            continue
        if mode == "pscatter":
            for d in range(1, k // 2):
                tgt = (me + 2 * d) % k
                c = pltpu.make_async_remote_copy(
                    ins[i].at[tgt // 2], outs[i].at[me // 2], send_sem.at[i, d],
                    recv_sem.at[i, me], device_id=_dev(axis, tgt),
                    device_id_type=pl.DeviceIdType.MESH,
                )
                c.start()
                sends.append(c)
            continue
        if mode == "pgather":
            p = me % 2
            for d in range(1, k // 2):
                tgt = (me + 2 * d) % k
                c = pltpu.make_async_remote_copy(
                    ins[i], outs[i].at[p, me // 2], send_sem.at[i, d], recv_sem.at[i, me],
                    device_id=_dev(axis, tgt), device_id_type=pl.DeviceIdType.MESH,
                )
                c.start()
                sends.append(c)
            loc = pltpu.make_async_copy(ins[i], outs[i].at[p, me // 2], local_sem.at[i])
            loc.start()
            relays.append((i, loc))
            continue
        m = outs[i].shape[1]
        for d in range(1, k):
            tgt = (me + d) % k
            src = ins[i] if mode == "gather" else ins[i].at[pl.ds(tgt * m, m)]
            c = pltpu.make_async_remote_copy(
                src, outs[i].at[me], send_sem.at[i, d], recv_sem.at[i, me],
                device_id=_dev(axis, tgt), device_id_type=pl.DeviceIdType.MESH,
            )
            c.start()
            sends.append(c)
        if mode == "gather":
            loc = pltpu.make_async_copy(ins[i], outs[i].at[me], local_sem.at[i])
            loc.start()
            sends.append(loc)
    for i, loc in relays:
        axis = axes[i]
        k = lax.axis_size(axis)
        me = lax.axis_index(axis)
        p = me % 2
        partner = me + 1 - 2 * p
        for d in range(1, k // 2):
            srcdev = (me + k - 2 * d) % k
            pltpu.make_async_remote_copy(
                ins[i], outs[i].at[p, srcdev // 2], send_sem.at[i, d], recv_sem.at[i, srcdev],
                device_id=_dev(axis, srcdev), device_id_type=pl.DeviceIdType.MESH,
            ).wait_recv()
        loc.wait()
        c = pltpu.make_async_remote_copy(
            outs[i].at[p], outs[i].at[p], send_sem.at[i, 0], recv_sem.at[i, me],
            device_id=_dev(axis, partner), device_id_type=pl.DeviceIdType.MESH,
        )
        c.start()
        sends.append(c)
    for c in sends:
        if c.is_remote:
            c.wait_send()
        else:
            c.wait()
    for i, (mode, axis) in enumerate(zip(modes, axes)):
        k = lax.axis_size(axis)
        me = lax.axis_index(axis)
        if mode == "rgather":
            _ring_pair_wait(i, ins[i], lambda g: outs[i].at[g], lambda g: g, me, k,
                            send_sem, recv_sem, axis)
            continue
        if mode == "prgather":
            p = me % 2
            partner = me + 1 - 2 * p
            pltpu.make_async_remote_copy(
                outs[i].at[1 - p], outs[i].at[1 - p], send_sem.at[i, 2 * k - 1],
                recv_sem.at[i, 2 * k - 1],
                device_id=_dev(axis, partner), device_id_type=pl.DeviceIdType.MESH,
            ).wait_recv()
            continue
        if mode == "pswap":
            partner = me + 1 - 2 * (me % 2)
            pltpu.make_async_remote_copy(
                ins[i], outs[i], send_sem.at[i, 0], recv_sem.at[i, partner],
                device_id=_dev(axis, partner), device_id_type=pl.DeviceIdType.MESH,
            ).wait_recv()
            continue
        if mode == "pscatter":
            for d in range(1, k // 2):
                srcdev = (me + k - 2 * d) % k
                pltpu.make_async_remote_copy(
                    ins[i].at[0], outs[i].at[srcdev // 2], send_sem.at[i, d],
                    recv_sem.at[i, srcdev], device_id=_dev(axis, srcdev),
                    device_id_type=pl.DeviceIdType.MESH,
                ).wait_recv()
            continue
        if mode == "pgather":
            p = me % 2
            partner = me + 1 - 2 * p
            pltpu.make_async_remote_copy(
                outs[i].at[1 - p], outs[i].at[1 - p], send_sem.at[i, 0], recv_sem.at[i, partner],
                device_id=_dev(axis, partner), device_id_type=pl.DeviceIdType.MESH,
            ).wait_recv()
            continue
        m = outs[i].shape[1]
        for d in range(1, k):
            srcdev = (me + k - d) % k
            src = ins[i] if mode == "gather" else ins[i].at[pl.ds(0, m)]
            pltpu.make_async_remote_copy(
                src, outs[i].at[srcdev], send_sem.at[i, d], recv_sem.at[i, srcdev],
                device_id=_dev(axis, srcdev), device_id_type=pl.DeviceIdType.MESH,
            ).wait_recv()


def exchange(items, cid):
    modes = tuple(mode for _, _, mode in items)
    axes = tuple(axis for _, axis, _ in items)
    out_shapes = []
    kmax = 1
    for x, axis, mode in items:
        k = lax.axis_size(axis)
        kmax = max(kmax, k)
        if mode in ("gather", "rgather"):
            out_shapes.append(jax.ShapeDtypeStruct((k,) + x.shape, x.dtype))
        elif mode in ("pswap", "pscatter"):
            out_shapes.append(jax.ShapeDtypeStruct(x.shape, x.dtype))
        elif mode in ("pgather", "prgather"):
            out_shapes.append(jax.ShapeDtypeStruct((2, k // 2) + x.shape, x.dtype))
        else:
            out_shapes.append(
                jax.ShapeDtypeStruct((k, x.shape[0] // k) + x.shape[1:], x.dtype)
            )
    n = len(items)
    return pl.pallas_call(
        functools.partial(_exchange_kernel, modes, axes),
        out_shape=tuple(out_shapes),
        in_specs=[pl.BlockSpec(memory_space=pl.ANY)] * n,
        out_specs=tuple(pl.BlockSpec(memory_space=pl.ANY) for _ in range(n)),
        scratch_shapes=[
            pltpu.SemaphoreType.DMA((n, 2 * kmax)),
            pltpu.SemaphoreType.DMA((n, 2 * kmax)),
            pltpu.SemaphoreType.DMA((n,)),
        ],
        compiler_params=pltpu.CompilerParams(collective_id=cid, has_side_effects=True),
    )(*[x for x, _, _ in items])


def pair_order(v):
    return jnp.swapaxes(v, 0, 1).reshape((-1,) + v.shape[3:])


def reduce_scatter(parts, axis, cid, extra=()):
    k = lax.axis_size(axis)
    me = lax.axis_index(axis)
    m = parts.shape[0] // k
    outs = exchange([(parts.astype(WIRE), axis, "scatter")] + list(extra), cid)
    slots = outs[0]
    mine = lax.dynamic_slice_in_dim(parts, me * m, m, axis=0)
    keep = (jnp.arange(k) != me).reshape((k,) + (1,) * (slots.ndim - 1))
    other = jnp.sum(jnp.where(keep, slots.astype(jnp.float32), 0.0), axis=0)
    return (mine + other,) + tuple(outs[1:])


def pair_reduce_scatter(parts, axis, cid, extra=()):
    k = lax.axis_size(axis)
    me = lax.axis_index(axis)
    p = me % 2
    m = parts.shape[0] // k
    quad = parts.reshape((k // 2, 2, m) + parts.shape[1:])
    mine_half = jnp.where(p == 0, quad[:, 0], quad[:, 1])
    theirs_half = jnp.where(p == 0, quad[:, 1], quad[:, 0])
    (got,) = exchange([(theirs_half, axis, "pswap")], cid)
    pair = mine_half + got
    outs = exchange([(pair.astype(WIRE), axis, "pscatter")] + list(extra), cid + 1)
    slots = outs[0]
    own = lax.dynamic_index_in_dim(pair, me // 2, axis=0, keepdims=False)
    keep = (jnp.arange(k // 2) != me // 2).reshape((k // 2,) + (1,) * (slots.ndim - 1))
    other = jnp.sum(jnp.where(keep, slots.astype(jnp.float32), 0.0), axis=0)
    return (own + other,) + tuple(outs[1:])


def per_device(
    stream_in, grad_out, gate_pre, up_pre, keep_mask, segment_ids, norm_gain, w_gate, w_up, w_down
):
    n_row = lax.axis_size("row")
    n_col = lax.axis_size("col")
    RG = "rgather" if n_row == 8 else "gather"
    PG = "prgather" if n_col == 16 else "pgather"
    tok_col, feat_loc = stream_in.shape
    tok_row, ff_loc = gate_pre.shape
    total = tok_col * n_col
    xs = stream_in.astype(jnp.float32)
    onehot = (segment_ids[:, None] == jnp.arange(SEGS, dtype=jnp.int32)[None, :]).astype(
        jnp.float32
    )
    stats = jnp.concatenate([jnp.sum(xs * xs, axis=1), jnp.sum(onehot, axis=0)])[None, :]
    stats_all, cot_full = exchange([(stats, "row", "gather"), (grad_out, "col", PG)], 1)
    stats_sum = jnp.sum(stats_all, axis=(0, 1))
    squares, counts = stats_sum[:tok_col], stats_sum[tok_col:]
    weights = jnp.sum(onehot * (total / (SEGS * counts))[None, :], axis=1)
    recip = lax.rsqrt(squares / D + eps)
    normed = (xs * recip[:, None] * norm_gain[None, :]).astype(jnp.bfloat16)
    gate_f = gate_pre.astype(jnp.float32)
    up_f = up_pre.astype(jnp.float32)
    sig = jax.nn.sigmoid(gate_f)
    keep_f = keep_mask.astype(jnp.float32) * keep_scale
    dropped = (gate_f * sig * up_f * keep_f * weights[:, None]).astype(jnp.bfloat16)
    cot_full = pair_order(cot_full)
    back, normed_full, dropped_full = reduce_scatter(
        over_width(cot_full, w_down), "row", 2, [(normed, "col", PG), (dropped, "row", RG)]
    )
    dropped_full = dropped_full.reshape(total, ff_loc)
    normed_full = pair_order(normed_full)
    grad_act = back * weights[:, None] * keep_f
    grad_gpre = (grad_act * up_f * sig * (1.0 + gate_f * (1.0 - sig))).astype(jnp.bfloat16)
    grad_upre = (grad_act * gate_f * sig).astype(jnp.bfloat16)
    half = tok_col // 2
    n_chunk = tok_row // tok_col

    def split(v):
        v = v.reshape(n_chunk, 2, half, ff_loc)
        return v[:, 0].reshape(tok_row // 2, ff_loc), v[:, 1].reshape(tok_row // 2, ff_loc)

    def joined(a, b):
        a = a.reshape(n_row, n_chunk, 1, half, ff_loc)
        b = b.reshape(n_row, n_chunk, 1, half, ff_loc)
        return jnp.concatenate([a, b], axis=2).reshape(total, ff_loc)

    gpre_a, gpre_b = split(grad_gpre)
    upre_a, upre_b = split(grad_upre)
    ga_full, ua_full = exchange([(gpre_a, "row", RG), (upre_a, "row", RG)], 3)
    ga_full = ga_full.reshape(total // 2, ff_loc)
    ua_full = ua_full.reshape(total // 2, ff_loc)
    part_a = over_width(ga_full, w_gate) + over_width(ua_full, w_up)
    gn_a, gb_full, ub_full = pair_reduce_scatter(
        part_a, "col", 4, [(gpre_b, "row", RG), (upre_b, "row", RG)]
    )
    gb_full = gb_full.reshape(total // 2, ff_loc)
    ub_full = ub_full.reshape(total // 2, ff_loc)
    part_b = over_width(gb_full, w_gate) + over_width(ub_full, w_up)
    (gn_b,) = pair_reduce_scatter(part_b, "col", 6)
    grad_normed = jnp.concatenate([gn_a, gn_b], axis=0)
    gpre_full = joined(ga_full, gb_full)
    upre_full = joined(ua_full, ub_full)
    grad_down = over_tokens(dropped_full, cot_full).astype(jnp.bfloat16)
    grad_gate = over_tokens(normed_full, gpre_full).astype(jnp.bfloat16)
    grad_up = over_tokens(normed_full, upre_full).astype(jnp.bfloat16)
    scaled = grad_normed * norm_gain[None, :]
    (inner_all,) = exchange([(jnp.sum(scaled * xs, axis=1)[None, :], "row", "gather")], 8)
    inner = jnp.sum(inner_all, axis=(0, 1)) / D
    branch = recip[:, None] * (scaled - xs * (recip * recip * inner)[:, None])
    grad_in = (grad_out.astype(jnp.float32) + branch).astype(jnp.bfloat16)
    return (grad_in, grad_gate, grad_up, grad_down)


def solution(mesh):
    return jax.shard_map(
        per_device,
        mesh=mesh,
        in_specs=(
            P("col", "row"),
            P("col", "row"),
            P("row", "col"),
            P("row", "col"),
            P("row", "col"),
            P("row"),
            P("row"),
            P("row", "col"),
            P("row", "col"),
            P("col", "row"),
        ),
        out_specs=(P("col", "row"), P("row", "col"), P("row", "col"), P("col", "row")),
        check_vma=False,
    )
```

```python
import functools

import jax
import jax.numpy as jnp
from jax import lax
from jax.experimental import pallas as pl
from jax.experimental.pallas import tpu as pltpu
from jax.sharding import PartitionSpec as P

D = 8192
SEGS = 16
AXES = ("row", "col")
WIRE = jnp.bfloat16

eps = 1e-05
keep_scale = 1.0 / 0.9


def over_tokens(left, right):
    return lax.dot_general(
        left, right, (((0,), (0,)), ((), ())), preferred_element_type=jnp.float32
    )


def over_width(left, right):
    return lax.dot_general(
        left, right, (((1,), (1,)), ((), ())), preferred_element_type=jnp.float32
    )


def _dev(axis, idx):
    return tuple(idx if a == axis else lax.axis_index(a) for a in AXES)


def _barrier(modes, axes):
    barrier = pltpu.get_barrier_semaphore()
    count = 0
    for axis in sorted(set(axes)):
        k = lax.axis_size(axis)
        me = lax.axis_index(axis)
        kinds = {mode for mode, a in zip(modes, axes) if a == axis}
        if kinds <= {"pswap"}:
            peers = [1 - 2 * (me % 2)]
        elif kinds <= {"pswap", "pgather", "pscatter", "prgather"}:
            peers = [2 * d for d in range(1, k // 2)] + [1 - 2 * (me % 2)]
        else:
            peers = list(range(1, k))
        for d in peers:
            pl.semaphore_signal(
                barrier, inc=1, device_id=_dev(axis, (me + d) % k),
                device_id_type=pl.DeviceIdType.MESH,
            )
        count += len(peers)
    pl.semaphore_wait(barrier, count)


def _ring_pair_send(i, src_ref, slot, dev, me_g, ng, send_sem, recv_sem, sends, axis):
    ny = ng // 2
    ym, zm = me_g // 2, me_g % 2
    direct = [ym * 2 + 1 - zm] + [((ym + dy) % ny) * 2 + z for dy in (1, ny - 1) for z in (0, 1)]
    for d, tgt in enumerate(direct):
        c = pltpu.make_async_remote_copy(
            src_ref, slot(me_g), send_sem.at[i, d], recv_sem.at[i, me_g],
            device_id=_dev(axis, dev(tgt)), device_id_type=pl.DeviceIdType.MESH,
        )
        c.start()
        sends.append(c)
    h = src_ref.shape[0] // 2
    for e, (dy, lo, off) in enumerate([(ny - 1, 0, 0), (1, h, ng)]):
        for z in (0, 1):
            src = ((ym + dy) % ny) * 2 + z
            pltpu.make_async_remote_copy(
                src_ref, slot(src), send_sem.at[i, 0], recv_sem.at[i, src],
                device_id=_dev(axis, dev(src)), device_id_type=pl.DeviceIdType.MESH,
            ).wait_recv()
            fwd = ((ym + ny - dy) % ny) * 2 + zm
            c = pltpu.make_async_remote_copy(
                slot(src).at[pl.ds(lo, h)], slot(src).at[pl.ds(lo, h)],
                send_sem.at[i, ng + 2 * e + z], recv_sem.at[i, off + src],
                device_id=_dev(axis, dev(fwd)), device_id_type=pl.DeviceIdType.MESH,
            )
            c.start()
            sends.append(c)


def _ring_pair_wait(i, src_ref, slot, dev, me_g, ng, send_sem, recv_sem, axis):
    ny = ng // 2
    ym, zm = me_g // 2, me_g % 2
    h = src_ref.shape[0] // 2
    peer = ym * 2 + 1 - zm
    pltpu.make_async_remote_copy(
        src_ref, slot(peer), send_sem.at[i, 0], recv_sem.at[i, peer],
        device_id=_dev(axis, dev(peer)), device_id_type=pl.DeviceIdType.MESH,
    ).wait_recv()
    for z in (0, 1):
        far = ((ym + 2) % ny) * 2 + z
        for lo, off in ((0, 0), (h, ng)):
            pltpu.make_async_remote_copy(
                slot(far).at[pl.ds(lo, h)], slot(far).at[pl.ds(lo, h)],
                send_sem.at[i, 0], recv_sem.at[i, off + far],
                device_id=_dev(axis, dev(far)), device_id_type=pl.DeviceIdType.MESH,
            ).wait_recv()


def _exchange_kernel(modes, axes, *refs):
    n = len(modes)
    ins, outs = refs[:n], refs[n:2 * n]
    send_sem, recv_sem, local_sem = refs[2 * n:]
    _barrier(modes, axes)
    sends, relays = [], []
    for i, (mode, axis) in enumerate(zip(modes, axes)):
        k = lax.axis_size(axis)
        me = lax.axis_index(axis)
        if mode == "rgather":
            loc = pltpu.make_async_copy(ins[i], outs[i].at[me], local_sem.at[i])
            loc.start()
            sends.append(loc)
            _ring_pair_send(i, ins[i], lambda g: outs[i].at[g], lambda g: g, me, k,
                            send_sem, recv_sem, sends, axis)
            continue
        if mode == "prgather":
            p = me % 2
            partner = me + 1 - 2 * p
            slot = lambda g: outs[i].at[p, g]
            dev = lambda g: g * 2 + p
            loc = pltpu.make_async_copy(ins[i], slot(me // 2), local_sem.at[i])
            loc.start()
            _ring_pair_send(i, ins[i], slot, dev, me // 2, k // 2, send_sem, recv_sem, sends, axis)
            _ring_pair_wait(i, ins[i], slot, dev, me // 2, k // 2, send_sem, recv_sem, axis)
            loc.wait()
            c = pltpu.make_async_remote_copy(
                outs[i].at[p], outs[i].at[p], send_sem.at[i, 2 * k - 1], recv_sem.at[i, 2 * k - 1],
                device_id=_dev(axis, partner), device_id_type=pl.DeviceIdType.MESH,
            )
            c.start()
            sends.append(c)
            continue
        if mode == "pswap":
            c = pltpu.make_async_remote_copy(
                ins[i], outs[i], send_sem.at[i, 0], recv_sem.at[i, me],
                device_id=_dev(axis, me + 1 - 2 * (me % 2)),
                device_id_type=pl.DeviceIdType.MESH,
            )
            c.start()
            sends.append(c)
            continue
        if mode == "pscatter":
            for d in range(1, k // 2):
                tgt = (me + 2 * d) % k
                c = pltpu.make_async_remote_copy(
                    ins[i].at[tgt // 2], outs[i].at[me // 2], send_sem.at[i, d],
                    recv_sem.at[i, me], device_id=_dev(axis, tgt),
                    device_id_type=pl.DeviceIdType.MESH,
                )
                c.start()
                sends.append(c)
            continue
        if mode == "pgather":
            p = me % 2
            for d in range(1, k // 2):
                tgt = (me + 2 * d) % k
                c = pltpu.make_async_remote_copy(
                    ins[i], outs[i].at[p, me // 2], send_sem.at[i, d], recv_sem.at[i, me],
                    device_id=_dev(axis, tgt), device_id_type=pl.DeviceIdType.MESH,
                )
                c.start()
                sends.append(c)
            loc = pltpu.make_async_copy(ins[i], outs[i].at[p, me // 2], local_sem.at[i])
            loc.start()
            relays.append((i, loc))
            continue
        m = outs[i].shape[1]
        for d in range(1, k):
            tgt = (me + d) % k
            src = ins[i] if mode == "gather" else ins[i].at[pl.ds(tgt * m, m)]
            c = pltpu.make_async_remote_copy(
                src, outs[i].at[me], send_sem.at[i, d], recv_sem.at[i, me],
                device_id=_dev(axis, tgt), device_id_type=pl.DeviceIdType.MESH,
            )
            c.start()
            sends.append(c)
        if mode == "gather":
            loc = pltpu.make_async_copy(ins[i], outs[i].at[me], local_sem.at[i])
            loc.start()
            sends.append(loc)
    for i, loc in relays:
        axis = axes[i]
        k = lax.axis_size(axis)
        me = lax.axis_index(axis)
        p = me % 2
        partner = me + 1 - 2 * p
        for d in range(1, k // 2):
            srcdev = (me + k - 2 * d) % k
            pltpu.make_async_remote_copy(
                ins[i], outs[i].at[p, srcdev // 2], send_sem.at[i, d], recv_sem.at[i, srcdev],
                device_id=_dev(axis, srcdev), device_id_type=pl.DeviceIdType.MESH,
            ).wait_recv()
        loc.wait()
        c = pltpu.make_async_remote_copy(
            outs[i].at[p], outs[i].at[p], send_sem.at[i, 0], recv_sem.at[i, me],
            device_id=_dev(axis, partner), device_id_type=pl.DeviceIdType.MESH,
        )
        c.start()
        sends.append(c)
    for c in sends:
        if c.is_remote:
            c.wait_send()
        else:
            c.wait()
    for i, (mode, axis) in enumerate(zip(modes, axes)):
        k = lax.axis_size(axis)
        me = lax.axis_index(axis)
        if mode == "rgather":
            _ring_pair_wait(i, ins[i], lambda g: outs[i].at[g], lambda g: g, me, k,
                            send_sem, recv_sem, axis)
            continue
        if mode == "prgather":
            p = me % 2
            partner = me + 1 - 2 * p
            pltpu.make_async_remote_copy(
                outs[i].at[1 - p], outs[i].at[1 - p], send_sem.at[i, 2 * k - 1],
                recv_sem.at[i, 2 * k - 1],
                device_id=_dev(axis, partner), device_id_type=pl.DeviceIdType.MESH,
            ).wait_recv()
            continue
        if mode == "pswap":
            partner = me + 1 - 2 * (me % 2)
            pltpu.make_async_remote_copy(
                ins[i], outs[i], send_sem.at[i, 0], recv_sem.at[i, partner],
                device_id=_dev(axis, partner), device_id_type=pl.DeviceIdType.MESH,
            ).wait_recv()
            continue
        if mode == "pscatter":
            for d in range(1, k // 2):
                srcdev = (me + k - 2 * d) % k
                pltpu.make_async_remote_copy(
                    ins[i].at[0], outs[i].at[srcdev // 2], send_sem.at[i, d],
                    recv_sem.at[i, srcdev], device_id=_dev(axis, srcdev),
                    device_id_type=pl.DeviceIdType.MESH,
                ).wait_recv()
            continue
        if mode == "pgather":
            p = me % 2
            partner = me + 1 - 2 * p
            pltpu.make_async_remote_copy(
                outs[i].at[1 - p], outs[i].at[1 - p], send_sem.at[i, 0], recv_sem.at[i, partner],
                device_id=_dev(axis, partner), device_id_type=pl.DeviceIdType.MESH,
            ).wait_recv()
            continue
        m = outs[i].shape[1]
        for d in range(1, k):
            srcdev = (me + k - d) % k
            src = ins[i] if mode == "gather" else ins[i].at[pl.ds(0, m)]
            pltpu.make_async_remote_copy(
                src, outs[i].at[srcdev], send_sem.at[i, d], recv_sem.at[i, srcdev],
                device_id=_dev(axis, srcdev), device_id_type=pl.DeviceIdType.MESH,
            ).wait_recv()


def exchange(items, cid):
    modes = tuple(mode for _, _, mode in items)
    axes = tuple(axis for _, axis, _ in items)
    out_shapes = []
    kmax = 1
    for x, axis, mode in items:
        k = lax.axis_size(axis)
        kmax = max(kmax, k)
        if mode in ("gather", "rgather"):
            out_shapes.append(jax.ShapeDtypeStruct((k,) + x.shape, x.dtype))
        elif mode in ("pswap", "pscatter"):
            out_shapes.append(jax.ShapeDtypeStruct(x.shape, x.dtype))
        elif mode in ("pgather", "prgather"):
            out_shapes.append(jax.ShapeDtypeStruct((2, k // 2) + x.shape, x.dtype))
        else:
            out_shapes.append(
                jax.ShapeDtypeStruct((k, x.shape[0] // k) + x.shape[1:], x.dtype)
            )
    n = len(items)
    return pl.pallas_call(
        functools.partial(_exchange_kernel, modes, axes),
        out_shape=tuple(out_shapes),
        in_specs=[pl.BlockSpec(memory_space=pl.ANY)] * n,
        out_specs=tuple(pl.BlockSpec(memory_space=pl.ANY) for _ in range(n)),
        scratch_shapes=[
            pltpu.SemaphoreType.DMA((n, 2 * kmax)),
            pltpu.SemaphoreType.DMA((n, 2 * kmax)),
            pltpu.SemaphoreType.DMA((n,)),
        ],
        compiler_params=pltpu.CompilerParams(collective_id=cid, has_side_effects=True),
    )(*[x for x, _, _ in items])


def pair_order(v):
    return jnp.swapaxes(v, 0, 1).reshape((-1,) + v.shape[3:])


def reduce_scatter(parts, axis, cid, extra=()):
    k = lax.axis_size(axis)
    me = lax.axis_index(axis)
    m = parts.shape[0] // k
    outs = exchange([(parts.astype(WIRE), axis, "scatter")] + list(extra), cid)
    slots = outs[0]
    mine = lax.dynamic_slice_in_dim(parts, me * m, m, axis=0)
    keep = (jnp.arange(k) != me).reshape((k,) + (1,) * (slots.ndim - 1))
    other = jnp.sum(jnp.where(keep, slots.astype(jnp.float32), 0.0), axis=0)
    return (mine + other,) + tuple(outs[1:])


def pair_reduce_scatter(parts, axis, cid, extra=()):
    k = lax.axis_size(axis)
    me = lax.axis_index(axis)
    p = me % 2
    m = parts.shape[0] // k
    quad = parts.reshape((k // 2, 2, m) + parts.shape[1:])
    mine_half = jnp.where(p == 0, quad[:, 0], quad[:, 1])
    theirs_half = jnp.where(p == 0, quad[:, 1], quad[:, 0])
    (got,) = exchange([(theirs_half, axis, "pswap")], cid)
    pair = mine_half + got
    outs = exchange([(pair.astype(WIRE), axis, "pscatter")] + list(extra), cid + 1)
    slots = outs[0]
    own = lax.dynamic_index_in_dim(pair, me // 2, axis=0, keepdims=False)
    keep = (jnp.arange(k // 2) != me // 2).reshape((k // 2,) + (1,) * (slots.ndim - 1))
    other = jnp.sum(jnp.where(keep, slots.astype(jnp.float32), 0.0), axis=0)
    return (own + other,) + tuple(outs[1:])


def per_device(
    stream_in, grad_out, gate_pre, up_pre, keep_mask, segment_ids, norm_gain, w_gate, w_up, w_down
):
    n_row = lax.axis_size("row")
    n_col = lax.axis_size("col")
    RG = "rgather" if n_row == 8 else "gather"
    PG = "prgather" if n_col == 16 else "pgather"
    tok_col, feat_loc = stream_in.shape
    tok_row, ff_loc = gate_pre.shape
    total = tok_col * n_col
    xs = stream_in.astype(jnp.float32)
    onehot = (segment_ids[:, None] == jnp.arange(SEGS, dtype=jnp.int32)[None, :]).astype(
        jnp.float32
    )
    stats = jnp.concatenate([jnp.sum(xs * xs, axis=1), jnp.sum(onehot, axis=0)])[None, :]
    (stats_all,) = exchange([(stats, "row", "gather")], 0)
    stats_sum = jnp.sum(stats_all, axis=(0, 1))
    squares, counts = stats_sum[:tok_col], stats_sum[tok_col:]
    weights = jnp.sum(onehot * (total / (SEGS * counts))[None, :], axis=1)
    recip = lax.rsqrt(squares / D + eps)
    normed = (xs * recip[:, None] * norm_gain[None, :]).astype(jnp.bfloat16)
    gate_f = gate_pre.astype(jnp.float32)
    up_f = up_pre.astype(jnp.float32)
    sig = jax.nn.sigmoid(gate_f)
    keep_f = keep_mask.astype(jnp.float32) * keep_scale
    dropped = (gate_f * sig * up_f * keep_f * weights[:, None]).astype(jnp.bfloat16)
    cot_full, dropped_full = exchange([(grad_out, "col", PG), (dropped, "row", RG)], 1)
    cot_full = pair_order(cot_full)
    dropped_full = dropped_full.reshape(total, ff_loc)
    back, normed_full = reduce_scatter(
        over_width(cot_full, w_down), "row", 2, [(normed, "col", PG)]
    )
    normed_full = normed_full.reshape(total, feat_loc)
    grad_act = back * weights[:, None] * keep_f
    grad_gpre = (grad_act * up_f * sig * (1.0 + gate_f * (1.0 - sig))).astype(jnp.bfloat16)
    grad_upre = (grad_act * gate_f * sig).astype(jnp.bfloat16)
    half = tok_col // 2
    n_chunk = tok_row // tok_col

    def split(v):
        v = v.reshape(n_chunk, 2, half, ff_loc)
        return v[:, 0].reshape(tok_row // 2, ff_loc), v[:, 1].reshape(tok_row // 2, ff_loc)

    def joined(a, b):
        a = a.reshape(n_row, n_chunk, 1, half, ff_loc)
        b = b.reshape(n_row, n_chunk, 1, half, ff_loc)
        both = jnp.concatenate([a, b], axis=2)
        return jnp.swapaxes(both, 0, 1).reshape(total, ff_loc)

    gpre_a, gpre_b = split(grad_gpre)
    upre_a, upre_b = split(grad_upre)
    ga_full, ua_full = exchange([(gpre_a, "row", RG), (upre_a, "row", RG)], 3)
    ga_full = ga_full.reshape(total // 2, ff_loc)
    ua_full = ua_full.reshape(total // 2, ff_loc)
    part_a = over_width(ga_full, w_gate) + over_width(ua_full, w_up)
    gn_a, gb_full, ub_full = pair_reduce_scatter(
        part_a, "col", 4, [(gpre_b, "row", RG), (upre_b, "row", RG)]
    )
    gb_full = gb_full.reshape(total // 2, ff_loc)
    ub_full = ub_full.reshape(total // 2, ff_loc)
    part_b = over_width(gb_full, w_gate) + over_width(ub_full, w_up)
    (gn_b,) = pair_reduce_scatter(part_b, "col", 6)
    grad_normed = jnp.concatenate([gn_a, gn_b], axis=0)
    gpre_full = joined(ga_full, gb_full)
    upre_full = joined(ua_full, ub_full)
    grad_down = over_tokens(dropped_full, cot_full).astype(jnp.bfloat16)
    grad_gate = over_tokens(normed_full, gpre_full).astype(jnp.bfloat16)
    grad_up = over_tokens(normed_full, upre_full).astype(jnp.bfloat16)
    scaled = grad_normed * norm_gain[None, :]
    (inner_all,) = exchange([(jnp.sum(scaled * xs, axis=1)[None, :], "row", "gather")], 8)
    inner = jnp.sum(inner_all, axis=(0, 1)) / D
    branch = recip[:, None] * (scaled - xs * (recip * recip * inner)[:, None])
    grad_in = (grad_out.astype(jnp.float32) + branch).astype(jnp.bfloat16)
    return (grad_in, grad_gate, grad_up, grad_down)


def solution(mesh):
    return jax.shard_map(
        per_device,
        mesh=mesh,
        in_specs=(
            P("col", "row"),
            P("col", "row"),
            P("row", "col"),
            P("row", "col"),
            P("row", "col"),
            P("row"),
            P("row"),
            P("row", "col"),
            P("row", "col"),
            P("col", "row"),
        ),
        out_specs=(P("col", "row"), P("row", "col"), P("row", "col"), P("col", "row")),
        check_vma=False,
    )
```

```python
import functools

import jax
import jax.numpy as jnp
from jax import lax
from jax.experimental import pallas as pl
from jax.experimental.pallas import tpu as pltpu
from jax.sharding import PartitionSpec as P

D = 8192
SEGS = 16
AXES = ("row", "col")
WIRE = jnp.bfloat16

eps = 1e-05
keep_scale = 1.0 / 0.9


def over_tokens(left, right):
    return lax.dot_general(
        left, right, (((0,), (0,)), ((), ())), preferred_element_type=jnp.float32
    )


def over_width(left, right):
    return lax.dot_general(
        left, right, (((1,), (1,)), ((), ())), preferred_element_type=jnp.float32
    )


def _dev(axis, idx):
    return tuple(idx if a == axis else lax.axis_index(a) for a in AXES)


def _barrier(modes, axes):
    barrier = pltpu.get_barrier_semaphore()
    count = 0
    for axis in sorted(set(axes)):
        k = lax.axis_size(axis)
        me = lax.axis_index(axis)
        kinds = {mode for mode, a in zip(modes, axes) if a == axis}
        if kinds <= {"pswap"}:
            peers = [1 - 2 * (me % 2)]
        elif kinds <= {"pswap", "pgather", "pscatter", "prgather"}:
            peers = [2 * d for d in range(1, k // 2)] + [1 - 2 * (me % 2)]
        else:
            peers = list(range(1, k))
        for d in peers:
            pl.semaphore_signal(
                barrier, inc=1, device_id=_dev(axis, (me + d) % k),
                device_id_type=pl.DeviceIdType.MESH,
            )
        count += len(peers)
    pl.semaphore_wait(barrier, count)


def _ring_pair_send(i, src_ref, slot, dev, me_g, ng, send_sem, recv_sem, sends, axis):
    ny = ng // 2
    ym, zm = me_g // 2, me_g % 2
    direct = [ym * 2 + 1 - zm] + [((ym + dy) % ny) * 2 + z for dy in (1, ny - 1) for z in (0, 1)]
    for d, tgt in enumerate(direct):
        c = pltpu.make_async_remote_copy(
            src_ref, slot(me_g), send_sem.at[i, d], recv_sem.at[i, me_g],
            device_id=_dev(axis, dev(tgt)), device_id_type=pl.DeviceIdType.MESH,
        )
        c.start()
        sends.append(c)
    h = src_ref.shape[0] // 2
    for e, (dy, lo, off) in enumerate([(ny - 1, 0, 0), (1, h, ng)]):
        for z in (0, 1):
            src = ((ym + dy) % ny) * 2 + z
            pltpu.make_async_remote_copy(
                src_ref, slot(src), send_sem.at[i, 0], recv_sem.at[i, src],
                device_id=_dev(axis, dev(src)), device_id_type=pl.DeviceIdType.MESH,
            ).wait_recv()
            fwd = ((ym + ny - dy) % ny) * 2 + zm
            c = pltpu.make_async_remote_copy(
                slot(src).at[pl.ds(lo, h)], slot(src).at[pl.ds(lo, h)],
                send_sem.at[i, ng + 2 * e + z], recv_sem.at[i, off + src],
                device_id=_dev(axis, dev(fwd)), device_id_type=pl.DeviceIdType.MESH,
            )
            c.start()
            sends.append(c)


def _ring_pair_wait(i, src_ref, slot, dev, me_g, ng, send_sem, recv_sem, axis):
    ny = ng // 2
    ym, zm = me_g // 2, me_g % 2
    h = src_ref.shape[0] // 2
    peer = ym * 2 + 1 - zm
    pltpu.make_async_remote_copy(
        src_ref, slot(peer), send_sem.at[i, 0], recv_sem.at[i, peer],
        device_id=_dev(axis, dev(peer)), device_id_type=pl.DeviceIdType.MESH,
    ).wait_recv()
    for z in (0, 1):
        far = ((ym + 2) % ny) * 2 + z
        for lo, off in ((0, 0), (h, ng)):
            pltpu.make_async_remote_copy(
                slot(far).at[pl.ds(lo, h)], slot(far).at[pl.ds(lo, h)],
                send_sem.at[i, 0], recv_sem.at[i, off + far],
                device_id=_dev(axis, dev(far)), device_id_type=pl.DeviceIdType.MESH,
            ).wait_recv()


def _exchange_kernel(modes, axes, *refs):
    n = len(modes)
    ins, outs = refs[:n], refs[n:2 * n]
    send_sem, recv_sem, local_sem = refs[2 * n:]
    _barrier(modes, axes)
    sends, relays = [], []
    for i, (mode, axis) in enumerate(zip(modes, axes)):
        k = lax.axis_size(axis)
        me = lax.axis_index(axis)
        if mode == "rgather":
            loc = pltpu.make_async_copy(ins[i], outs[i].at[me], local_sem.at[i])
            loc.start()
            sends.append(loc)
            _ring_pair_send(i, ins[i], lambda g: outs[i].at[g], lambda g: g, me, k,
                            send_sem, recv_sem, sends, axis)
            continue
        if mode == "prgather":
            p = me % 2
            partner = me + 1 - 2 * p
            slot = lambda g: outs[i].at[p, g]
            dev = lambda g: g * 2 + p
            loc = pltpu.make_async_copy(ins[i], slot(me // 2), local_sem.at[i])
            loc.start()
            _ring_pair_send(i, ins[i], slot, dev, me // 2, k // 2, send_sem, recv_sem, sends, axis)
            _ring_pair_wait(i, ins[i], slot, dev, me // 2, k // 2, send_sem, recv_sem, axis)
            loc.wait()
            c = pltpu.make_async_remote_copy(
                outs[i].at[p], outs[i].at[p], send_sem.at[i, 2 * k - 1], recv_sem.at[i, 2 * k - 1],
                device_id=_dev(axis, partner), device_id_type=pl.DeviceIdType.MESH,
            )
            c.start()
            sends.append(c)
            continue
        if mode == "pswap":
            c = pltpu.make_async_remote_copy(
                ins[i].at[:, 1 - me % 2], outs[i], send_sem.at[i, 0], recv_sem.at[i, me],
                device_id=_dev(axis, me + 1 - 2 * (me % 2)),
                device_id_type=pl.DeviceIdType.MESH,
            )
            c.start()
            sends.append(c)
            continue
        if mode == "pscatter":
            for d in range(1, k // 2):
                tgt = (me + 2 * d) % k
                c = pltpu.make_async_remote_copy(
                    ins[i].at[tgt // 2], outs[i].at[me // 2], send_sem.at[i, d],
                    recv_sem.at[i, me], device_id=_dev(axis, tgt),
                    device_id_type=pl.DeviceIdType.MESH,
                )
                c.start()
                sends.append(c)
            continue
        if mode == "pgather":
            p = me % 2
            for d in range(1, k // 2):
                tgt = (me + 2 * d) % k
                c = pltpu.make_async_remote_copy(
                    ins[i], outs[i].at[p, me // 2], send_sem.at[i, d], recv_sem.at[i, me],
                    device_id=_dev(axis, tgt), device_id_type=pl.DeviceIdType.MESH,
                )
                c.start()
                sends.append(c)
            loc = pltpu.make_async_copy(ins[i], outs[i].at[p, me // 2], local_sem.at[i])
            loc.start()
            relays.append((i, loc))
            continue
        m = outs[i].shape[1]
        for d in range(1, k):
            tgt = (me + d) % k
            src = ins[i] if mode == "gather" else ins[i].at[pl.ds(tgt * m, m)]
            c = pltpu.make_async_remote_copy(
                src, outs[i].at[me], send_sem.at[i, d], recv_sem.at[i, me],
                device_id=_dev(axis, tgt), device_id_type=pl.DeviceIdType.MESH,
            )
            c.start()
            sends.append(c)
        if mode == "gather":
            loc = pltpu.make_async_copy(ins[i], outs[i].at[me], local_sem.at[i])
            loc.start()
            sends.append(loc)
    for i, loc in relays:
        axis = axes[i]
        k = lax.axis_size(axis)
        me = lax.axis_index(axis)
        p = me % 2
        partner = me + 1 - 2 * p
        for d in range(1, k // 2):
            srcdev = (me + k - 2 * d) % k
            pltpu.make_async_remote_copy(
                ins[i], outs[i].at[p, srcdev // 2], send_sem.at[i, d], recv_sem.at[i, srcdev],
                device_id=_dev(axis, srcdev), device_id_type=pl.DeviceIdType.MESH,
            ).wait_recv()
        loc.wait()
        c = pltpu.make_async_remote_copy(
            outs[i].at[p], outs[i].at[p], send_sem.at[i, 0], recv_sem.at[i, me],
            device_id=_dev(axis, partner), device_id_type=pl.DeviceIdType.MESH,
        )
        c.start()
        sends.append(c)
    for c in sends:
        if c.is_remote:
            c.wait_send()
        else:
            c.wait()
    for i, (mode, axis) in enumerate(zip(modes, axes)):
        k = lax.axis_size(axis)
        me = lax.axis_index(axis)
        if mode == "rgather":
            _ring_pair_wait(i, ins[i], lambda g: outs[i].at[g], lambda g: g, me, k,
                            send_sem, recv_sem, axis)
            continue
        if mode == "prgather":
            p = me % 2
            partner = me + 1 - 2 * p
            pltpu.make_async_remote_copy(
                outs[i].at[1 - p], outs[i].at[1 - p], send_sem.at[i, 2 * k - 1],
                recv_sem.at[i, 2 * k - 1],
                device_id=_dev(axis, partner), device_id_type=pl.DeviceIdType.MESH,
            ).wait_recv()
            continue
        if mode == "pswap":
            partner = me + 1 - 2 * (me % 2)
            pltpu.make_async_remote_copy(
                outs[i], outs[i], send_sem.at[i, 0], recv_sem.at[i, partner],
                device_id=_dev(axis, partner), device_id_type=pl.DeviceIdType.MESH,
            ).wait_recv()
            continue
        if mode == "pscatter":
            for d in range(1, k // 2):
                srcdev = (me + k - 2 * d) % k
                pltpu.make_async_remote_copy(
                    ins[i].at[0], outs[i].at[srcdev // 2], send_sem.at[i, d],
                    recv_sem.at[i, srcdev], device_id=_dev(axis, srcdev),
                    device_id_type=pl.DeviceIdType.MESH,
                ).wait_recv()
            continue
        if mode == "pgather":
            p = me % 2
            partner = me + 1 - 2 * p
            pltpu.make_async_remote_copy(
                outs[i].at[1 - p], outs[i].at[1 - p], send_sem.at[i, 0], recv_sem.at[i, partner],
                device_id=_dev(axis, partner), device_id_type=pl.DeviceIdType.MESH,
            ).wait_recv()
            continue
        m = outs[i].shape[1]
        for d in range(1, k):
            srcdev = (me + k - d) % k
            src = ins[i] if mode == "gather" else ins[i].at[pl.ds(0, m)]
            pltpu.make_async_remote_copy(
                src, outs[i].at[srcdev], send_sem.at[i, d], recv_sem.at[i, srcdev],
                device_id=_dev(axis, srcdev), device_id_type=pl.DeviceIdType.MESH,
            ).wait_recv()


def exchange(items, cid):
    modes = tuple(mode for _, _, mode in items)
    axes = tuple(axis for _, axis, _ in items)
    out_shapes = []
    kmax = 1
    for x, axis, mode in items:
        k = lax.axis_size(axis)
        kmax = max(kmax, k)
        if mode in ("gather", "rgather"):
            out_shapes.append(jax.ShapeDtypeStruct((k,) + x.shape, x.dtype))
        elif mode == "pswap":
            out_shapes.append(jax.ShapeDtypeStruct((x.shape[0],) + x.shape[2:], x.dtype))
        elif mode == "pscatter":
            out_shapes.append(jax.ShapeDtypeStruct(x.shape, x.dtype))
        elif mode in ("pgather", "prgather"):
            out_shapes.append(jax.ShapeDtypeStruct((2, k // 2) + x.shape, x.dtype))
        else:
            out_shapes.append(
                jax.ShapeDtypeStruct((k, x.shape[0] // k) + x.shape[1:], x.dtype)
            )
    n = len(items)
    return pl.pallas_call(
        functools.partial(_exchange_kernel, modes, axes),
        out_shape=tuple(out_shapes),
        in_specs=[pl.BlockSpec(memory_space=pl.ANY)] * n,
        out_specs=tuple(pl.BlockSpec(memory_space=pl.ANY) for _ in range(n)),
        scratch_shapes=[
            pltpu.SemaphoreType.DMA((n, 2 * kmax)),
            pltpu.SemaphoreType.DMA((n, 2 * kmax)),
            pltpu.SemaphoreType.DMA((n,)),
        ],
        compiler_params=pltpu.CompilerParams(collective_id=cid, has_side_effects=True),
    )(*[x for x, _, _ in items])


def pair_order(v):
    return jnp.swapaxes(v, 0, 1).reshape((-1,) + v.shape[3:])


def reduce_scatter(parts, axis, cid, extra=()):
    k = lax.axis_size(axis)
    me = lax.axis_index(axis)
    m = parts.shape[0] // k
    outs = exchange([(parts.astype(WIRE), axis, "scatter")] + list(extra), cid)
    slots = outs[0]
    mine = lax.dynamic_slice_in_dim(parts, me * m, m, axis=0)
    keep = (jnp.arange(k) != me).reshape((k,) + (1,) * (slots.ndim - 1))
    other = jnp.sum(jnp.where(keep, slots.astype(jnp.float32), 0.0), axis=0)
    return (mine + other,) + tuple(outs[1:])


def pair_reduce_scatter(parts, axis, cid, extra=()):
    k = lax.axis_size(axis)
    me = lax.axis_index(axis)
    p = me % 2
    m = parts.shape[0] // k
    quad = parts.reshape((k // 2, 2, m) + parts.shape[1:])
    (got,) = exchange([(quad, axis, "pswap")], cid)
    pair = lax.dynamic_index_in_dim(quad, p, axis=1, keepdims=False) + got
    outs = exchange([(pair.astype(WIRE), axis, "pscatter")] + list(extra), cid + 1)
    slots = outs[0]
    own = lax.dynamic_index_in_dim(pair, me // 2, axis=0, keepdims=False)
    keep = (jnp.arange(k // 2) != me // 2).reshape((k // 2,) + (1,) * (slots.ndim - 1))
    other = jnp.sum(jnp.where(keep, slots.astype(jnp.float32), 0.0), axis=0)
    return (own + other,) + tuple(outs[1:])


def per_device(
    stream_in, grad_out, gate_pre, up_pre, keep_mask, segment_ids, norm_gain, w_gate, w_up, w_down
):
    n_row = lax.axis_size("row")
    n_col = lax.axis_size("col")
    RG = "rgather" if n_row == 8 else "gather"
    PG = "prgather" if n_col == 16 else "pgather"
    tok_col, feat_loc = stream_in.shape
    tok_row, ff_loc = gate_pre.shape
    total = tok_col * n_col
    xs = stream_in.astype(jnp.float32)
    onehot = (segment_ids[:, None] == jnp.arange(SEGS, dtype=jnp.int32)[None, :]).astype(
        jnp.float32
    )
    stats = jnp.concatenate([jnp.sum(xs * xs, axis=1), jnp.sum(onehot, axis=0)])[None, :]
    (stats_all,) = exchange([(stats, "row", "gather")], 0)
    stats_sum = jnp.sum(stats_all, axis=(0, 1))
    squares, counts = stats_sum[:tok_col], stats_sum[tok_col:]
    weights = jnp.sum(onehot * (total / (SEGS * counts))[None, :], axis=1)
    recip = lax.rsqrt(squares / D + eps)
    normed = (xs * recip[:, None] * norm_gain[None, :]).astype(jnp.bfloat16)
    gate_f = gate_pre.astype(jnp.float32)
    up_f = up_pre.astype(jnp.float32)
    sig = jax.nn.sigmoid(gate_f)
    keep_f = keep_mask.astype(jnp.float32) * keep_scale
    dropped = (gate_f * sig * up_f * keep_f * weights[:, None]).astype(jnp.bfloat16)
    cot_full, dropped_full = exchange([(grad_out, "col", PG), (dropped, "row", RG)], 1)
    cot_full = pair_order(cot_full)
    dropped_full = dropped_full.reshape(total, ff_loc)
    back, normed_full = reduce_scatter(
        over_width(cot_full, w_down), "row", 2, [(normed, "col", PG)]
    )
    normed_full = normed_full.reshape(total, feat_loc)
    grad_act = back * weights[:, None] * keep_f
    grad_gpre = (grad_act * up_f * sig * (1.0 + gate_f * (1.0 - sig))).astype(jnp.bfloat16)
    grad_upre = (grad_act * gate_f * sig).astype(jnp.bfloat16)
    half = tok_col // 2
    n_chunk = tok_row // tok_col

    def split(v):
        v = v.reshape(n_chunk, 2, half, ff_loc)
        return v[:, 0].reshape(tok_row // 2, ff_loc), v[:, 1].reshape(tok_row // 2, ff_loc)

    def joined(a, b):
        a = a.reshape(n_row, n_chunk, 1, half, ff_loc)
        b = b.reshape(n_row, n_chunk, 1, half, ff_loc)
        both = jnp.concatenate([a, b], axis=2)
        return jnp.swapaxes(both, 0, 1).reshape(total, ff_loc)

    gpre_a, gpre_b = split(grad_gpre)
    upre_a, upre_b = split(grad_upre)
    ga_full, ua_full = exchange([(gpre_a, "row", RG), (upre_a, "row", RG)], 3)
    ga_full = ga_full.reshape(total // 2, ff_loc)
    ua_full = ua_full.reshape(total // 2, ff_loc)
    part_a = over_width(ga_full, w_gate) + over_width(ua_full, w_up)
    gn_a, gb_full, ub_full = pair_reduce_scatter(
        part_a, "col", 4, [(gpre_b, "row", RG), (upre_b, "row", RG)]
    )
    gb_full = gb_full.reshape(total // 2, ff_loc)
    ub_full = ub_full.reshape(total // 2, ff_loc)
    part_b = over_width(gb_full, w_gate) + over_width(ub_full, w_up)
    (gn_b,) = pair_reduce_scatter(part_b, "col", 6)
    grad_normed = jnp.concatenate([gn_a, gn_b], axis=0)
    gpre_full = joined(ga_full, gb_full)
    upre_full = joined(ua_full, ub_full)
    grad_down = over_tokens(dropped_full, cot_full).astype(jnp.bfloat16)
    grad_gate = over_tokens(normed_full, gpre_full).astype(jnp.bfloat16)
    grad_up = over_tokens(normed_full, upre_full).astype(jnp.bfloat16)
    scaled = grad_normed * norm_gain[None, :]
    (inner_all,) = exchange([(jnp.sum(scaled * xs, axis=1)[None, :], "row", "gather")], 8)
    inner = jnp.sum(inner_all, axis=(0, 1)) / D
    branch = recip[:, None] * (scaled - xs * (recip * recip * inner)[:, None])
    grad_in = (grad_out.astype(jnp.float32) + branch).astype(jnp.bfloat16)
    return (grad_in, grad_gate, grad_up, grad_down)


def solution(mesh):
    return jax.shard_map(
        per_device,
        mesh=mesh,
        in_specs=(
            P("col", "row"),
            P("col", "row"),
            P("row", "col"),
            P("row", "col"),
            P("row", "col"),
            P("row"),
            P("row"),
            P("row", "col"),
            P("row", "col"),
            P("col", "row"),
        ),
        out_specs=(P("col", "row"), P("row", "col"), P("row", "col"), P("col", "row")),
        check_vma=False,
    )
```

```python
import functools

import jax
import jax.numpy as jnp
from jax import lax
from jax.experimental import pallas as pl
from jax.experimental.pallas import tpu as pltpu
from jax.sharding import PartitionSpec as P

D = 8192
SEGS = 16
AXES = ("row", "col")
WIRE = jnp.bfloat16

eps = 1e-05
keep_scale = 1.0 / 0.9


def over_tokens(left, right):
    return lax.dot_general(
        left, right, (((0,), (0,)), ((), ())), preferred_element_type=jnp.float32
    )


def over_width(left, right):
    return lax.dot_general(
        left, right, (((1,), (1,)), ((), ())), preferred_element_type=jnp.float32
    )


def _dev(axis, idx):
    return tuple(idx if a == axis else lax.axis_index(a) for a in AXES)


def _barrier(modes, axes):
    barrier = pltpu.get_barrier_semaphore()
    count = 0
    for axis in sorted(set(axes)):
        k = lax.axis_size(axis)
        me = lax.axis_index(axis)
        kinds = {mode for mode, a in zip(modes, axes) if a == axis}
        if kinds <= {"pswap"}:
            peers = [1 - 2 * (me % 2)]
        elif kinds <= {"pswap", "pgather", "pscatter", "prgather"}:
            peers = [2 * d for d in range(1, k // 2)] + [1 - 2 * (me % 2)]
        else:
            peers = list(range(1, k))
        for d in peers:
            pl.semaphore_signal(
                barrier, inc=1, device_id=_dev(axis, (me + d) % k),
                device_id_type=pl.DeviceIdType.MESH,
            )
        count += len(peers)
    pl.semaphore_wait(barrier, count)


def _ring_pair_send(i, src_ref, slot, dev, me_g, ng, send_sem, recv_sem, sends, axis, part):
    ny = ng // 2
    ym, zm = me_g // 2, me_g % 2
    direct = [ym * 2 + 1 - zm] + [((ym + dy) % ny) * 2 + z for dy in (1, ny - 1) for z in (0, 1)]
    if part == "direct":
        for d, tgt in enumerate(direct):
            c = pltpu.make_async_remote_copy(
                src_ref, slot(me_g), send_sem.at[i, d], recv_sem.at[i, me_g],
                device_id=_dev(axis, dev(tgt)), device_id_type=pl.DeviceIdType.MESH,
            )
            c.start()
            sends.append(c)
        return
    h = src_ref.shape[0] // 2
    for e, (dy, lo, off) in enumerate([(ny - 1, 0, 0), (1, h, ng)]):
        for z in (0, 1):
            src = ((ym + dy) % ny) * 2 + z
            pltpu.make_async_remote_copy(
                src_ref, slot(src), send_sem.at[i, 0], recv_sem.at[i, src],
                device_id=_dev(axis, dev(src)), device_id_type=pl.DeviceIdType.MESH,
            ).wait_recv()
            fwd = ((ym + ny - dy) % ny) * 2 + zm
            c = pltpu.make_async_remote_copy(
                slot(src).at[pl.ds(lo, h)], slot(src).at[pl.ds(lo, h)],
                send_sem.at[i, ng + 2 * e + z], recv_sem.at[i, off + src],
                device_id=_dev(axis, dev(fwd)), device_id_type=pl.DeviceIdType.MESH,
            )
            c.start()
            sends.append(c)


def _ring_pair_wait(i, src_ref, slot, dev, me_g, ng, send_sem, recv_sem, axis):
    ny = ng // 2
    ym, zm = me_g // 2, me_g % 2
    h = src_ref.shape[0] // 2
    peer = ym * 2 + 1 - zm
    pltpu.make_async_remote_copy(
        src_ref, slot(peer), send_sem.at[i, 0], recv_sem.at[i, peer],
        device_id=_dev(axis, dev(peer)), device_id_type=pl.DeviceIdType.MESH,
    ).wait_recv()
    for z in (0, 1):
        far = ((ym + 2) % ny) * 2 + z
        for lo, off in ((0, 0), (h, ng)):
            pltpu.make_async_remote_copy(
                slot(far).at[pl.ds(lo, h)], slot(far).at[pl.ds(lo, h)],
                send_sem.at[i, 0], recv_sem.at[i, off + far],
                device_id=_dev(axis, dev(far)), device_id_type=pl.DeviceIdType.MESH,
            ).wait_recv()


def _exchange_kernel(modes, axes, *refs):
    n = len(modes)
    ins, outs = refs[:n], refs[n:2 * n]
    send_sem, recv_sem, local_sem = refs[2 * n:]
    _barrier(modes, axes)
    sends, relays, locals_ = [], [], {}
    for i, (mode, axis) in enumerate(zip(modes, axes)):
        k = lax.axis_size(axis)
        me = lax.axis_index(axis)
        if mode == "rgather":
            loc = pltpu.make_async_copy(ins[i], outs[i].at[me], local_sem.at[i])
            loc.start()
            sends.append(loc)
            _ring_pair_send(i, ins[i], lambda g: outs[i].at[g], lambda g: g, me, k,
                            send_sem, recv_sem, sends, axis, "direct")
            continue
        if mode == "prgather":
            p = me % 2
            loc = pltpu.make_async_copy(ins[i], outs[i].at[p, me // 2], local_sem.at[i])
            loc.start()
            locals_[i] = loc
            _ring_pair_send(i, ins[i], lambda g: outs[i].at[p, g], lambda g: g * 2 + p,
                            me // 2, k // 2, send_sem, recv_sem, sends, axis, "direct")
            continue
        if mode == "pswap":
            c = pltpu.make_async_remote_copy(
                ins[i].at[:, 1 - me % 2], outs[i], send_sem.at[i, 0], recv_sem.at[i, me],
                device_id=_dev(axis, me + 1 - 2 * (me % 2)),
                device_id_type=pl.DeviceIdType.MESH,
            )
            c.start()
            sends.append(c)
            continue
        if mode == "pscatter":
            for d in range(1, k // 2):
                tgt = (me + 2 * d) % k
                c = pltpu.make_async_remote_copy(
                    ins[i].at[tgt // 2], outs[i].at[me // 2], send_sem.at[i, d],
                    recv_sem.at[i, me], device_id=_dev(axis, tgt),
                    device_id_type=pl.DeviceIdType.MESH,
                )
                c.start()
                sends.append(c)
            continue
        if mode == "pgather":
            p = me % 2
            for d in range(1, k // 2):
                tgt = (me + 2 * d) % k
                c = pltpu.make_async_remote_copy(
                    ins[i], outs[i].at[p, me // 2], send_sem.at[i, d], recv_sem.at[i, me],
                    device_id=_dev(axis, tgt), device_id_type=pl.DeviceIdType.MESH,
                )
                c.start()
                sends.append(c)
            loc = pltpu.make_async_copy(ins[i], outs[i].at[p, me // 2], local_sem.at[i])
            loc.start()
            relays.append((i, loc))
            continue
        m = outs[i].shape[1]
        for d in range(1, k):
            tgt = (me + d) % k
            src = ins[i] if mode == "gather" else ins[i].at[pl.ds(tgt * m, m)]
            c = pltpu.make_async_remote_copy(
                src, outs[i].at[me], send_sem.at[i, d], recv_sem.at[i, me],
                device_id=_dev(axis, tgt), device_id_type=pl.DeviceIdType.MESH,
            )
            c.start()
            sends.append(c)
        if mode == "gather":
            loc = pltpu.make_async_copy(ins[i], outs[i].at[me], local_sem.at[i])
            loc.start()
            sends.append(loc)
    for i, (mode, axis) in enumerate(zip(modes, axes)):
        k = lax.axis_size(axis)
        me = lax.axis_index(axis)
        if mode == "rgather":
            _ring_pair_send(i, ins[i], lambda g: outs[i].at[g], lambda g: g, me, k,
                            send_sem, recv_sem, sends, axis, "relay")
        elif mode == "prgather":
            p = me % 2
            _ring_pair_send(i, ins[i], lambda g: outs[i].at[p, g], lambda g: g * 2 + p,
                            me // 2, k // 2, send_sem, recv_sem, sends, axis, "relay")
    for i, (mode, axis) in enumerate(zip(modes, axes)):
        if mode != "prgather":
            continue
        k = lax.axis_size(axis)
        me = lax.axis_index(axis)
        p = me % 2
        partner = me + 1 - 2 * p
        _ring_pair_wait(i, ins[i], lambda g: outs[i].at[p, g], lambda g: g * 2 + p,
                        me // 2, k // 2, send_sem, recv_sem, axis)
        locals_[i].wait()
        c = pltpu.make_async_remote_copy(
            outs[i].at[p], outs[i].at[p], send_sem.at[i, 2 * k - 1], recv_sem.at[i, 2 * k - 1],
            device_id=_dev(axis, partner), device_id_type=pl.DeviceIdType.MESH,
        )
        c.start()
        sends.append(c)
    for i, loc in relays:
        axis = axes[i]
        k = lax.axis_size(axis)
        me = lax.axis_index(axis)
        p = me % 2
        partner = me + 1 - 2 * p
        for d in range(1, k // 2):
            srcdev = (me + k - 2 * d) % k
            pltpu.make_async_remote_copy(
                ins[i], outs[i].at[p, srcdev // 2], send_sem.at[i, d], recv_sem.at[i, srcdev],
                device_id=_dev(axis, srcdev), device_id_type=pl.DeviceIdType.MESH,
            ).wait_recv()
        loc.wait()
        c = pltpu.make_async_remote_copy(
            outs[i].at[p], outs[i].at[p], send_sem.at[i, 0], recv_sem.at[i, me],
            device_id=_dev(axis, partner), device_id_type=pl.DeviceIdType.MESH,
        )
        c.start()
        sends.append(c)
    for c in sends:
        if c.is_remote:
            c.wait_send()
        else:
            c.wait()
    for i, (mode, axis) in enumerate(zip(modes, axes)):
        k = lax.axis_size(axis)
        me = lax.axis_index(axis)
        if mode == "rgather":
            _ring_pair_wait(i, ins[i], lambda g: outs[i].at[g], lambda g: g, me, k,
                            send_sem, recv_sem, axis)
            continue
        if mode == "prgather":
            p = me % 2
            partner = me + 1 - 2 * p
            pltpu.make_async_remote_copy(
                outs[i].at[1 - p], outs[i].at[1 - p], send_sem.at[i, 2 * k - 1],
                recv_sem.at[i, 2 * k - 1],
                device_id=_dev(axis, partner), device_id_type=pl.DeviceIdType.MESH,
            ).wait_recv()
            continue
        if mode == "pswap":
            partner = me + 1 - 2 * (me % 2)
            pltpu.make_async_remote_copy(
                outs[i], outs[i], send_sem.at[i, 0], recv_sem.at[i, partner],
                device_id=_dev(axis, partner), device_id_type=pl.DeviceIdType.MESH,
            ).wait_recv()
            continue
        if mode == "pscatter":
            for d in range(1, k // 2):
                srcdev = (me + k - 2 * d) % k
                pltpu.make_async_remote_copy(
                    ins[i].at[0], outs[i].at[srcdev // 2], send_sem.at[i, d],
                    recv_sem.at[i, srcdev], device_id=_dev(axis, srcdev),
                    device_id_type=pl.DeviceIdType.MESH,
                ).wait_recv()
            continue
        if mode == "pgather":
            p = me % 2
            partner = me + 1 - 2 * p
            pltpu.make_async_remote_copy(
                outs[i].at[1 - p], outs[i].at[1 - p], send_sem.at[i, 0], recv_sem.at[i, partner],
                device_id=_dev(axis, partner), device_id_type=pl.DeviceIdType.MESH,
            ).wait_recv()
            continue
        m = outs[i].shape[1]
        for d in range(1, k):
            srcdev = (me + k - d) % k
            src = ins[i] if mode == "gather" else ins[i].at[pl.ds(0, m)]
            pltpu.make_async_remote_copy(
                src, outs[i].at[srcdev], send_sem.at[i, d], recv_sem.at[i, srcdev],
                device_id=_dev(axis, srcdev), device_id_type=pl.DeviceIdType.MESH,
            ).wait_recv()


def exchange(items, cid):
    modes = tuple(mode for _, _, mode in items)
    axes = tuple(axis for _, axis, _ in items)
    out_shapes = []
    kmax = 1
    for x, axis, mode in items:
        k = lax.axis_size(axis)
        kmax = max(kmax, k)
        if mode in ("gather", "rgather"):
            out_shapes.append(jax.ShapeDtypeStruct((k,) + x.shape, x.dtype))
        elif mode == "pswap":
            out_shapes.append(jax.ShapeDtypeStruct((x.shape[0],) + x.shape[2:], x.dtype))
        elif mode == "pscatter":
            out_shapes.append(jax.ShapeDtypeStruct(x.shape, x.dtype))
        elif mode in ("pgather", "prgather"):
            out_shapes.append(jax.ShapeDtypeStruct((2, k // 2) + x.shape, x.dtype))
        else:
            out_shapes.append(
                jax.ShapeDtypeStruct((k, x.shape[0] // k) + x.shape[1:], x.dtype)
            )
    n = len(items)
    return pl.pallas_call(
        functools.partial(_exchange_kernel, modes, axes),
        out_shape=tuple(out_shapes),
        in_specs=[pl.BlockSpec(memory_space=pl.ANY)] * n,
        out_specs=tuple(pl.BlockSpec(memory_space=pl.ANY) for _ in range(n)),
        scratch_shapes=[
            pltpu.SemaphoreType.DMA((n, 2 * kmax)),
            pltpu.SemaphoreType.DMA((n, 2 * kmax)),
            pltpu.SemaphoreType.DMA((n,)),
        ],
        compiler_params=pltpu.CompilerParams(collective_id=cid, has_side_effects=True),
    )(*[x for x, _, _ in items])


def pair_order(v):
    return jnp.swapaxes(v, 0, 1).reshape((-1,) + v.shape[3:])


def reduce_scatter(parts, axis, cid, extra=()):
    k = lax.axis_size(axis)
    me = lax.axis_index(axis)
    m = parts.shape[0] // k
    outs = exchange([(parts.astype(WIRE), axis, "scatter")] + list(extra), cid)
    slots = outs[0]
    mine = lax.dynamic_slice_in_dim(parts, me * m, m, axis=0)
    keep = (jnp.arange(k) != me).reshape((k,) + (1,) * (slots.ndim - 1))
    other = jnp.sum(jnp.where(keep, slots.astype(jnp.float32), 0.0), axis=0)
    return (mine + other,) + tuple(outs[1:])


def pair_reduce_scatter(parts, axis, cid, extra=()):
    k = lax.axis_size(axis)
    me = lax.axis_index(axis)
    p = me % 2
    m = parts.shape[0] // k
    quad = parts.reshape((k // 2, 2, m) + parts.shape[1:])
    (got,) = exchange([(quad, axis, "pswap")], cid)
    pair = lax.dynamic_index_in_dim(quad, p, axis=1, keepdims=False) + got
    outs = exchange([(pair.astype(WIRE), axis, "pscatter")] + list(extra), cid + 1)
    slots = outs[0]
    own = lax.dynamic_index_in_dim(pair, me // 2, axis=0, keepdims=False)
    keep = (jnp.arange(k // 2) != me // 2).reshape((k // 2,) + (1,) * (slots.ndim - 1))
    other = jnp.sum(jnp.where(keep, slots.astype(jnp.float32), 0.0), axis=0)
    return (own + other,) + tuple(outs[1:])


def per_device(
    stream_in, grad_out, gate_pre, up_pre, keep_mask, segment_ids, norm_gain, w_gate, w_up, w_down
):
    n_row = lax.axis_size("row")
    n_col = lax.axis_size("col")
    RG = "rgather" if n_row == 8 else "gather"
    PG = "prgather" if n_col == 16 else "pgather"
    tok_col, feat_loc = stream_in.shape
    tok_row, ff_loc = gate_pre.shape
    total = tok_col * n_col
    xs = stream_in.astype(jnp.float32)
    onehot = (segment_ids[:, None] == jnp.arange(SEGS, dtype=jnp.int32)[None, :]).astype(
        jnp.float32
    )
    stats = jnp.concatenate([jnp.sum(xs * xs, axis=1), jnp.sum(onehot, axis=0)])[None, :]
    (stats_all,) = exchange([(stats, "row", "gather")], 0)
    stats_sum = jnp.sum(stats_all, axis=(0, 1))
    squares, counts = stats_sum[:tok_col], stats_sum[tok_col:]
    weights = jnp.sum(onehot * (total / (SEGS * counts))[None, :], axis=1)
    recip = lax.rsqrt(squares / D + eps)
    normed = (xs * recip[:, None] * norm_gain[None, :]).astype(jnp.bfloat16)
    gate_f = gate_pre.astype(jnp.float32)
    up_f = up_pre.astype(jnp.float32)
    sig = jax.nn.sigmoid(gate_f)
    keep_f = keep_mask.astype(jnp.float32) * keep_scale
    dropped = (gate_f * sig * up_f * keep_f * weights[:, None]).astype(jnp.bfloat16)
    cot_full, dropped_full = exchange([(grad_out, "col", PG), (dropped, "row", RG)], 1)
    cot_full = pair_order(cot_full)
    dropped_full = dropped_full.reshape(total, ff_loc)
    back, normed_full = reduce_scatter(
        over_width(cot_full, w_down), "row", 2, [(normed, "col", PG)]
    )
    normed_full = normed_full.reshape(total, feat_loc)
    grad_act = back * weights[:, None] * keep_f
    grad_gpre = (grad_act * up_f * sig * (1.0 + gate_f * (1.0 - sig))).astype(jnp.bfloat16)
    grad_upre = (grad_act * gate_f * sig).astype(jnp.bfloat16)
    half = tok_col // 2
    n_chunk = tok_row // tok_col

    def split(v):
        v = v.reshape(n_chunk, 2, half, ff_loc)
        return v[:, 0].reshape(tok_row // 2, ff_loc), v[:, 1].reshape(tok_row // 2, ff_loc)

    def joined(a, b):
        a = a.reshape(n_row, n_chunk, 1, half, ff_loc)
        b = b.reshape(n_row, n_chunk, 1, half, ff_loc)
        both = jnp.concatenate([a, b], axis=2)
        return jnp.swapaxes(both, 0, 1).reshape(total, ff_loc)

    gpre_a, gpre_b = split(grad_gpre)
    upre_a, upre_b = split(grad_upre)
    ga_full, ua_full = exchange([(gpre_a, "row", RG), (upre_a, "row", RG)], 3)
    ga_full = ga_full.reshape(total // 2, ff_loc)
    ua_full = ua_full.reshape(total // 2, ff_loc)
    part_a = over_width(ga_full, w_gate) + over_width(ua_full, w_up)
    gn_a, gb_full, ub_full = pair_reduce_scatter(
        part_a, "col", 4, [(gpre_b, "row", RG), (upre_b, "row", RG)]
    )
    gb_full = gb_full.reshape(total // 2, ff_loc)
    ub_full = ub_full.reshape(total // 2, ff_loc)
    part_b = over_width(gb_full, w_gate) + over_width(ub_full, w_up)
    (gn_b,) = pair_reduce_scatter(part_b, "col", 6)
    grad_normed = jnp.concatenate([gn_a, gn_b], axis=0)
    gpre_full = joined(ga_full, gb_full)
    upre_full = joined(ua_full, ub_full)
    grad_down = over_tokens(dropped_full, cot_full).astype(jnp.bfloat16)
    grad_gate = over_tokens(normed_full, gpre_full).astype(jnp.bfloat16)
    grad_up = over_tokens(normed_full, upre_full).astype(jnp.bfloat16)
    scaled = grad_normed * norm_gain[None, :]
    (inner_all,) = exchange([(jnp.sum(scaled * xs, axis=1)[None, :], "row", "gather")], 8)
    inner = jnp.sum(inner_all, axis=(0, 1)) / D
    branch = recip[:, None] * (scaled - xs * (recip * recip * inner)[:, None])
    grad_in = (grad_out.astype(jnp.float32) + branch).astype(jnp.bfloat16)
    return (grad_in, grad_gate, grad_up, grad_down)


def solution(mesh):
    return jax.shard_map(
        per_device,
        mesh=mesh,
        in_specs=(
            P("col", "row"),
            P("col", "row"),
            P("row", "col"),
            P("row", "col"),
            P("row", "col"),
            P("row"),
            P("row"),
            P("row", "col"),
            P("row", "col"),
            P("col", "row"),
        ),
        out_specs=(P("col", "row"), P("row", "col"), P("row", "col"), P("col", "row")),
        check_vma=False,
    )
```

```python
import functools

import jax
import jax.numpy as jnp
from jax import lax
from jax.experimental import pallas as pl
from jax.experimental.pallas import tpu as pltpu
from jax.sharding import PartitionSpec as P

D = 8192
SEGS = 16
AXES = ("row", "col")
WIRE = jnp.bfloat16

eps = 1e-05
keep_scale = 1.0 / 0.9


def over_tokens(left, right):
    return lax.dot_general(
        left, right, (((0,), (0,)), ((), ())), preferred_element_type=jnp.float32
    )


def over_width(left, right):
    return lax.dot_general(
        left, right, (((1,), (1,)), ((), ())), preferred_element_type=jnp.float32
    )


def _dev(axis, idx):
    return tuple(idx if a == axis else lax.axis_index(a) for a in AXES)


def _barrier(modes, axes):
    barrier = pltpu.get_barrier_semaphore()
    count = 0
    for axis in sorted(set(axes)):
        k = lax.axis_size(axis)
        me = lax.axis_index(axis)
        kinds = {mode for mode, a in zip(modes, axes) if a == axis}
        if kinds <= {"pswap"}:
            peers = [1 - 2 * (me % 2)]
        elif kinds <= {"pswap", "pgather", "pscatter", "prgather"}:
            peers = [2 * d for d in range(1, k // 2)] + [1 - 2 * (me % 2)]
        else:
            peers = list(range(1, k))
        for d in peers:
            pl.semaphore_signal(
                barrier, inc=1, device_id=_dev(axis, (me + d) % k),
                device_id_type=pl.DeviceIdType.MESH,
            )
        count += len(peers)
    pl.semaphore_wait(barrier, count)


def _ring_pair_send(i, src_ref, slot, dev, me_g, ng, send_sem, recv_sem, sends, axis, part):
    ny = ng // 2
    ym, zm = me_g // 2, me_g % 2
    direct = [ym * 2 + 1 - zm] + [((ym + dy) % ny) * 2 + z for dy in (1, ny - 1) for z in (0, 1)]
    if part == "direct":
        for d, tgt in enumerate(direct):
            c = pltpu.make_async_remote_copy(
                src_ref, slot(me_g), send_sem.at[i, d], recv_sem.at[i, me_g],
                device_id=_dev(axis, dev(tgt)), device_id_type=pl.DeviceIdType.MESH,
            )
            c.start()
            sends.append(c)
        return
    h = src_ref.shape[0] // 2
    for e, (dy, lo, off) in enumerate([(ny - 1, 0, 0), (1, h, ng)]):
        for z in (0, 1):
            src = ((ym + dy) % ny) * 2 + z
            pltpu.make_async_remote_copy(
                src_ref, slot(src), send_sem.at[i, 0], recv_sem.at[i, src],
                device_id=_dev(axis, dev(src)), device_id_type=pl.DeviceIdType.MESH,
            ).wait_recv()
            fwd = ((ym + ny - dy) % ny) * 2 + zm
            c = pltpu.make_async_remote_copy(
                slot(src).at[pl.ds(lo, h)], slot(src).at[pl.ds(lo, h)],
                send_sem.at[i, ng + 2 * e + z], recv_sem.at[i, off + src],
                device_id=_dev(axis, dev(fwd)), device_id_type=pl.DeviceIdType.MESH,
            )
            c.start()
            sends.append(c)


def _ring_pair_wait(i, src_ref, slot, dev, me_g, ng, send_sem, recv_sem, axis):
    ny = ng // 2
    ym, zm = me_g // 2, me_g % 2
    h = src_ref.shape[0] // 2
    peer = ym * 2 + 1 - zm
    pltpu.make_async_remote_copy(
        src_ref, slot(peer), send_sem.at[i, 0], recv_sem.at[i, peer],
        device_id=_dev(axis, dev(peer)), device_id_type=pl.DeviceIdType.MESH,
    ).wait_recv()
    for z in (0, 1):
        far = ((ym + 2) % ny) * 2 + z
        for lo, off in ((0, 0), (h, ng)):
            pltpu.make_async_remote_copy(
                slot(far).at[pl.ds(lo, h)], slot(far).at[pl.ds(lo, h)],
                send_sem.at[i, 0], recv_sem.at[i, off + far],
                device_id=_dev(axis, dev(far)), device_id_type=pl.DeviceIdType.MESH,
            ).wait_recv()


def _exchange_kernel(modes, axes, *refs):
    n = len(modes)
    ins, outs = refs[:n], refs[n:2 * n]
    send_sem, recv_sem, local_sem = refs[2 * n:]
    _barrier(modes, axes)
    sends, relays, locals_ = [], [], {}
    for i, (mode, axis) in enumerate(zip(modes, axes)):
        k = lax.axis_size(axis)
        me = lax.axis_index(axis)
        if mode == "rgather":
            loc = pltpu.make_async_copy(ins[i], outs[i].at[me], local_sem.at[i])
            loc.start()
            sends.append(loc)
            _ring_pair_send(i, ins[i], lambda g: outs[i].at[g], lambda g: g, me, k,
                            send_sem, recv_sem, sends, axis, "direct")
            continue
        if mode == "prgather":
            p = me % 2
            loc = pltpu.make_async_copy(ins[i], outs[i].at[p, me // 2], local_sem.at[i])
            loc.start()
            locals_[i] = loc
            _ring_pair_send(i, ins[i], lambda g: outs[i].at[p, g], lambda g: g * 2 + p,
                            me // 2, k // 2, send_sem, recv_sem, sends, axis, "direct")
            continue
        if mode == "pswap":
            c = pltpu.make_async_remote_copy(
                ins[i].at[:, 1 - me % 2], outs[i], send_sem.at[i, 0], recv_sem.at[i, me],
                device_id=_dev(axis, me + 1 - 2 * (me % 2)),
                device_id_type=pl.DeviceIdType.MESH,
            )
            c.start()
            sends.append(c)
            continue
        if mode == "pscatter":
            for d in range(1, k // 2):
                tgt = (me + 2 * d) % k
                c = pltpu.make_async_remote_copy(
                    ins[i].at[tgt // 2], outs[i].at[me // 2], send_sem.at[i, d],
                    recv_sem.at[i, me], device_id=_dev(axis, tgt),
                    device_id_type=pl.DeviceIdType.MESH,
                )
                c.start()
                sends.append(c)
            continue
        if mode == "pgather":
            p = me % 2
            for d in range(1, k // 2):
                tgt = (me + 2 * d) % k
                c = pltpu.make_async_remote_copy(
                    ins[i], outs[i].at[p, me // 2], send_sem.at[i, d], recv_sem.at[i, me],
                    device_id=_dev(axis, tgt), device_id_type=pl.DeviceIdType.MESH,
                )
                c.start()
                sends.append(c)
            loc = pltpu.make_async_copy(ins[i], outs[i].at[p, me // 2], local_sem.at[i])
            loc.start()
            relays.append((i, loc))
            continue
        m = outs[i].shape[1]
        for d in range(1, k):
            tgt = (me + d) % k
            src = ins[i] if mode == "gather" else ins[i].at[pl.ds(tgt * m, m)]
            c = pltpu.make_async_remote_copy(
                src, outs[i].at[me], send_sem.at[i, d], recv_sem.at[i, me],
                device_id=_dev(axis, tgt), device_id_type=pl.DeviceIdType.MESH,
            )
            c.start()
            sends.append(c)
        if mode == "gather":
            loc = pltpu.make_async_copy(ins[i], outs[i].at[me], local_sem.at[i])
            loc.start()
            sends.append(loc)
    for i, (mode, axis) in enumerate(zip(modes, axes)):
        k = lax.axis_size(axis)
        me = lax.axis_index(axis)
        if mode == "rgather":
            _ring_pair_send(i, ins[i], lambda g: outs[i].at[g], lambda g: g, me, k,
                            send_sem, recv_sem, sends, axis, "relay")
        elif mode == "prgather":
            p = me % 2
            _ring_pair_send(i, ins[i], lambda g: outs[i].at[p, g], lambda g: g * 2 + p,
                            me // 2, k // 2, send_sem, recv_sem, sends, axis, "relay")
    for i, (mode, axis) in enumerate(zip(modes, axes)):
        if mode != "prgather":
            continue
        k = lax.axis_size(axis)
        me = lax.axis_index(axis)
        p = me % 2
        partner = me + 1 - 2 * p
        _ring_pair_wait(i, ins[i], lambda g: outs[i].at[p, g], lambda g: g * 2 + p,
                        me // 2, k // 2, send_sem, recv_sem, axis)
        locals_[i].wait()
        c = pltpu.make_async_remote_copy(
            outs[i].at[p], outs[i].at[p], send_sem.at[i, 2 * k - 1], recv_sem.at[i, 2 * k - 1],
            device_id=_dev(axis, partner), device_id_type=pl.DeviceIdType.MESH,
        )
        c.start()
        sends.append(c)
    for i, loc in relays:
        axis = axes[i]
        k = lax.axis_size(axis)
        me = lax.axis_index(axis)
        p = me % 2
        partner = me + 1 - 2 * p
        for d in range(1, k // 2):
            srcdev = (me + k - 2 * d) % k
            pltpu.make_async_remote_copy(
                ins[i], outs[i].at[p, srcdev // 2], send_sem.at[i, d], recv_sem.at[i, srcdev],
                device_id=_dev(axis, srcdev), device_id_type=pl.DeviceIdType.MESH,
            ).wait_recv()
        loc.wait()
        c = pltpu.make_async_remote_copy(
            outs[i].at[p], outs[i].at[p], send_sem.at[i, 0], recv_sem.at[i, me],
            device_id=_dev(axis, partner), device_id_type=pl.DeviceIdType.MESH,
        )
        c.start()
        sends.append(c)
    for c in sends:
        if c.is_remote:
            c.wait_send()
        else:
            c.wait()
    for i, (mode, axis) in enumerate(zip(modes, axes)):
        k = lax.axis_size(axis)
        me = lax.axis_index(axis)
        if mode == "rgather":
            _ring_pair_wait(i, ins[i], lambda g: outs[i].at[g], lambda g: g, me, k,
                            send_sem, recv_sem, axis)
            continue
        if mode == "prgather":
            p = me % 2
            partner = me + 1 - 2 * p
            pltpu.make_async_remote_copy(
                outs[i].at[1 - p], outs[i].at[1 - p], send_sem.at[i, 2 * k - 1],
                recv_sem.at[i, 2 * k - 1],
                device_id=_dev(axis, partner), device_id_type=pl.DeviceIdType.MESH,
            ).wait_recv()
            continue
        if mode == "pswap":
            partner = me + 1 - 2 * (me % 2)
            pltpu.make_async_remote_copy(
                outs[i], outs[i], send_sem.at[i, 0], recv_sem.at[i, partner],
                device_id=_dev(axis, partner), device_id_type=pl.DeviceIdType.MESH,
            ).wait_recv()
            continue
        if mode == "pscatter":
            for d in range(1, k // 2):
                srcdev = (me + k - 2 * d) % k
                pltpu.make_async_remote_copy(
                    ins[i].at[0], outs[i].at[srcdev // 2], send_sem.at[i, d],
                    recv_sem.at[i, srcdev], device_id=_dev(axis, srcdev),
                    device_id_type=pl.DeviceIdType.MESH,
                ).wait_recv()
            continue
        if mode == "pgather":
            p = me % 2
            partner = me + 1 - 2 * p
            pltpu.make_async_remote_copy(
                outs[i].at[1 - p], outs[i].at[1 - p], send_sem.at[i, 0], recv_sem.at[i, partner],
                device_id=_dev(axis, partner), device_id_type=pl.DeviceIdType.MESH,
            ).wait_recv()
            continue
        m = outs[i].shape[1]
        for d in range(1, k):
            srcdev = (me + k - d) % k
            src = ins[i] if mode == "gather" else ins[i].at[pl.ds(0, m)]
            pltpu.make_async_remote_copy(
                src, outs[i].at[srcdev], send_sem.at[i, d], recv_sem.at[i, srcdev],
                device_id=_dev(axis, srcdev), device_id_type=pl.DeviceIdType.MESH,
            ).wait_recv()


def exchange(items, cid):
    modes = tuple(mode for _, _, mode in items)
    axes = tuple(axis for _, axis, _ in items)
    out_shapes = []
    kmax = 1
    for x, axis, mode in items:
        k = lax.axis_size(axis)
        kmax = max(kmax, k)
        if mode in ("gather", "rgather"):
            out_shapes.append(jax.ShapeDtypeStruct((k,) + x.shape, x.dtype))
        elif mode == "pswap":
            out_shapes.append(jax.ShapeDtypeStruct((x.shape[0],) + x.shape[2:], x.dtype))
        elif mode == "pscatter":
            out_shapes.append(jax.ShapeDtypeStruct(x.shape, x.dtype))
        elif mode in ("pgather", "prgather"):
            out_shapes.append(jax.ShapeDtypeStruct((2, k // 2) + x.shape, x.dtype))
        else:
            out_shapes.append(
                jax.ShapeDtypeStruct((k, x.shape[0] // k) + x.shape[1:], x.dtype)
            )
    n = len(items)
    return pl.pallas_call(
        functools.partial(_exchange_kernel, modes, axes),
        out_shape=tuple(out_shapes),
        in_specs=[pl.BlockSpec(memory_space=pl.ANY)] * n,
        out_specs=tuple(pl.BlockSpec(memory_space=pl.ANY) for _ in range(n)),
        scratch_shapes=[
            pltpu.SemaphoreType.DMA((n, 2 * kmax)),
            pltpu.SemaphoreType.DMA((n, 2 * kmax)),
            pltpu.SemaphoreType.DMA((n,)),
        ],
        compiler_params=pltpu.CompilerParams(collective_id=cid, has_side_effects=True),
    )(*[x for x, _, _ in items])


def pair_order(v):
    return jnp.swapaxes(v, 0, 1).reshape((-1,) + v.shape[3:])


def reduce_scatter(parts, axis, cid, extra=()):
    k = lax.axis_size(axis)
    me = lax.axis_index(axis)
    m = parts.shape[0] // k
    outs = exchange([(parts.astype(WIRE), axis, "scatter")] + list(extra), cid)
    slots = outs[0]
    mine = lax.dynamic_slice_in_dim(parts, me * m, m, axis=0)
    keep = (jnp.arange(k) != me).reshape((k,) + (1,) * (slots.ndim - 1))
    other = jnp.sum(jnp.where(keep, slots.astype(jnp.float32), 0.0), axis=0)
    return (mine + other,) + tuple(outs[1:])


def pair_reduce_scatter(parts, axis, cid, extra=()):
    k = lax.axis_size(axis)
    me = lax.axis_index(axis)
    p = me % 2
    m = parts.shape[0] // k
    quad = parts.reshape((k // 2, 2, m) + parts.shape[1:])
    (got,) = exchange([(quad, axis, "pswap")], cid)
    pair = lax.dynamic_index_in_dim(quad, p, axis=1, keepdims=False) + got
    outs = exchange([(pair.astype(WIRE), axis, "pscatter")] + list(extra), cid + 1)
    slots = outs[0]
    own = lax.dynamic_index_in_dim(pair, me // 2, axis=0, keepdims=False)
    keep = (jnp.arange(k // 2) != me // 2).reshape((k // 2,) + (1,) * (slots.ndim - 1))
    other = jnp.sum(jnp.where(keep, slots.astype(jnp.float32), 0.0), axis=0)
    return (own + other,) + tuple(outs[1:])


def per_device(
    stream_in, grad_out, gate_pre, up_pre, keep_mask, segment_ids, norm_gain, w_gate, w_up, w_down
):
    n_row = lax.axis_size("row")
    n_col = lax.axis_size("col")
    RG = "rgather" if n_row == 8 else "gather"
    PG = "prgather" if n_col == 16 else "pgather"
    tok_col, feat_loc = stream_in.shape
    tok_row, ff_loc = gate_pre.shape
    total = tok_col * n_col
    xs = stream_in.astype(jnp.float32)
    onehot = (segment_ids[:, None] == jnp.arange(SEGS, dtype=jnp.int32)[None, :]).astype(
        jnp.float32
    )
    stats = jnp.concatenate([jnp.sum(xs * xs, axis=1), jnp.sum(onehot, axis=0)])[None, :]
    (stats_all,) = exchange([(stats, "row", "gather")], 0)
    stats_sum = jnp.sum(stats_all, axis=(0, 1))
    squares, counts = stats_sum[:tok_col], stats_sum[tok_col:]
    weights = jnp.sum(onehot * (total / (SEGS * counts))[None, :], axis=1)
    recip = lax.rsqrt(squares / D + eps)
    normed = (xs * recip[:, None] * norm_gain[None, :]).astype(jnp.bfloat16)
    gate_f = gate_pre.astype(jnp.float32)
    up_f = up_pre.astype(jnp.float32)
    sig = jax.nn.sigmoid(gate_f)
    keep_f = keep_mask.astype(jnp.float32) * keep_scale
    dropped = (gate_f * sig * up_f * keep_f * weights[:, None]).astype(jnp.bfloat16)
    cot_full, dropped_full = exchange([(grad_out, "col", PG), (dropped, "row", RG)], 1)
    cot_full = pair_order(cot_full)
    dropped_full = dropped_full.reshape(total, ff_loc)
    back, normed_full = reduce_scatter(
        over_width(cot_full, w_down), "row", 2, [(normed, "col", PG)]
    )
    normed_full = normed_full.reshape(total, feat_loc)
    grad_act = back * weights[:, None] * keep_f
    grad_gpre = (grad_act * up_f * sig * (1.0 + gate_f * (1.0 - sig))).astype(jnp.bfloat16)
    grad_upre = (grad_act * gate_f * sig).astype(jnp.bfloat16)
    half = tok_col // 2
    n_chunk = tok_row // tok_col

    def split(v):
        v = v.reshape(n_chunk, 2, half, ff_loc)
        return v[:, 0].reshape(tok_row // 2, ff_loc), v[:, 1].reshape(tok_row // 2, ff_loc)

    def joined(a, b):
        a = a.reshape(n_row, n_chunk, 1, half, ff_loc)
        b = b.reshape(n_row, n_chunk, 1, half, ff_loc)
        both = jnp.concatenate([a, b], axis=2)
        return jnp.swapaxes(both, 0, 1).reshape(total, ff_loc)

    gpre_a, gpre_b = split(grad_gpre)
    upre_a, upre_b = split(grad_upre)
    (gu_a,) = exchange([(jnp.stack([gpre_a, upre_a]), "row", RG)], 3)
    ga_full = gu_a[:, 0].reshape(total // 2, ff_loc)
    ua_full = gu_a[:, 1].reshape(total // 2, ff_loc)
    part_a = over_width(ga_full, w_gate) + over_width(ua_full, w_up)
    gn_a, gu_b = pair_reduce_scatter(part_a, "col", 4, [(jnp.stack([gpre_b, upre_b]), "row", RG)])
    gb_full = gu_b[:, 0].reshape(total // 2, ff_loc)
    ub_full = gu_b[:, 1].reshape(total // 2, ff_loc)
    part_b = over_width(gb_full, w_gate) + over_width(ub_full, w_up)
    (gn_b,) = pair_reduce_scatter(part_b, "col", 6)
    grad_normed = jnp.concatenate([gn_a, gn_b], axis=0)
    gpre_full = joined(ga_full, gb_full)
    upre_full = joined(ua_full, ub_full)
    grad_down = over_tokens(dropped_full, cot_full).astype(jnp.bfloat16)
    grad_gate = over_tokens(normed_full, gpre_full).astype(jnp.bfloat16)
    grad_up = over_tokens(normed_full, upre_full).astype(jnp.bfloat16)
    scaled = grad_normed * norm_gain[None, :]
    (inner_all,) = exchange([(jnp.sum(scaled * xs, axis=1)[None, :], "row", "gather")], 8)
    inner = jnp.sum(inner_all, axis=(0, 1)) / D
    branch = recip[:, None] * (scaled - xs * (recip * recip * inner)[:, None])
    grad_in = (grad_out.astype(jnp.float32) + branch).astype(jnp.bfloat16)
    return (grad_in, grad_gate, grad_up, grad_down)


def solution(mesh):
    return jax.shard_map(
        per_device,
        mesh=mesh,
        in_specs=(
            P("col", "row"),
            P("col", "row"),
            P("row", "col"),
            P("row", "col"),
            P("row", "col"),
            P("row"),
            P("row"),
            P("row", "col"),
            P("row", "col"),
            P("col", "row"),
        ),
        out_specs=(P("col", "row"), P("row", "col"), P("row", "col"), P("col", "row")),
        check_vma=False,
    )
```
